32 devices in a mesh: batch: 8 (over z, y), mp: 4 (over x, core).
Axes of the slice: x: 2, y: 2, z: 4, core: 2. Of those that a mesh axis runs over, the one named last changes fastest.
Arguments:
- tokens: bfloat16 [768, 128, 768], P('batch'), may hold values from -6 to 6
- lengths: int32 [768], P('batch'), may hold values from 20 to 128, as said below
- base_gains: float32 [2, 768], replicated, may hold values from 0.25 to 1.75
- base_qkv: bfloat16 [3, 768, 768], P(None, None, 'mp'), may hold values from -0.109375 to 0.109375
- base_out: bfloat16 [768, 768], replicated, may hold values from -0.75 to 0.75
- base_up: bfloat16 [768, 3072], replicated, may hold values from -0.21875 to 0.21875
- base_down: bfloat16 [3072, 768], replicated, may hold values from -0.15625 to 0.15625
- base_table: float32 [32, 12], replicated, may hold values from -4 to 4
- side_input: float32 [768, 128, 96], P(('batch', 'mp')), may hold values from -6 to 6
- output_grad: float32 [768, 128, 96], P(('batch', 'mp')), may hold values from -6 to 6
- side_weights: float32 [184320], P(('batch', 'mp'))
- weights_first: float32 [184320], P(('batch', 'mp')), may hold values from -0.00390625 to 0.00390625
- weights_second: float32 [184320], P(('batch', 'mp')), may hold values from 5.4253473e-09 to 2.170139e-08
- side_gains: float32 [3, 96], replicated
- gains_first: float32 [3, 96], replicated, may hold values from -0.0068359375 to 0.0068359375
- gains_second: float32 [3, 96], replicated, may hold values from 5.4253473e-09 to 2.7126736e-08
- side_table: float32 [32, 12], replicated, may hold values from -4 to 4
- table_first: float32 [32, 12], replicated, may hold values from -0.0014648438 to 0.0014648438
- table_second: float32 [32, 12], replicated, may hold values from 2.7126737e-10 to 1.0850695e-09
Outputs:
- side_output: float32 [768, 128, 96], P(('batch', 'mp'))
- input_grad: float32 [768, 128, 96], P(('batch', 'mp'))
- grad_norm: float32 [], replicated
- weights_moment: float32 [184320], P(('batch', 'mp'))
- weights_square: float32 [184320], P(('batch', 'mp'))
- weights_new: float32 [184320], P(('batch', 'mp'))
- weights_copy: bfloat16 [184320], P(('batch', 'mp'))
- gains_moment: float32 [3, 96], replicated
- gains_square: float32 [3, 96], replicated
- gains_new: float32 [3, 96], replicated
- table_moment: float32 [32, 12], replicated
- table_square: float32 [32, 12], replicated
- table_new: float32 [32, 12], replicated
The draws below stay inside these ranges and needn't reach their ends.
Inputs may be any that keep to these rules, and one draw needn't show every extreme that they name: `lengths`: each sentence has 20 to 128 true tokens, and the first sentence has exactly 128.
All inputs are finite; a program needn't handle non-finite values.
Results may differ from the reference program's by a relative error of at most 0.024.
Values may be sent and summed in bfloat16 or wider, within the bound.
No kernel may reach another device: no remote copies, remote signals or barrier semaphores. Data moves between devices by JAX's collectives and lax.ppermute only.
A program may use at most 192 MiB of HBM per device.

```python
import math
import jax
import jax.numpy as jnp
import numpy as np
from jax import lax

D = 768
HEADS = 12
HD = 64
FF = 3072
DS = 96
SH = 12
SHD = 8
SFF = 384
NB = 32
MAXD = 128
L = 128
LMIN = 20
ADAM_STEP = 10
NSEQ = 768
NPAR = 184320


def draw_lengths(key, part):
    drawn = jax.random.randint(key, (NSEQ,), LMIN, L + 1)
    return drawn.at[0].set(L).astype(jnp.int32)


def draw_side_weights(key, part):
    key_list = jax.random.split(key, 5)
    down_part = jax.random.normal(key_list[0], (D * DS,), jnp.float32) * (1.0 / math.sqrt(D))
    column_scale = jnp.concatenate([jnp.full((2 * DS,), 0.7, jnp.float32), jnp.ones((DS,), jnp.float32)]) / math.sqrt(DS)
    qkv_part = (jax.random.normal(key_list[1], (DS, 3 * DS), jnp.float32) * column_scale[None, :]).reshape(-1)
    out_part = jax.random.normal(key_list[2], (DS * DS,), jnp.float32) * (2.5 / math.sqrt(DS))
    up_part = jax.random.normal(key_list[3], (DS * SFF,), jnp.float32) * (1.0 / math.sqrt(DS))
    back_part = jax.random.normal(key_list[4], (SFF * DS,), jnp.float32) * math.sqrt(2.0 / SFF)
    return jnp.concatenate([down_part, qkv_part, out_part, up_part, back_part]).astype(jnp.float32)


def draw_side_gains(key, part):
    first_key, second_key = jax.random.split(key)
    norm_gains = 1.0 + 0.15 * jax.random.uniform(first_key, (2, DS), jnp.float32, -1.0, 1.0)
    gate_logits = jax.random.uniform(second_key, (1, DS), jnp.float32, -1.5, 1.5)
    return jnp.concatenate([norm_gains, gate_logits], axis=0).astype(jnp.float32)


def levels(rng, extent, cuts, low, high):
    def one(dim, shards_of):
        steps = jax.random.uniform(jax.random.fold_in(jax.random.fold_in(rng, 6), dim), (shards_of,), jnp.float32, low / len(cuts), high / len(cuts))
        return jnp.repeat(jnp.exp(steps), extent[dim] // shards_of).reshape((-1,) + (1,) * (len(extent) - dim - 1))

    gain = one(*cuts[0])
    for cut in cuts[1:]:
        gain = gain * one(*cut)
    return gain


def gaussian(rng, extent, width, bound, pieces=(), dtype=jnp.bfloat16):
    loudness = levels(rng, extent, pieces, -0.22, 0.18) if pieces else 1.0
    values = jax.random.normal(rng, extent, jnp.float32) * width * loudness
    return jnp.minimum(jnp.maximum(values, -bound), bound).astype(dtype)


def setup_inputs(seed: int = 0) -> dict:
    arg_keys = jax.random.split(jax.random.key(seed), 20)
    return {
        "tokens": gaussian(arg_keys[0], (NSEQ, L, D), 1.0, 6.0, ((0, 8),)),
        "lengths": draw_lengths(jax.random.fold_in(arg_keys[19], 71), 0),
        "base_gains": jnp.clip(1.0 + 0.15 * jax.random.normal(arg_keys[2], (2, D), jnp.float32), 0.25, 1.75),
        "base_qkv": gaussian(arg_keys[3], (3, D, D), (4 * D) ** -0.5, 0.109375, ((2, 4),)),
        "base_out": gaussian(arg_keys[4], (D, D), HD ** -0.5, 0.75),
        "base_up": gaussian(arg_keys[5], (D, FF), D ** -0.5, 0.21875),
        "base_down": gaussian(arg_keys[6], (FF, D), (FF // 2) ** -0.5, 0.15625),
        "base_table": gaussian(arg_keys[7], (NB, HEADS), 1.0, 4.0, (), jnp.float32),
        "side_input": gaussian(arg_keys[8], (NSEQ, L, DS), 1.0, 6.0, ((0, 32),), jnp.float32),
        "output_grad": gaussian(arg_keys[9], (NSEQ, L, DS), 1.0, 6.0, ((0, 32),), jnp.float32),
        "side_weights": draw_side_weights(jax.random.fold_in(arg_keys[19], 71), 0),
        "weights_first": gaussian(arg_keys[11], (NPAR,), (0.11 / NPAR ** 0.5), 0.00390625, ((0, 32),), jnp.float32),
        "weights_second": jnp.clip(jnp.exp(math.log(2.1701389130157622e-08) - 1.3862944 * jax.random.uniform(arg_keys[12], (NPAR,), jnp.float32) ** levels(arg_keys[12], (NPAR,), ((0, 32),), -0.2, 0.2)), 5.4253472825394056e-09, 2.1701389130157622e-08),
        "side_gains": draw_side_gains(jax.random.fold_in(arg_keys[19], 71), 0),
        "gains_first": gaussian(arg_keys[14], (3, DS), (0.2 / NPAR ** 0.5), 0.0068359375, (), jnp.float32),
        "gains_second": jnp.clip(jnp.exp(jax.random.uniform(arg_keys[15], (3, DS), jnp.float32, math.log(5.4253472825394056e-09), math.log(2.7126736412697028e-08))), 5.4253472825394056e-09, 2.7126736412697028e-08),
        "side_table": gaussian(arg_keys[16], (NB, SH), 0.5, 4.0, (), jnp.float32),
        "table_first": gaussian(arg_keys[17], (NB, SH), (0.04 / NPAR ** 0.5), 0.0014648438, (), jnp.float32),
        "table_second": jnp.clip(jnp.exp(jax.random.uniform(arg_keys[18], (NB, SH), jnp.float32, math.log(2.712673696780854e-10), math.log(1.0850694787123416e-09))), 2.712673696780854e-10, 1.0850694787123416e-09),
    }


NORM_EPS = 1e-06
CLIP_NORM = 1.0
BETA_ONE = 0.9
BETA_TWO = 0.999
ADAM_EPS = 1e-08
RATE_MATRIX = 0.1
RATE_SMALL = 0.5
WEIGHT_DECAY = 0.01
MASKED = -1e+30
PRECISE = lax.Precision.HIGHEST

@jax.custom_vjp
def low(v):
    return lax.optimization_barrier(v.astype(jnp.bfloat16)).astype(jnp.float32)

@jax.custom_vjp
def low_back(v):
    return v

def low_keep(v):
    return (low(v), None)

def low_pass(kept, grad):
    return (grad,)

def back_keep(v):
    return (v, None)

def back_low(kept, grad):
    return (low(grad),)
low.defvjp(low_keep, low_pass)
low_back.defvjp(back_keep, back_low)

def bucket_ids(length, buckets, reach):
    offset = np.arange(length)[None, :] - np.arange(length)[:, None]
    half_count = buckets // 2
    exact_count = half_count // 2
    distance = np.abs(offset)
    spread_part = np.log(np.maximum(distance, 1) / exact_count) / np.log(reach / exact_count) * (half_count - exact_count)
    far_bucket = np.minimum(exact_count + np.floor(spread_part).astype(np.int32), half_count - 1)
    near_side = np.where(distance < exact_count, distance, far_bucket)
    return (near_side + (offset > 0) * half_count).astype(np.int32)

def position_bias(table):
    ident = jnp.asarray(bucket_ids(L, NB, MAXD))
    return jnp.transpose(table[ident], (2, 0, 1))

def rms_scale(values):
    return lax.rsqrt(lax.optimization_barrier(jnp.mean(values * values, axis=-1, keepdims=True)) + NORM_EPS)

def key_mask(row_lengths):
    return jnp.arange(L)[None, :] < row_lengths[:, None]

def backbone_rows(token_rows, row_lengths, base_gains, base_qkv, base_out, base_up, base_down, base_bias):
    inputs = token_rows.astype(jnp.float32)
    count = inputs.shape[0]
    normed = low(inputs * rms_scale(inputs) * base_gains[0])
    projected = low(jnp.einsum('bld,kdc->kblc', normed, base_qkv, precision=PRECISE))
    queries = projected[0].reshape(count, L, HEADS, HD)
    keys_all = projected[1].reshape(count, L, HEADS, HD)
    values_all = projected[2].reshape(count, L, HEADS, HD)
    scores = jnp.einsum('bqhe,bkhe->bhqk', queries, keys_all, precision=PRECISE) + base_bias[None]
    visible = key_mask(row_lengths)[:, None, None, :]
    attn_probs = low(jax.nn.softmax(jnp.where(visible, scores, MASKED), axis=-1))
    context = low(jnp.einsum('bhqk,bkhe->bqhe', attn_probs, values_all, precision=PRECISE).reshape(count, L, D))
    middle = inputs + jnp.einsum('bld,de->ble', context, base_out, precision=PRECISE)
    normed_two = low(middle * rms_scale(middle) * base_gains[1])
    hidden = low(jax.nn.gelu(jnp.einsum('bld,df->blf', normed_two, base_up, precision=PRECISE)))
    result = middle + jnp.einsum('blf,fd->bld', hidden, base_down, precision=PRECISE)
    return result.astype(jnp.bfloat16)

def unpack(flat):
    first_end = D * DS
    second_end = first_end + 3 * DS * DS
    third_end = second_end + DS * DS
    fourth_end = third_end + DS * SFF
    return (flat[:first_end].reshape(D, DS), flat[first_end:second_end].reshape(DS, 3 * DS), flat[second_end:third_end].reshape(DS, DS), flat[third_end:fourth_end].reshape(DS, SFF), flat[fourth_end:].reshape(SFF, DS))

def side_rows(master, gain_rows, table_rows, inputs_rows, tap_rows, row_lengths):
    w_down, w_qkv, w_out, w_up, w_back = unpack(low(master))
    count = inputs_rows.shape[0]
    mixing = jax.nn.sigmoid(gain_rows[2])
    tapped = low_back(jnp.einsum('bld,dc->blc', tap_rows, w_down, precision=PRECISE))
    mixed = mixing * inputs_rows + (1.0 - mixing) * tapped
    normed = low(mixed * rms_scale(mixed) * gain_rows[0])
    projected = low_back(low(jnp.einsum('blc,cj->blj', normed, w_qkv, precision=PRECISE)))
    queries = projected[..., :DS].reshape(count, L, SH, SHD)
    keys_all = projected[..., DS:2 * DS].reshape(count, L, SH, SHD)
    values_all = projected[..., 2 * DS:].reshape(count, L, SH, SHD)
    scores = low_back(jnp.einsum('bqhe,bkhe->bhqk', queries, keys_all, precision=PRECISE) + position_bias(table_rows)[None])
    visible = key_mask(row_lengths)[:, None, None, :]
    attn_probs = low(jax.nn.softmax(jnp.where(visible, scores, MASKED), axis=-1))
    context = low_back(low(jnp.einsum('bhqk,bkhe->bqhe', attn_probs, values_all, precision=PRECISE).reshape(count, L, DS)))
    attended = low_back(jnp.einsum('blc,ce->ble', context, w_out, precision=PRECISE))
    middle = mixed + attended
    normed_two = low(middle * rms_scale(middle) * gain_rows[1])
    pre_act = low_back(jnp.einsum('blc,cf->blf', normed_two, w_up, precision=PRECISE))
    hidden = low(jax.nn.gelu(pre_act))
    return middle + low_back(jnp.einsum('blf,fc->blc', hidden, w_back, precision=PRECISE))

def adamw_update(weight_now, first_now, second_now, gradient, rate, decay_rate):
    first_new = BETA_ONE * first_now + (1.0 - BETA_ONE) * gradient
    second_new = BETA_TWO * second_now + (1.0 - BETA_TWO) * gradient * gradient
    first_hat = first_new / (1.0 - BETA_ONE ** ADAM_STEP)
    second_hat = second_new / (1.0 - BETA_TWO ** ADAM_STEP)
    weight_new = weight_now - rate * (first_hat / (jnp.sqrt(second_hat) + ADAM_EPS) + decay_rate * weight_now)
    return (first_new, second_new, weight_new)

def reference(tokens, lengths, base_gains, base_qkv, base_out, base_up, base_down, base_table, side_input, output_grad, side_weights, weights_first, weights_second, side_gains, gains_first, gains_second, side_table, table_first, table_second):
    group = math.gcd(NSEQ, max(1, 4096 // L))
    blocks = NSEQ // group
    base_bias = position_bias(base_table)
    qkv_float = base_qkv.astype(jnp.float32)
    out_float = base_out.astype(jnp.float32)
    up_float = base_up.astype(jnp.float32)
    down_float = base_down.astype(jnp.float32)

    def backbone_block(items):
        token_rows, row_lengths = items
        return backbone_rows(token_rows, row_lengths, base_gains, qkv_float, out_float, up_float, down_float, base_bias)
    length_blocks = lengths.reshape(blocks, group)
    taps = lax.map(backbone_block, (tokens.reshape(blocks, group, L, D), length_blocks))
    row_weight = key_mask(lengths).astype(jnp.float32)[..., None]
    cotangent = (output_grad * row_weight).reshape(blocks, group, L, DS)

    def side_block(carry, items):
        inputs_rows, tap_rows, row_lengths, cot_rows = items

        def forward(master, gain_rows, table_rows, rows_in):
            return side_rows(master, gain_rows, table_rows, rows_in, tap_rows.astype(jnp.float32), row_lengths)
        result, pullback = jax.vjp(forward, side_weights, side_gains, side_table, inputs_rows)
        grad_master, grad_gains, grad_table, grad_rows = pullback(cot_rows)
        return ((carry[0] + grad_master, carry[1] + grad_gains, carry[2] + grad_table), (result, grad_rows))
    start = (jnp.zeros((NPAR,), jnp.float32), jnp.zeros((3, DS), jnp.float32), jnp.zeros((NB, SH), jnp.float32))
    totals, (outputs_all, grads_all) = lax.scan(side_block, start, (side_input.reshape(blocks, group, L, DS), taps, length_blocks, cotangent))
    grad_master, grad_gains, grad_table = totals
    grad_norm = jnp.sqrt(jnp.sum(grad_master * grad_master) + jnp.sum(grad_gains * grad_gains) + jnp.sum(grad_table * grad_table))
    factor = CLIP_NORM / jnp.maximum(grad_norm, CLIP_NORM)
    weights_moment, weights_square, weights_new = adamw_update(side_weights, weights_first, weights_second, factor * grad_master, RATE_MATRIX, WEIGHT_DECAY)
    gains_moment, gains_square, gains_new = adamw_update(side_gains, gains_first, gains_second, factor * grad_gains, RATE_SMALL, 0.0)
    table_moment, table_square, table_new = adamw_update(side_table, table_first, table_second, factor * grad_table, RATE_SMALL, 0.0)
    return (outputs_all.reshape(NSEQ, L, DS), grads_all.reshape(NSEQ, L, DS), grad_norm, weights_moment, weights_square, weights_new, weights_new.astype(jnp.bfloat16), gains_moment, gains_square, gains_new, table_moment, table_square, table_new)
```

```python
import functools
import math
import jax
import jax.numpy as jnp
import numpy as np
from jax import lax
from jax.experimental import pallas as pl
from jax.experimental.pallas import tpu as pltpu
from jax.sharding import PartitionSpec as P

D = 768
HD = 64
DS = 96
SH = 12
SHD = 8
SFF = 384
MAXD = 128
L = 128
ADAM_STEP = 10
PAIR = 2 * HD
SPAN = 2 * L

NORM_EPS = 1e-06
CLIP_NORM = 1.0
BETA_ONE = 0.9
BETA_TWO = 0.999
ADAM_EPS = 1e-08
RATE_MATRIX = 0.1
RATE_SMALL = 0.5
WEIGHT_DECAY = 0.01
MASKED = -1e30
PRECISE = lax.Precision.HIGHEST
MIB = 1 << 20
GELU_RATE = math.sqrt(2.0 / math.pi)
GELU_CUBE = 0.044715

NN = (((1,), (0,)), ((), ()))
NT = (((1,), (1,)), ((), ()))
TN = (((0,), (0,)), ((), ()))


def mm(left, right, dims=NN):
    return lax.dot_general(left, right, dims, preferred_element_type=jnp.float32)


def bucket_of(offset, buckets, reach):
    half_count = buckets // 2
    exact_count = half_count // 2
    distance = np.abs(offset)
    spread_part = (
        np.log(np.maximum(distance, 1) / exact_count)
        / np.log(reach / exact_count)
        * (half_count - exact_count)
    )
    far_bucket = np.minimum(exact_count + np.floor(spread_part).astype(np.int32), half_count - 1)
    near_side = np.where(distance < exact_count, distance, far_bucket)
    return (near_side + (offset > 0) * half_count).astype(np.int32)


def diagonal_onehot(buckets):
    column = np.arange(SPAN)
    offset = np.where(column < L, -column, SPAN - column)
    onehot = bucket_of(offset, buckets, MAXD)[None, :] == np.arange(buckets)[:, None]
    onehot = onehot & (column != L)[None, :]
    return onehot.astype(np.float32)


def gradient_onehot(buckets):
    column = np.arange(SPAN)
    onehot = bucket_of(L - 1 - column, buckets, MAXD)[None, :] == np.arange(buckets)[:, None]
    onehot = onehot & (column != SPAN - 1)[None, :]
    return onehot.astype(np.float32)


def rms_scale(values):
    return lax.rsqrt(jnp.mean(values * values, axis=-1, keepdims=True) + NORM_EPS)


def gelu(v):
    return 0.5 * v * (1.0 + jnp.tanh(GELU_RATE * (v + GELU_CUBE * (v * v * v))))


def spread_bias(row):
    full = jnp.broadcast_to(row, (L, SPAN))
    return pltpu.roll(full, 0, 1, stride=1, stride_axis=0)[:, :L]


def attention_kernel(seqs, meta_ref, len_ref, tok_ref, gain_ref, own_ref, mate_ref, diag_ref, ctx_ref, w_scr, bias_scr):
    step = pl.program_id(0)
    third = own_ref.shape[2]
    pairs = 2 * third // PAIR
    width = 2 * third

    def place(low_ref, high_ref):
        for part in range(3):
            w_scr[:, part * width : part * width + third] = low_ref[part]
            w_scr[:, part * width + third : (part + 1) * width] = high_ref[part]

    @pl.when(step == 0)
    def _():
        @pl.when(meta_ref[1] == 0)
        def _():
            place(own_ref, mate_ref)

        @pl.when(meta_ref[1] == 1)
        def _():
            place(mate_ref, own_ref)

        for head in range(2 * pairs):
            bias_scr[head * L : (head + 1) * L, :] = spread_bias(
                diag_ref[pl.ds(meta_ref[2] * 2 * pairs + head, 1), :]
            )

    rows = tok_ref[...].reshape(seqs * L, D).astype(jnp.float32)
    normed = (rows * rms_scale(rows) * gain_ref[0:1, :]).astype(jnp.bfloat16)
    qkv = mm(normed, w_scr[...]).astype(jnp.bfloat16)
    low_lane = lax.broadcasted_iota(jnp.int32, (L, PAIR), 1) < HD
    key_row = lax.broadcasted_iota(jnp.int32, (2 * L, L), 0) % L
    for s in range(seqs):
        length = len_ref[meta_ref[0] + step * seqs + s]
        seen = key_row < length
        for p in range(pairs):
            at = slice(s * L, (s + 1) * L)
            query = qkv[at, p * PAIR : (p + 1) * PAIR]
            key = qkv[at, width + p * PAIR : width + (p + 1) * PAIR]
            value = qkv[at, 2 * width + p * PAIR : 2 * width + (p + 1) * PAIR]
            zero = jnp.zeros_like(key)
            key_two = jnp.concatenate(
                [jnp.where(low_lane, key, zero), jnp.where(low_lane, zero, key)], axis=0
            )
            value_two = jnp.concatenate(
                [jnp.where(low_lane, value, zero), jnp.where(low_lane, zero, value)], axis=0
            )
            scores = mm(key_two, query, NT) + bias_scr[p * 2 * L : (p + 1) * 2 * L, :]
            scores = jnp.where(seen, scores, MASKED).reshape(2, L, L)
            shifted = jnp.exp(scores - jnp.max(scores, axis=1, keepdims=True))
            probs = shifted * (1.0 / jnp.sum(shifted, axis=1, keepdims=True))
            probs = probs.astype(jnp.bfloat16).reshape(2 * L, L)
            ctx_ref[at, p * PAIR : (p + 1) * PAIR] = mm(probs, value_two, TN).astype(jnp.bfloat16)


def attention_part(meta, lengths, tokens, gains, own, mate, diag, own_seqs, seqs):
    width = 2 * own.shape[2]
    grid = own_seqs // seqs
    fixed = lambda *dims: pl.BlockSpec(dims, lambda i, m, n: (0,) * len(dims))
    return pl.pallas_call(
        functools.partial(attention_kernel, seqs),
        name="attend",
        grid_spec=pltpu.PrefetchScalarGridSpec(
            num_scalar_prefetch=2,
            grid=(grid,),
            in_specs=[
                pl.BlockSpec((seqs, L, D), lambda i, m, n: (m[0] // seqs + i, 0, 0)),
                fixed(2, D),
                fixed(*own.shape),
                fixed(*mate.shape),
                fixed(*diag.shape),
            ],
            out_specs=pl.BlockSpec((seqs * L, width), lambda i, m, n: (i, 0)),
            scratch_shapes=[
                pltpu.VMEM((D, 3 * width), jnp.bfloat16),
                pltpu.VMEM((width // HD * L, L), jnp.float32),
            ],
        ),
        out_shape=jax.ShapeDtypeStruct((own_seqs * L, width), jnp.bfloat16),
        compiler_params=pltpu.CompilerParams(
            dimension_semantics=("arbitrary",), vmem_limit_bytes=56 * MIB
        ),
        cost_estimate=pl.CostEstimate(
            flops=2 * own_seqs * L * width * (3 * D + 2 * L),
            bytes_accessed=own_seqs * L * (D + width) * 2 + 6 * D * width,
            transcendentals=own_seqs * width // HD * L * L,
        ),
    )(meta, lengths, tokens, gains, own, mate, diag)


def ffn_kernel(seqs, chunk, meta_ref, ca_ref, cb_ref, tok_ref, gain_ref, wa_ref, wb_ref, up_ref, down_ref, taps_ref):
    rows = tok_ref[...].reshape(seqs * L, D).astype(jnp.float32)
    middle = rows + mm(ca_ref[...], wa_ref[...]) + mm(cb_ref[...], wb_ref[...])
    normed = (middle * rms_scale(middle) * gain_ref[1:2, :]).astype(jnp.bfloat16)
    total = jnp.zeros_like(middle)
    for c in range(0, up_ref.shape[1], chunk):
        hidden = gelu(mm(normed, up_ref[:, c : c + chunk])).astype(jnp.bfloat16)
        total = total + mm(hidden, down_ref[c : c + chunk, :])
    taps_ref[...] = (middle + total).astype(jnp.bfloat16)


def ffn_part(meta, ctx_a, ctx_b, tokens, gains, w_out, w_up, w_down, own_seqs, seqs, chunk):
    width = ctx_a.shape[1]
    grid = own_seqs // seqs
    ff = w_up.shape[1]
    fixed = lambda *dims: pl.BlockSpec(dims, lambda i, m: (0,) * len(dims))
    return pl.pallas_call(
        functools.partial(ffn_kernel, seqs, chunk),
        name="feed",
        grid_spec=pltpu.PrefetchScalarGridSpec(
            num_scalar_prefetch=1,
            grid=(grid,),
            in_specs=[
                pl.BlockSpec((seqs * L, width), lambda i, m: (i, 0)),
                pl.BlockSpec((seqs * L, width), lambda i, m: (i, 0)),
                pl.BlockSpec((seqs, L, D), lambda i, m: (m[0] // seqs + i, 0, 0)),
                fixed(2, D),
                pl.BlockSpec((width, D), lambda i, m: (m[2], 0)),
                pl.BlockSpec((width, D), lambda i, m: (1 - m[2], 0)),
                fixed(*w_up.shape),
                fixed(*w_down.shape),
            ],
            out_specs=pl.BlockSpec((seqs * L, D), lambda i, m: (i, 0)),
        ),
        out_shape=jax.ShapeDtypeStruct((own_seqs * L, D), jnp.bfloat16),
        compiler_params=pltpu.CompilerParams(
            dimension_semantics=("arbitrary",), vmem_limit_bytes=60 * MIB
        ),
        cost_estimate=pl.CostEstimate(
            flops=2 * own_seqs * L * D * (D + 2 * ff),
            bytes_accessed=own_seqs * L * 3 * D * 2 + 2 * D * (D + 2 * ff),
            transcendentals=own_seqs * L * ff,
        ),
    )(meta, ctx_a, ctx_b, tokens, gains, w_out, w_out, w_up, w_down)


def pick_rows(step, phase, count):
    row = lax.broadcasted_iota(jnp.int32, (count, step * count), 0)
    column = lax.broadcasted_iota(jnp.int32, (count, step * count), 1)
    return (column == step * row + phase).astype(jnp.bfloat16)


def by_head_rows(block):
    head = lax.broadcasted_iota(jnp.int32, block.shape, 1) // SHD
    zero = jnp.zeros_like(block)
    return jnp.concatenate([jnp.where(head == h, block, zero) for h in range(SH)], axis=0)


def by_head_lanes(block):
    head = lax.broadcasted_iota(jnp.int32, block.shape, 0) // SHD
    zero = jnp.zeros_like(block)
    return jnp.concatenate([jnp.where(head == h, block, zero) for h in range(SH)], axis=1)


def lanes_of(stacked):
    return jnp.concatenate([stacked[h * L : (h + 1) * L] for h in range(SH)], axis=1)


def norm_back(unit, scale, gain, grad):
    scaled = grad * gain
    back = scale * (scaled - unit * jnp.mean(scaled * unit, axis=-1, keepdims=True))
    return back, jnp.sum(grad * unit, axis=0, keepdims=True)


def side_kernel(
    seqs,
    meta_ref,
    len_ref,
    taps_ref,
    x_ref,
    go_ref,
    gain_ref,
    w_ref,
    diag_ref,
    onehot_ref,
    out_ref,
    ig_ref,
    grow_ref,
    gsmall_ref,
    wqkv_scr,
    wup_scr,
    bias_scr,
    gbias_scr,
    p_scr,
    plow_scr,
    gdown_scr,
    gqkv_scr,
    gproj_scr,
    gup_scr,
    gback_scr,
    ggain_scr,
):
    step = pl.program_id(0)
    at_qkv, at_out, at_up, at_back = D, D + 3 * DS, D + 4 * DS, D + 8 * DS

    @pl.when(step == 0)
    def _():
        for t in range(3):
            wqkv_scr[t] = mm(pick_rows(3, t, DS), w_ref[at_qkv:at_out, :]).astype(jnp.bfloat16)
        for t in range(4):
            wup_scr[:, t * DS : (t + 1) * DS] = mm(
                pick_rows(4, t, DS), w_ref[at_up:at_back, :]
            ).astype(jnp.bfloat16)
        for head in range(SH):
            bias_scr[head * L : (head + 1) * L, :] = spread_bias(diag_ref[head : head + 1, :])
        for ref in (gbias_scr, gdown_scr, gqkv_scr, gproj_scr, gup_scr, gback_scr, ggain_scr):
            ref[...] = jnp.zeros_like(ref)

    rows = seqs * L
    gain_one, gain_two = gain_ref[0:1, :], gain_ref[1:2, :]
    gate = jax.nn.sigmoid(gain_ref[2:3, :])
    w_out = w_ref[at_out:at_up, :]
    w_back = w_ref[at_back : at_back + SFF, :]
    lengths = [len_ref[meta_ref[0] + step * seqs + s] for s in range(seqs)]
    key_row = lax.broadcasted_iota(jnp.int32, (SH, L, L), 1)
    own_row = lax.broadcasted_iota(jnp.int32, (L, DS), 0)
    taps = taps_ref[...]
    x = x_ref[...].reshape(rows, DS)
    grad_out = jnp.concatenate(
        [jnp.where(own_row < lengths[s], go_ref[s], 0.0) for s in range(seqs)], axis=0
    )

    tapped = mm(taps, w_ref[0:D, :])
    mixed = gate * x + (1.0 - gate) * tapped
    scale_one = rms_scale(mixed)
    unit_one = mixed * scale_one
    normed_one = (unit_one * gain_one).astype(jnp.bfloat16)
    query = mm(normed_one, wqkv_scr[0]).astype(jnp.bfloat16)
    key = mm(normed_one, wqkv_scr[1]).astype(jnp.bfloat16)
    value = mm(normed_one, wqkv_scr[2]).astype(jnp.bfloat16)

    context = []
    for s in range(seqs):
        at = slice(s * L, (s + 1) * L)
        scores = mm(by_head_rows(key[at]), query[at], NT) + bias_scr[...]
        scores = scores.reshape(SH, L, L)
        scores = jnp.where(key_row < lengths[s], scores, MASKED)
        shifted = jnp.exp(scores - jnp.max(scores, axis=1, keepdims=True))
        probs = shifted * (1.0 / jnp.sum(shifted, axis=1, keepdims=True))
        p_scr[s] = probs
        probs_low = probs.astype(jnp.bfloat16).reshape(SH * L, L)
        plow_scr[s] = probs_low
        turned = mm(by_head_lanes(value[at].T), probs_low)
        context.append(turned.T.astype(jnp.bfloat16))
    context = jnp.concatenate(context, axis=0)

    middle = mixed + mm(context, w_out)
    scale_two = rms_scale(middle)
    unit_two = middle * scale_two
    normed_two = (unit_two * gain_two).astype(jnp.bfloat16)
    pre = mm(normed_two, wup_scr[...])
    square = pre * pre
    bend = jnp.tanh(GELU_RATE * pre * (1.0 + GELU_CUBE * square))
    half = 0.5 * (1.0 + bend)
    hidden = (pre * half).astype(jnp.bfloat16)
    slope = half + (0.5 * GELU_RATE) * pre * (1.0 - bend * bend) * (1.0 + 3.0 * GELU_CUBE * square)
    out_ref[...] = (middle + mm(hidden, w_back)).reshape(seqs, L, DS)

    grad_low = grad_out.astype(jnp.bfloat16)
    gback_scr[...] += mm(grad_low, hidden, TN)
    grad_pre = (mm(grad_low, w_back, NT) * slope).astype(jnp.bfloat16)
    gup_scr[...] += mm(normed_two, grad_pre, TN)
    back_two, gain_two_grad = norm_back(
        unit_two, scale_two, gain_two, mm(grad_pre, wup_scr[...], NT)
    )
    ggain_scr[1:2, :] += gain_two_grad
    grad_middle = grad_out + back_two
    grad_attended = grad_middle.astype(jnp.bfloat16)
    gproj_scr[...] += mm(context, grad_attended, TN)
    grad_context = mm(grad_attended, w_out, NT).astype(jnp.bfloat16)

    grad_query, grad_key, grad_value = [], [], []
    for s in range(seqs):
        at = slice(s * L, (s + 1) * L)
        grad_probs = mm(by_head_rows(value[at]), grad_context[at], NT).reshape(SH, L, L)
        probs = p_scr[s]
        row_dot = jnp.sum(probs * grad_probs, axis=1, keepdims=True)
        grad_scores = (probs * (grad_probs - row_dot)).astype(jnp.bfloat16).reshape(SH * L, L)
        gbias_scr[...] += grad_scores.astype(jnp.float32)
        turned = mm(by_head_lanes(key[at].T), grad_scores)
        grad_query.append(turned.T.astype(jnp.bfloat16))
        grad_key.append(mm(lanes_of(grad_scores), by_head_rows(query[at])).astype(jnp.bfloat16))
        grad_value.append(
            mm(lanes_of(plow_scr[s]), by_head_rows(grad_context[at])).astype(jnp.bfloat16)
        )
    grad_query = jnp.concatenate(grad_query, axis=0)
    grad_key = jnp.concatenate(grad_key, axis=0)
    grad_value = jnp.concatenate(grad_value, axis=0)

    grad_normed = mm(grad_query, wqkv_scr[0], NT)
    grad_normed += mm(grad_key, wqkv_scr[1], NT)
    grad_normed += mm(grad_value, wqkv_scr[2], NT)
    gqkv_scr[0] += mm(normed_one, grad_query, TN)
    gqkv_scr[1] += mm(normed_one, grad_key, TN)
    gqkv_scr[2] += mm(normed_one, grad_value, TN)
    back_one, gain_one_grad = norm_back(unit_one, scale_one, gain_one, grad_normed)
    ggain_scr[0:1, :] += gain_one_grad
    grad_mixed = grad_middle + back_one
    ig_ref[...] = (gate * grad_mixed).reshape(seqs, L, DS)
    grad_tap = ((1.0 - gate) * grad_mixed).astype(jnp.bfloat16)
    gdown_scr[...] += mm(grad_tap, taps, TN)
    ggain_scr[2:3, :] += jnp.sum(grad_mixed * (x - tapped), axis=0, keepdims=True)

    @pl.when(step == pl.num_programs(0) - 1)
    def _():
        low = lambda v: v.astype(jnp.bfloat16)
        pad = jnp.zeros((grow_ref.shape[0], grow_ref.shape[1] - DS), jnp.bfloat16)
        grow_ref[:, DS:] = pad
        grow_ref[0:D, 0:DS] = low(gdown_scr[...].T)
        spread = mm(pick_rows(3, 0, DS), low(gqkv_scr[0]), TN)
        for t in range(1, 3):
            spread = spread + mm(pick_rows(3, t, DS), low(gqkv_scr[t]), TN)
        grow_ref[at_qkv:at_out, 0:DS] = low(spread)
        grow_ref[at_out:at_up, 0:DS] = low(gproj_scr[...])
        spread = mm(pick_rows(4, 0, DS), low(gup_scr[:, 0:DS]), TN)
        for t in range(1, 4):
            spread = spread + mm(pick_rows(4, t, DS), low(gup_scr[:, t * DS : (t + 1) * DS]), TN)
        grow_ref[at_up:at_back, 0:DS] = low(spread)
        grow_ref[at_back : at_back + SFF, 0:DS] = low(gback_scr[...].T)
        flip_row = lax.broadcasted_iota(jnp.int32, (L, L), 0)
        flip_column = lax.broadcasted_iota(jnp.int32, (L, L), 1)
        flip = (flip_row + flip_column == L - 1).astype(jnp.float32)
        diagonals = []
        for head in range(SH):
            square = lax.dot_general(
                flip,
                gbias_scr[head * L : (head + 1) * L, :],
                NN,
                precision=PRECISE,
                preferred_element_type=jnp.float32,
            )
            full = jnp.concatenate([square, jnp.zeros_like(square)], axis=1)
            rolled = pltpu.roll(full, 0, 1, stride=1, stride_axis=0)
            diagonals.append(jnp.sum(rolled, axis=0, keepdims=True))
        diagonals = jnp.concatenate(diagonals, axis=0)
        gsmall_ref[...] = jnp.zeros_like(gsmall_ref)
        gsmall_ref[0:3, 0:DS] = ggain_scr[0:3, :] * jnp.concatenate(
            [jnp.ones((2, DS), jnp.float32), gate * (1.0 - gate)], axis=0
        )
        gsmall_ref[4 : 4 + SH, 0 : onehot_ref.shape[0]] = lax.dot_general(
            diagonals, onehot_ref[...], NT, precision=PRECISE, preferred_element_type=jnp.float32
        )


def side_part(meta, lengths, taps, side_input, output_grad, gains, w_rows, diag, onehot, seqs):
    own_seqs = side_input.shape[0]
    grid = own_seqs // seqs
    fixed = lambda *dims: pl.BlockSpec(dims, lambda i, m, n: (0,) * len(dims))
    block = pl.BlockSpec((seqs, L, DS), lambda i, m, n: (i, 0, 0))
    f32, bf16 = jnp.float32, jnp.bfloat16
    return pl.pallas_call(
        functools.partial(side_kernel, seqs),
        name="side",
        grid_spec=pltpu.PrefetchScalarGridSpec(
            num_scalar_prefetch=2,
            grid=(grid,),
            in_specs=[
                pl.BlockSpec((seqs * L, D), lambda i, m, n: (i, 0)),
                block,
                block,
                fixed(*gains.shape),
                fixed(*w_rows.shape),
                fixed(*diag.shape),
                fixed(*onehot.shape),
            ],
            out_specs=[block, block, fixed(w_rows.shape[0], L), fixed(16, L)],
            scratch_shapes=[
                pltpu.VMEM((3, DS, DS), bf16),
                pltpu.VMEM((DS, SFF), bf16),
                pltpu.VMEM((SH * L, L), f32),
                pltpu.VMEM((SH * L, L), f32),
                pltpu.VMEM((seqs, SH, L, L), f32),
                pltpu.VMEM((seqs, SH * L, L), bf16),
                pltpu.VMEM((DS, D), f32),
                pltpu.VMEM((3, DS, DS), f32),
                pltpu.VMEM((DS, DS), f32),
                pltpu.VMEM((DS, SFF), f32),
                pltpu.VMEM((DS, SFF), f32),
                pltpu.VMEM((8, DS), f32),
            ],
        ),
        out_shape=[
            jax.ShapeDtypeStruct(side_input.shape, f32),
            jax.ShapeDtypeStruct(side_input.shape, f32),
            jax.ShapeDtypeStruct((w_rows.shape[0], L), bf16),
            jax.ShapeDtypeStruct((16, L), f32),
        ],
        compiler_params=pltpu.CompilerParams(
            dimension_semantics=("arbitrary",), vmem_limit_bytes=56 * MIB
        ),
        cost_estimate=pl.CostEstimate(
            flops=own_seqs * 300_000_000,
            bytes_accessed=own_seqs * L * (2 * D + 16 * DS),
            transcendentals=own_seqs * L * (SH * L + SFF),
        ),
    )(meta, lengths, taps, side_input, output_grad, gains, w_rows, diag, onehot)


def adamw_update(weight_now, first_now, second_now, gradient, rate, decay_rate):
    first_new = BETA_ONE * first_now + (1.0 - BETA_ONE) * gradient
    second_new = BETA_TWO * second_now + (1.0 - BETA_TWO) * gradient * gradient
    first_hat = first_new / (1.0 - BETA_ONE**ADAM_STEP)
    second_hat = second_new / (1.0 - BETA_TWO**ADAM_STEP)
    weight_new = weight_now - rate * (
        first_hat / (jnp.sqrt(second_hat) + ADAM_EPS) + decay_rate * weight_now
    )
    return (first_new, second_new, weight_new)


def swap(values, distance):
    size = lax.axis_size("mp")
    return lax.ppermute(values, "mp", [(i, i ^ distance) for i in range(size)])


def exchange(values):
    return lax.all_to_all(values, ("batch", "mp"), split_axis=0, concat_axis=0, tiled=True)


def on_device(
    tokens,
    lengths,
    base_gains,
    base_qkv,
    base_out,
    base_up,
    base_down,
    base_table,
    side_input,
    output_grad,
    side_weights,
    weights_first,
    weights_second,
    side_gains,
    gains_first,
    gains_second,
    side_table,
    table_first,
    table_second,
):
    devices = lax.axis_size(("batch", "mp"))
    model_index = lax.axis_index("mp")
    own_seqs = side_input.shape[0]
    shard_rows = side_weights.shape[0] // DS
    buckets = side_table.shape[0]
    group = model_index // 2
    near = jnp.stack([model_index * own_seqs, model_index % 2, group]).astype(jnp.int32)
    far = jnp.stack([model_index * own_seqs, model_index % 2, 1 - group]).astype(jnp.int32)

    qkv_mate = swap(base_qkv, 1)
    qkv_far = swap(base_qkv, 2)
    qkv_far_mate = swap(qkv_far, 1)
    low_rows = side_weights.astype(jnp.bfloat16).reshape(1, shard_rows, DS)
    w_rows = exchange(jnp.broadcast_to(low_rows, (devices, shard_rows, DS)))
    w_rows = w_rows.reshape(devices * shard_rows, DS)

    onehot = jnp.asarray(diagonal_onehot(buckets))
    base_diag = jnp.dot(base_table.T, onehot, precision=PRECISE)
    side_diag = jnp.dot(side_table.T, onehot, precision=PRECISE)

    ctx_near = attention_part(
        near, lengths, tokens, base_gains, base_qkv, qkv_mate, base_diag, own_seqs, 2
    )
    ctx_far = attention_part(
        far, lengths, tokens, base_gains, qkv_far, qkv_far_mate, base_diag, own_seqs, 2
    )
    taps = ffn_part(
        near, ctx_near, ctx_far, tokens, base_gains, base_out, base_up, base_down, own_seqs, 4, 1024
    )
    side_output, input_grad, grad_rows, grad_small = side_part(
        near,
        lengths,
        taps,
        side_input,
        output_grad,
        side_gains,
        w_rows,
        side_diag,
        jnp.asarray(gradient_onehot(buckets)),
        2,
    )

    small_high = grad_small.astype(jnp.bfloat16)
    small_low = (grad_small - small_high.astype(jnp.float32)).astype(jnp.bfloat16)
    small = jnp.concatenate([small_high, small_low], axis=0)
    outgoing = jnp.concatenate(
        [
            grad_rows.reshape(devices, shard_rows, L),
            jnp.broadcast_to(small[None], (devices,) + small.shape),
        ],
        axis=1,
    )
    summed = jnp.sum(exchange(outgoing).astype(jnp.float32), axis=0)
    grad_shard = summed[:shard_rows, :DS]
    small_total = summed[shard_rows : shard_rows + 16] + summed[shard_rows + 16 :]
    gains_total = small_total[0:3, :DS]
    table_total = small_total[4 : 4 + SH, :buckets].T
    square = jnp.sum(grad_shard * grad_shard)
    squares = exchange(jnp.broadcast_to(square, (devices, L)))
    grad_norm = jnp.sqrt(
        jnp.sum(squares[:, 0])
        + jnp.sum(gains_total * gains_total)
        + jnp.sum(table_total * table_total)
    )
    factor = CLIP_NORM / jnp.maximum(grad_norm, CLIP_NORM)
    weights_moment, weights_square, weights_new = adamw_update(
        side_weights,
        weights_first,
        weights_second,
        factor * grad_shard.reshape(-1),
        RATE_MATRIX,
        WEIGHT_DECAY,
    )
    gains_moment, gains_square, gains_new = adamw_update(
        side_gains, gains_first, gains_second, factor * gains_total, RATE_SMALL, 0.0
    )
    table_moment, table_square, table_new = adamw_update(
        side_table, table_first, table_second, factor * table_total, RATE_SMALL, 0.0
    )
    return (
        side_output,
        input_grad,
        grad_norm,
        weights_moment,
        weights_square,
        weights_new,
        weights_new.astype(jnp.bfloat16),
        gains_moment,
        gains_square,
        gains_new,
        table_moment,
        table_square,
        table_new,
    )


def solution(mesh):
    return jax.shard_map(
        on_device,
        mesh=mesh,
        in_specs=(
            P("batch", None, None),
            P("batch"),
            P(),
            P(None, None, "mp"),
            P(),
            P(),
            P(),
            P(),
            P(("batch", "mp"), None, None),
            P(("batch", "mp"), None, None),
            P(("batch", "mp")),
            P(("batch", "mp")),
            P(("batch", "mp")),
            P(),
            P(),
            P(),
            P(),
            P(),
            P(),
        ),
        out_specs=(
            P(("batch", "mp"), None, None),
            P(("batch", "mp"), None, None),
            P(),
            P(("batch", "mp")),
            P(("batch", "mp")),
            P(("batch", "mp")),
            P(("batch", "mp")),
            P(),
            P(),
            P(),
            P(),
            P(),
            P(),
        ),
        check_vma=False,
    )
```

```python
import functools
import math
import jax
import jax.numpy as jnp
import numpy as np
from jax import lax
from jax.experimental import pallas as pl
from jax.experimental.pallas import tpu as pltpu
from jax.sharding import PartitionSpec as P

D = 768
HD = 64
DS = 96
SH = 12
SHD = 8
SFF = 384
MAXD = 128
L = 128
ADAM_STEP = 10
PAIR = 2 * HD
SPAN = 2 * L

NORM_EPS = 1e-06
CLIP_NORM = 1.0
BETA_ONE = 0.9
BETA_TWO = 0.999
ADAM_EPS = 1e-08
RATE_MATRIX = 0.1
RATE_SMALL = 0.5
WEIGHT_DECAY = 0.01
MASKED = -1e30
PRECISE = lax.Precision.HIGHEST
MIB = 1 << 20
GELU_RATE = math.sqrt(2.0 / math.pi)
GELU_CUBE = 0.044715

NN = (((1,), (0,)), ((), ()))
NT = (((1,), (1,)), ((), ()))
TN = (((0,), (0,)), ((), ()))


def mm(left, right, dims=NN):
    return lax.dot_general(left, right, dims, preferred_element_type=jnp.float32)


def bucket_of(offset, buckets, reach):
    half_count = buckets // 2
    exact_count = half_count // 2
    distance = np.abs(offset)
    spread_part = (
        np.log(np.maximum(distance, 1) / exact_count)
        / np.log(reach / exact_count)
        * (half_count - exact_count)
    )
    far_bucket = np.minimum(exact_count + np.floor(spread_part).astype(np.int32), half_count - 1)
    near_side = np.where(distance < exact_count, distance, far_bucket)
    return (near_side + (offset > 0) * half_count).astype(np.int32)


def diagonal_onehot(buckets):
    column = np.arange(SPAN)
    offset = np.where(column < L, -column, SPAN - column)
    onehot = bucket_of(offset, buckets, MAXD)[None, :] == np.arange(buckets)[:, None]
    onehot = onehot & (column != L)[None, :]
    return onehot.astype(np.float32)


def gradient_onehot(buckets):
    column = np.arange(SPAN)
    onehot = bucket_of(L - 1 - column, buckets, MAXD)[None, :] == np.arange(buckets)[:, None]
    onehot = onehot & (column != SPAN - 1)[None, :]
    return onehot.astype(np.float32)


def rms_scale(values):
    return lax.rsqrt(jnp.mean(values * values, axis=-1, keepdims=True) + NORM_EPS)


def gelu(v):
    return 0.5 * v * (1.0 + jnp.tanh(GELU_RATE * (v + GELU_CUBE * (v * v * v))))


def spread_bias(row):
    full = jnp.broadcast_to(row, (L, SPAN))
    return pltpu.roll(full, 0, 1, stride=1, stride_axis=0)[:, :L]


def attention_kernel(seqs, meta_ref, len_ref, tok_ref, gain_ref, own_ref, mate_ref, diag_ref, ctx_ref, w_scr, bias_scr):
    step = pl.program_id(0)
    third = own_ref.shape[1]
    width = 2 * third
    pairs = width // PAIR

    def place(low_ref, high_ref):
        for part in range(3):
            w_scr[part * width : part * width + third, :] = low_ref[part]
            w_scr[part * width + third : (part + 1) * width, :] = high_ref[part]

    @pl.when(step == 0)
    def _():
        @pl.when(meta_ref[1] == 0)
        def _():
            place(own_ref, mate_ref)

        @pl.when(meta_ref[1] == 1)
        def _():
            place(mate_ref, own_ref)

        for head in range(2 * pairs):
            bias_scr[head * L : (head + 1) * L, :] = spread_bias(
                diag_ref[pl.ds(meta_ref[2] * 2 * pairs + head, 1), :]
            )

    rows = tok_ref[...].reshape(seqs * L, D).astype(jnp.float32)
    normed = (rows * rms_scale(rows) * gain_ref[0:1, :]).astype(jnp.bfloat16)
    query = mm(w_scr[0:width, :], normed, NT).astype(jnp.bfloat16)
    key = mm(normed, w_scr[width : 2 * width, :], NT).astype(jnp.bfloat16)
    value = mm(w_scr[2 * width :, :], normed, NT).astype(jnp.bfloat16)
    low_lane = lax.broadcasted_iota(jnp.int32, (L, PAIR), 1) < HD
    low_row = lax.broadcasted_iota(jnp.int32, (PAIR, L), 0) < HD
    key_row = lax.broadcasted_iota(jnp.int32, (2, L, L), 1)
    for s in range(seqs):
        at = slice(s * L, (s + 1) * L)
        seen = key_row < len_ref[meta_ref[0] + step * seqs + s]
        for p in range(pairs):
            head = slice(p * PAIR, (p + 1) * PAIR)
            k_one, v_one = key[at, head], value[head, at]
            zero = jnp.zeros_like(k_one)
            k_two = jnp.concatenate(
                [jnp.where(low_lane, k_one, zero), jnp.where(low_lane, zero, k_one)], axis=0
            )
            v_two = jnp.concatenate(
                [jnp.where(low_row, v_one, zero), jnp.where(low_row, zero, v_one)], axis=1
            )
            scores = mm(k_two, query[head, at]) + bias_scr[p * 2 * L : (p + 1) * 2 * L, :]
            scores = jnp.where(seen, scores.reshape(2, L, L), MASKED)
            shifted = jnp.exp(scores - jnp.max(scores, axis=1, keepdims=True))
            scale = 1.0 / jnp.sum(shifted, axis=1, keepdims=True)
            scale = jnp.broadcast_to(scale, (2, HD, L)).reshape(PAIR, L)
            probs = shifted.astype(jnp.bfloat16).reshape(2 * L, L)
            ctx_ref[head, at] = (mm(v_two, probs) * scale).astype(jnp.bfloat16)


def attention_part(meta, lengths, tokens, gains, own, mate, diag, own_seqs, seqs):
    width = 2 * own.shape[1]
    fixed = lambda *dims: pl.BlockSpec(dims, lambda i, m, n: (0,) * len(dims))
    return pl.pallas_call(
        functools.partial(attention_kernel, seqs),
        name="attend",
        grid_spec=pltpu.PrefetchScalarGridSpec(
            num_scalar_prefetch=2,
            grid=(own_seqs // seqs,),
            in_specs=[
                pl.BlockSpec((seqs, L, D), lambda i, m, n: (m[0] // seqs + i, 0, 0)),
                fixed(2, D),
                fixed(*own.shape),
                fixed(*mate.shape),
                fixed(*diag.shape),
            ],
            out_specs=pl.BlockSpec((width, seqs * L), lambda i, m, n: (0, i)),
            scratch_shapes=[
                pltpu.VMEM((3 * width, D), jnp.bfloat16),
                pltpu.VMEM((width // HD * L, L), jnp.float32),
            ],
        ),
        out_shape=jax.ShapeDtypeStruct((width, own_seqs * L), jnp.bfloat16),
        compiler_params=pltpu.CompilerParams(
            dimension_semantics=("arbitrary",), vmem_limit_bytes=56 * MIB
        ),
        cost_estimate=pl.CostEstimate(
            flops=2 * own_seqs * L * width * (3 * D + 2 * L),
            bytes_accessed=own_seqs * L * (D + width) * 2 + 6 * D * width,
            transcendentals=own_seqs * width // HD * L * L,
        ),
    )(meta, lengths, tokens, gains, own, mate, diag)


def ffn_kernel(seqs, chunk, meta_ref, ca_ref, cb_ref, tok_ref, gain_ref, wa_ref, wb_ref, up_ref, down_ref, taps_ref):
    rows = tok_ref[...].reshape(seqs * L, D).astype(jnp.float32)
    middle = rows + mm(ca_ref[...], wa_ref[...], TN) + mm(cb_ref[...], wb_ref[...], TN)
    normed = (middle * rms_scale(middle) * gain_ref[1:2, :]).astype(jnp.bfloat16)
    total = jnp.zeros_like(middle)
    for c in range(0, up_ref.shape[1], chunk):
        hidden = gelu(mm(normed, up_ref[:, c : c + chunk])).astype(jnp.bfloat16)
        total = total + mm(hidden, down_ref[c : c + chunk, :])
    taps_ref[...] = (middle + total).astype(jnp.bfloat16)


def ffn_part(meta, ctx_a, ctx_b, tokens, gains, w_out, w_up, w_down, own_seqs, seqs, chunk):
    width = ctx_a.shape[0]
    grid = own_seqs // seqs
    ff = w_up.shape[1]
    fixed = lambda *dims: pl.BlockSpec(dims, lambda i, m: (0,) * len(dims))
    return pl.pallas_call(
        functools.partial(ffn_kernel, seqs, chunk),
        name="feed",
        grid_spec=pltpu.PrefetchScalarGridSpec(
            num_scalar_prefetch=1,
            grid=(grid,),
            in_specs=[
                pl.BlockSpec((width, seqs * L), lambda i, m: (0, i)),
                pl.BlockSpec((width, seqs * L), lambda i, m: (0, i)),
                pl.BlockSpec((seqs, L, D), lambda i, m: (m[0] // seqs + i, 0, 0)),
                fixed(2, D),
                pl.BlockSpec((width, D), lambda i, m: (m[2], 0)),
                pl.BlockSpec((width, D), lambda i, m: (1 - m[2], 0)),
                fixed(*w_up.shape),
                fixed(*w_down.shape),
            ],
            out_specs=pl.BlockSpec((seqs * L, D), lambda i, m: (i, 0)),
        ),
        out_shape=jax.ShapeDtypeStruct((own_seqs * L, D), jnp.bfloat16),
        compiler_params=pltpu.CompilerParams(
            dimension_semantics=("arbitrary",), vmem_limit_bytes=60 * MIB
        ),
        cost_estimate=pl.CostEstimate(
            flops=2 * own_seqs * L * D * (D + 2 * ff),
            bytes_accessed=own_seqs * L * 3 * D * 2 + 2 * D * (D + 2 * ff),
            transcendentals=own_seqs * L * ff,
        ),
    )(meta, ctx_a, ctx_b, tokens, gains, w_out, w_out, w_up, w_down)


def pick_rows(step, phase, count):
    row = lax.broadcasted_iota(jnp.int32, (count, step * count), 0)
    column = lax.broadcasted_iota(jnp.int32, (count, step * count), 1)
    return (column == step * row + phase).astype(jnp.bfloat16)


def by_head_rows(block):
    head = lax.broadcasted_iota(jnp.int32, block.shape, 1) // SHD
    zero = jnp.zeros_like(block)
    return jnp.concatenate([jnp.where(head == h, block, zero) for h in range(SH)], axis=0)


def by_head_lanes(block):
    head = lax.broadcasted_iota(jnp.int32, block.shape, 0) // SHD
    zero = jnp.zeros_like(block)
    return jnp.concatenate([jnp.where(head == h, block, zero) for h in range(SH)], axis=1)


def lanes_of(stacked):
    return jnp.concatenate([stacked[h * L : (h + 1) * L] for h in range(SH)], axis=1)


def norm_back(unit, scale, gain, grad):
    scaled = grad * gain
    return scale * (scaled - unit * jnp.mean(scaled * unit, axis=0, keepdims=True))


def two_by_head(turned, first):
    blocks = [by_head_rows(turned[:, s * L : (s + 1) * L].T) for s in (first, first + 1)]
    return jnp.concatenate(blocks, axis=1)


def two_apart(turned, first):
    zero = jnp.zeros((L, L), turned.dtype)
    one, two = turned[:, first * L : (first + 1) * L], turned[:, (first + 1) * L : (first + 2) * L]
    return jnp.concatenate(
        [jnp.concatenate([one, zero], axis=1), jnp.concatenate([zero, two], axis=1)], axis=0
    )


def column_scale(values):
    return lax.rsqrt(jnp.mean(values * values, axis=0, keepdims=True) + NORM_EPS)


def fold_lanes(values):
    total = values[:, 0:L]
    for s in range(1, values.shape[1] // L):
        total = total + values[:, s * L : (s + 1) * L]
    return total


def side_kernel(
    seqs,
    meta_ref,
    len_ref,
    taps_ref,
    x_ref,
    go_ref,
    gain_ref,
    w_ref,
    diag_ref,
    onehot_ref,
    out_ref,
    ig_ref,
    grow_ref,
    gsmall_ref,
    gain_scr,
    wdown_scr,
    wqkv_scr,
    wqkv_turn_scr,
    wout_turn_scr,
    wup_scr,
    wup_turn_scr,
    wback_turn_scr,
    bias_scr,
    gbias_scr,
    e_scr,
    elow_scr,
    gdown_scr,
    gqkv_scr,
    gproj_scr,
    gup_scr,
    gback_scr,
    ggain_scr,
):
    step = pl.program_id(0)
    at_qkv, at_out, at_up, at_back = D, D + 3 * DS, D + 4 * DS, D + 8 * DS
    low = lambda v: v.astype(jnp.bfloat16)

    @pl.when(step == 0)
    def _():
        wdown_scr[...] = w_ref[0:D, :].T
        for t in range(3):
            part = mm(pick_rows(3, t, DS), w_ref[at_qkv:at_out, :])
            wqkv_scr[t] = low(part)
            wqkv_turn_scr[t * L : t * L + DS, :] = low(part.T)
            wqkv_turn_scr[t * L + DS : (t + 1) * L, :] = jnp.zeros((L - DS, DS), jnp.bfloat16)
        wout_turn_scr[...] = w_ref[at_out:at_up, :].T
        for t in range(4):
            part = mm(pick_rows(4, t, DS), w_ref[at_up:at_back, :])
            wup_scr[:, t * DS : (t + 1) * DS] = low(part)
            wup_turn_scr[t * DS : (t + 1) * DS, :] = low(part.T)
        wback_turn_scr[...] = w_ref[at_back : at_back + SFF, :].T
        for row in range(3):
            wide = jnp.broadcast_to(gain_ref[row : row + 1, :], (L, DS)).T
            gain_scr[row] = jax.nn.sigmoid(wide) if row == 2 else wide
        for head in range(SH):
            bias_scr[head * L : (head + 1) * L, :] = spread_bias(diag_ref[head : head + 1, :])
        for ref in (gbias_scr, gdown_scr, gqkv_scr, gproj_scr, gup_scr, gback_scr, ggain_scr):
            ref[...] = jnp.zeros_like(ref)

    wide = lambda row: jnp.concatenate([gain_scr[row]] * seqs, axis=1)
    gain_one, gain_two, gate = wide(0), wide(1), wide(2)
    w_out = w_ref[at_out:at_up, :]
    w_back = w_ref[at_back : at_back + SFF, :]
    lengths = [len_ref[meta_ref[0] + step * seqs + s] for s in range(seqs)]
    key_row = lax.broadcasted_iota(jnp.int32, (SH, L, L), 1)
    token = lax.broadcasted_iota(jnp.int32, (DS, L), 1)
    taps = taps_ref[...]
    x = jnp.concatenate([x_ref[s] for s in range(seqs)], axis=1)
    grad_out = jnp.concatenate(
        [jnp.where(token < lengths[s], go_ref[s], 0.0) for s in range(seqs)], axis=1
    )

    tapped = mm(wdown_scr[...], taps, NT)
    mixed = gate * x + (1.0 - gate) * tapped
    scale_one = column_scale(mixed)
    unit_one = mixed * scale_one
    normed_one = low(unit_one * gain_one)
    qkv = low(mm(wqkv_turn_scr[...], normed_one))

    query, key, value = qkv[0:L], qkv[L : 2 * L], qkv[2 * L :]
    context, inverse = [], []
    for s in range(0, seqs, 2):
        score_two = mm(two_by_head(key, s), two_apart(query, s))
        for side in range(2):
            at = slice((s + side) * L, (s + side + 1) * L)
            scores = score_two[:, side * L : (side + 1) * L] + bias_scr[...]
            scores = jnp.where(key_row < lengths[s + side], scores.reshape(SH, L, L), MASKED)
            shifted = jnp.exp(scores - jnp.max(scores, axis=1, keepdims=True))
            e_scr[s + side] = shifted
            e_low = low(shifted).reshape(SH * L, L)
            elow_scr[s + side] = e_low
            total = 1.0 / jnp.sum(shifted, axis=1, keepdims=True)
            inverse.append(jnp.broadcast_to(total, (SH, SHD, L)).reshape(DS, L))
            context.append(mm(by_head_lanes(value[0:DS, at]), e_low) * inverse[-1])
    context = jnp.concatenate(context, axis=1)
    inverse = jnp.concatenate(inverse, axis=1)
    context_low = low(context)

    middle = mixed + mm(wout_turn_scr[...], context_low)
    scale_two = column_scale(middle)
    unit_two = middle * scale_two
    normed_two = low(unit_two * gain_two)
    pre = mm(wup_turn_scr[...], normed_two)
    square = pre * pre
    bend = jnp.tanh(GELU_RATE * pre * (1.0 + GELU_CUBE * square))
    half = 0.5 * (1.0 + bend)
    hidden = low(pre * half)
    slope = half + (0.5 * GELU_RATE) * pre * (1.0 - bend * bend) * (1.0 + 3.0 * GELU_CUBE * square)
    side_out = middle + mm(wback_turn_scr[...], hidden)

    grad_low = low(grad_out)
    gback_scr[...] += mm(hidden, grad_low, NT)
    grad_pre = low(mm(w_back, grad_low) * slope)
    gup_scr[...] += mm(normed_two, grad_pre, NT)
    grad_normed_two = mm(wup_scr[...], grad_pre)
    ggain_scr[1] += fold_lanes(grad_normed_two * unit_two)
    grad_middle = grad_out + norm_back(unit_two, scale_two, gain_two, grad_normed_two)
    grad_attended = low(grad_middle)
    gproj_scr[...] += mm(context_low, grad_attended, NT)
    grad_context = low(mm(w_out, grad_attended) * inverse)
    pad = jnp.zeros((L - DS, seqs * L), jnp.bfloat16)
    dots = (grad_context.astype(jnp.float32) * context).reshape(SH, SHD, seqs * L)
    dots = jnp.sum(dots, axis=1, keepdims=True)

    grad_context = jnp.concatenate([grad_context, pad], axis=0)
    grad_query, grad_key, grad_value = [], [], []
    for s in range(0, seqs, 2):
        prob_two = mm(two_by_head(value, s), two_apart(grad_context, s))
        for side in range(2):
            at = slice((s + side) * L, (s + side + 1) * L)
            grad_probs = prob_two[:, side * L : (side + 1) * L].reshape(SH, L, L)
            grad_scores = e_scr[s + side] * (grad_probs - dots[:, :, at])
            gbias_scr[...] += grad_scores.reshape(SH * L, L)
            grad_scores = low(grad_scores).reshape(SH * L, L)
            grad_query.append(low(mm(by_head_lanes(key[0:DS, at]), grad_scores)))
            grad_key.append(low(mm(lanes_of(grad_scores), by_head_rows(query[0:DS, at].T))))
            grad_value.append(
                low(mm(lanes_of(elow_scr[s + side]), by_head_rows(grad_context[0:DS, at].T)))
            )
    grad_query = jnp.concatenate(grad_query, axis=1)
    grad_key = jnp.concatenate(grad_key, axis=0)
    grad_value = jnp.concatenate(grad_value, axis=0)

    grad_normed = mm(wqkv_scr[0], grad_query)
    grad_normed += mm(wqkv_scr[1], grad_key, NT)
    grad_normed += mm(wqkv_scr[2], grad_value, NT)
    gqkv_scr[0] += mm(normed_one, grad_query, NT)
    gqkv_scr[1] += mm(normed_one, grad_key)
    gqkv_scr[2] += mm(normed_one, grad_value)
    ggain_scr[0] += fold_lanes(grad_normed * unit_one)
    grad_mixed = grad_middle + norm_back(unit_one, scale_one, gain_one, grad_normed)
    input_grad = gate * grad_mixed
    grad_tap = low((1.0 - gate) * grad_mixed)
    gdown_scr[...] += mm(grad_tap, taps)
    ggain_scr[2] += fold_lanes(grad_mixed * (x - tapped))
    for s in range(seqs):
        out_ref[s] = side_out[:, s * L : (s + 1) * L]
        ig_ref[s] = input_grad[:, s * L : (s + 1) * L]

    @pl.when(step == pl.num_programs(0) - 1)
    def _():
        grow_ref[:, DS:] = jnp.zeros((grow_ref.shape[0], grow_ref.shape[1] - DS), jnp.bfloat16)
        grow_ref[0:D, 0:DS] = low(gdown_scr[...].T)
        spread = mm(pick_rows(3, 0, DS), low(gqkv_scr[0]), TN)
        for t in range(1, 3):
            spread = spread + mm(pick_rows(3, t, DS), low(gqkv_scr[t]), TN)
        grow_ref[at_qkv:at_out, 0:DS] = low(spread)
        grow_ref[at_out:at_up, 0:DS] = low(gproj_scr[...])
        spread = mm(pick_rows(4, 0, DS), low(gup_scr[:, 0:DS]), TN)
        for t in range(1, 4):
            spread = spread + mm(pick_rows(4, t, DS), low(gup_scr[:, t * DS : (t + 1) * DS]), TN)
        grow_ref[at_up:at_back, 0:DS] = low(spread)
        grow_ref[at_back : at_back + SFF, 0:DS] = low(gback_scr[...])
        flip_row = lax.broadcasted_iota(jnp.int32, (L, L), 0)
        flip_column = lax.broadcasted_iota(jnp.int32, (L, L), 1)
        flip = (flip_row + flip_column == L - 1).astype(jnp.float32)
        diagonals = []
        for head in range(SH):
            square = lax.dot_general(
                flip,
                gbias_scr[head * L : (head + 1) * L, :],
                NN,
                precision=PRECISE,
                preferred_element_type=jnp.float32,
            )
            full = jnp.concatenate([square, jnp.zeros_like(square)], axis=1)
            rolled = pltpu.roll(full, 0, 1, stride=1, stride_axis=0)
            diagonals.append(jnp.sum(rolled, axis=0, keepdims=True))
        diagonals = jnp.concatenate(diagonals, axis=0)
        gsmall_ref[...] = jnp.zeros_like(gsmall_ref)
        for row in range(3):
            total = ggain_scr[row]
            if row == 2:
                total = total * (gain_scr[2] * (1.0 - gain_scr[2]))
            gsmall_ref[row : row + 1, 0:DS] = jnp.sum(total.T, axis=0, keepdims=True)
        gsmall_ref[4 : 4 + SH, 0 : onehot_ref.shape[0]] = lax.dot_general(
            diagonals, onehot_ref[...], NT, precision=PRECISE, preferred_element_type=jnp.float32
        )


def side_part(meta, lengths, taps, side_input, output_grad, gains, w_rows, diag, onehot, seqs):
    own_seqs = side_input.shape[0]
    grid = own_seqs // seqs
    fixed = lambda *dims: pl.BlockSpec(dims, lambda i, m, n: (0,) * len(dims))
    block = pl.BlockSpec((seqs, DS, L), lambda i, m, n: (i, 0, 0))
    f32, bf16 = jnp.float32, jnp.bfloat16
    return pl.pallas_call(
        functools.partial(side_kernel, seqs),
        name="side",
        grid_spec=pltpu.PrefetchScalarGridSpec(
            num_scalar_prefetch=2,
            grid=(grid,),
            in_specs=[
                pl.BlockSpec((seqs * L, D), lambda i, m, n: (i, 0)),
                block,
                block,
                fixed(*gains.shape),
                fixed(*w_rows.shape),
                fixed(*diag.shape),
                fixed(*onehot.shape),
            ],
            out_specs=[block, block, fixed(w_rows.shape[0], L), fixed(16, L)],
            scratch_shapes=[
                pltpu.VMEM((3, DS, L), f32),
                pltpu.VMEM((DS, D), bf16),
                pltpu.VMEM((3, DS, DS), bf16),
                pltpu.VMEM((3 * L, DS), bf16),
                pltpu.VMEM((DS, DS), bf16),
                pltpu.VMEM((DS, SFF), bf16),
                pltpu.VMEM((SFF, DS), bf16),
                pltpu.VMEM((DS, SFF), bf16),
                pltpu.VMEM((SH * L, L), f32),
                pltpu.VMEM((SH * L, L), f32),
                pltpu.VMEM((seqs, SH, L, L), f32),
                pltpu.VMEM((seqs, SH * L, L), bf16),
                pltpu.VMEM((DS, D), f32),
                pltpu.VMEM((3, DS, DS), f32),
                pltpu.VMEM((DS, DS), f32),
                pltpu.VMEM((DS, SFF), f32),
                pltpu.VMEM((SFF, DS), f32),
                pltpu.VMEM((3, DS, L), f32),
            ],
        ),
        out_shape=[
            jax.ShapeDtypeStruct(side_input.shape, f32),
            jax.ShapeDtypeStruct(side_input.shape, f32),
            jax.ShapeDtypeStruct((w_rows.shape[0], L), bf16),
            jax.ShapeDtypeStruct((16, L), f32),
        ],
        compiler_params=pltpu.CompilerParams(
            dimension_semantics=("arbitrary",), vmem_limit_bytes=56 * MIB
        ),
        cost_estimate=pl.CostEstimate(
            flops=own_seqs * 300_000_000,
            bytes_accessed=own_seqs * L * (2 * D + 16 * DS),
            transcendentals=own_seqs * L * (SH * L + SFF),
        ),
    )(meta, lengths, taps, side_input, output_grad, gains, w_rows, diag, onehot)


def adamw_update(weight_now, first_now, second_now, gradient, rate, decay_rate):
    first_new = BETA_ONE * first_now + (1.0 - BETA_ONE) * gradient
    second_new = BETA_TWO * second_now + (1.0 - BETA_TWO) * gradient * gradient
    first_hat = first_new / (1.0 - BETA_ONE**ADAM_STEP)
    second_hat = second_new / (1.0 - BETA_TWO**ADAM_STEP)
    weight_new = weight_now - rate * (
        first_hat / (jnp.sqrt(second_hat) + ADAM_EPS) + decay_rate * weight_now
    )
    return (first_new, second_new, weight_new)


def swap(values, distance):
    size = lax.axis_size("mp")
    return lax.ppermute(values, "mp", [(i, i ^ distance) for i in range(size)])


def exchange(values):
    return lax.all_to_all(values, ("batch", "mp"), split_axis=0, concat_axis=0, tiled=True)


def on_device(
    tokens,
    lengths,
    base_gains,
    base_qkv,
    base_out,
    base_up,
    base_down,
    base_table,
    side_input,
    output_grad,
    side_weights,
    weights_first,
    weights_second,
    side_gains,
    gains_first,
    gains_second,
    side_table,
    table_first,
    table_second,
):
    devices = lax.axis_size(("batch", "mp"))
    model_index = lax.axis_index("mp")
    own_seqs = side_input.shape[0]
    shard_rows = side_weights.shape[0] // DS
    buckets = side_table.shape[0]
    group = model_index // 2
    near = jnp.stack([model_index * own_seqs, model_index % 2, group]).astype(jnp.int32)
    far = jnp.stack([model_index * own_seqs, model_index % 2, 1 - group]).astype(jnp.int32)

    turn = lambda values: jnp.transpose(values, (0, 2, 1))
    qkv_own = turn(base_qkv)
    qkv_far = swap(qkv_own, 2)
    qkv_mate = swap(qkv_own, 1)

    onehot = jnp.asarray(diagonal_onehot(buckets))
    base_diag = jnp.dot(base_table.T, onehot, precision=PRECISE)
    side_diag = jnp.dot(side_table.T, onehot, precision=PRECISE)

    ctx_near = attention_part(
        near, lengths, tokens, base_gains, qkv_own, qkv_mate, base_diag, own_seqs, 8
    )
    ctx_near, qkv_far, low_rows = lax.optimization_barrier(
        (ctx_near, qkv_far, side_weights.astype(jnp.bfloat16).reshape(1, shard_rows, DS))
    )
    qkv_far_mate = swap(qkv_far, 1)
    w_rows = exchange(jnp.broadcast_to(low_rows, (devices, shard_rows, DS)))
    ctx_far = attention_part(
        far, lengths, tokens, base_gains, qkv_far, qkv_far_mate, base_diag, own_seqs, 8
    )
    taps = ffn_part(
        near, ctx_near, ctx_far, tokens, base_gains, base_out, base_up, base_down, own_seqs, 8, 1024
    )
    taps, w_rows = lax.optimization_barrier((taps, w_rows))
    w_rows = w_rows.reshape(devices * shard_rows, DS)
    side_output, input_grad, grad_rows, grad_small = side_part(
        near,
        lengths,
        taps,
        turn(side_input),
        turn(output_grad),
        side_gains,
        w_rows,
        side_diag,
        jnp.asarray(gradient_onehot(buckets)),
        8,
    )

    small_high = grad_small.astype(jnp.bfloat16)
    small_low = (grad_small - small_high.astype(jnp.float32)).astype(jnp.bfloat16)
    small = jnp.concatenate([small_high, small_low], axis=0)
    outgoing = jnp.concatenate(
        [
            grad_rows.reshape(devices, shard_rows, L),
            jnp.broadcast_to(small[None], (devices,) + small.shape),
        ],
        axis=1,
    )
    summed = jnp.sum(exchange(outgoing).astype(jnp.float32), axis=0)
    grad_shard = lax.optimization_barrier(summed[:shard_rows, :DS].reshape(-1))
    small_total = summed[shard_rows : shard_rows + 16] + summed[shard_rows + 16 :]
    gains_total = small_total[0:3, :DS]
    table_total = small_total[4 : 4 + SH, :buckets].T
    square = jnp.sum(grad_shard * grad_shard)
    squares = exchange(jnp.broadcast_to(square, (devices, L)))
    grad_norm = jnp.sqrt(
        jnp.sum(squares[:, 0])
        + jnp.sum(gains_total * gains_total)
        + jnp.sum(table_total * table_total)
    )
    factor = CLIP_NORM / jnp.maximum(grad_norm, CLIP_NORM)
    weights_moment, weights_square, weights_new = adamw_update(
        side_weights,
        weights_first,
        weights_second,
        factor * grad_shard,
        RATE_MATRIX,
        WEIGHT_DECAY,
    )
    gains_moment, gains_square, gains_new = adamw_update(
        side_gains, gains_first, gains_second, factor * gains_total, RATE_SMALL, 0.0
    )
    table_moment, table_square, table_new = adamw_update(
        side_table, table_first, table_second, factor * table_total, RATE_SMALL, 0.0
    )
    return (
        turn(side_output),
        turn(input_grad),
        grad_norm,
        weights_moment,
        weights_square,
        weights_new,
        weights_new.astype(jnp.bfloat16),
        gains_moment,
        gains_square,
        gains_new,
        table_moment,
        table_square,
        table_new,
    )


def solution(mesh):
    return jax.shard_map(
        on_device,
        mesh=mesh,
        in_specs=(
            P("batch", None, None),
            P("batch"),
            P(),
            P(None, None, "mp"),
            P(),
            P(),
            P(),
            P(),
            P(("batch", "mp"), None, None),
            P(("batch", "mp"), None, None),
            P(("batch", "mp")),
            P(("batch", "mp")),
            P(("batch", "mp")),
            P(),
            P(),
            P(),
            P(),
            P(),
            P(),
        ),
        out_specs=(
            P(("batch", "mp"), None, None),
            P(("batch", "mp"), None, None),
            P(),
            P(("batch", "mp")),
            P(("batch", "mp")),
            P(("batch", "mp")),
            P(("batch", "mp")),
            P(),
            P(),
            P(),
            P(),
            P(),
            P(),
        ),
        check_vma=False,
    )
```

```python
import functools
import math
import jax
import jax.numpy as jnp
import numpy as np
from jax import lax
from jax.experimental import pallas as pl
from jax.experimental.pallas import tpu as pltpu
from jax.sharding import PartitionSpec as P

D = 768
HD = 64
DS = 96
SH = 12
SHD = 8
SFF = 384
MAXD = 128
L = 128
ADAM_STEP = 10
PAIR = 2 * HD
SPAN = 2 * L

NORM_EPS = 1e-06
CLIP_NORM = 1.0
BETA_ONE = 0.9
BETA_TWO = 0.999
ADAM_EPS = 1e-08
RATE_MATRIX = 0.1
RATE_SMALL = 0.5
WEIGHT_DECAY = 0.01
MASKED = -1e30
PRECISE = lax.Precision.HIGHEST
MIB = 1 << 20
VMEM_MAIN = 60
GELU_RATE = math.sqrt(2.0 / math.pi)
GELU_CUBE = 0.044715

NN = (((1,), (0,)), ((), ()))
NT = (((1,), (1,)), ((), ()))
TN = (((0,), (0,)), ((), ()))


def mm(left, right, dims=NN):
    return lax.dot_general(left, right, dims, preferred_element_type=jnp.float32)


def bucket_of(offset, buckets, reach):
    half_count = buckets // 2
    exact_count = half_count // 2
    distance = np.abs(offset)
    spread_part = (
        np.log(np.maximum(distance, 1) / exact_count)
        / np.log(reach / exact_count)
        * (half_count - exact_count)
    )
    far_bucket = np.minimum(exact_count + np.floor(spread_part).astype(np.int32), half_count - 1)
    near_side = np.where(distance < exact_count, distance, far_bucket)
    return (near_side + (offset > 0) * half_count).astype(np.int32)


def diagonal_onehot(buckets):
    column = np.arange(SPAN)
    offset = np.where(column < L, -column, SPAN - column)
    onehot = bucket_of(offset, buckets, MAXD)[None, :] == np.arange(buckets)[:, None]
    onehot = onehot & (column != L)[None, :]
    return onehot.astype(np.float32)


def gradient_onehot(buckets):
    column = np.arange(SPAN)
    onehot = bucket_of(L - 1 - column, buckets, MAXD)[None, :] == np.arange(buckets)[:, None]
    onehot = onehot & (column != SPAN - 1)[None, :]
    return onehot.astype(np.float32)


def rms_scale(values):
    return lax.rsqrt(jnp.mean(values * values, axis=-1, keepdims=True) + NORM_EPS)


def gelu(v):
    return 0.5 * v * (1.0 + jnp.tanh(GELU_RATE * (v + GELU_CUBE * (v * v * v))))


def spread_bias(row):
    full = jnp.broadcast_to(row, (L, SPAN))
    return pltpu.roll(full, 0, 1, stride=1, stride_axis=0)[:, :L]


def attention_setup(parity, group, own_ref, mate_ref, diag_ref, w_scr, bias_scr):
    third = own_ref.shape[1]
    width = 2 * third
    heads = width // HD

    def place(low_ref, high_ref):
        for part in range(3):
            w_scr[part * width : part * width + third, :] = low_ref[part]
            w_scr[part * width + third : (part + 1) * width, :] = high_ref[part]

    @pl.when(parity == 0)
    def _():
        place(own_ref, mate_ref)

    @pl.when(parity == 1)
    def _():
        place(mate_ref, own_ref)

    for head in range(heads):
        bias_scr[head * L : (head + 1) * L, :] = spread_bias(
            diag_ref[pl.ds(group * heads + head, 1), :]
        )


def attention_block(lengths, rows, gain, w_scr, bias_scr, ctx_ref):
    width = w_scr.shape[0] // 3
    normed = (rows * rms_scale(rows) * gain).astype(jnp.bfloat16)
    query = mm(w_scr[0:width, :], normed, NT).astype(jnp.bfloat16)
    key = mm(normed, w_scr[width : 2 * width, :], NT).astype(jnp.bfloat16)
    value = mm(w_scr[2 * width :, :], normed, NT).astype(jnp.bfloat16)
    low_lane = lax.broadcasted_iota(jnp.int32, (L, PAIR), 1) < HD
    low_row = lax.broadcasted_iota(jnp.int32, (PAIR, L), 0) < HD
    key_row = lax.broadcasted_iota(jnp.int32, (2, L, L), 1)
    for s, length in enumerate(lengths):
        at = slice(s * L, (s + 1) * L)
        seen = key_row < length
        for p in range(width // PAIR):
            head = slice(p * PAIR, (p + 1) * PAIR)
            k_one, v_one = key[at, head], value[head, at]
            zero = jnp.zeros_like(k_one)
            k_two = jnp.concatenate(
                [jnp.where(low_lane, k_one, zero), jnp.where(low_lane, zero, k_one)], axis=0
            )
            v_two = jnp.concatenate(
                [jnp.where(low_row, v_one, zero), jnp.where(low_row, zero, v_one)], axis=1
            )
            scores = mm(k_two, query[head, at]) + bias_scr[p * 2 * L : (p + 1) * 2 * L, :]
            scores = jnp.where(seen, scores.reshape(2, L, L), MASKED)
            shifted = jnp.exp(scores - jnp.max(scores, axis=1, keepdims=True))
            scale = 1.0 / jnp.sum(shifted, axis=1, keepdims=True)
            scale = jnp.broadcast_to(scale, (2, HD, L)).reshape(PAIR, L)
            probs = shifted.astype(jnp.bfloat16).reshape(2 * L, L)
            ctx_ref[head, at] = (mm(v_two, probs) * scale).astype(jnp.bfloat16)


def near_kernel(seqs, meta_ref, len_ref, tok_ref, gain_ref, own_ref, mate_ref, diag_ref, ctx_ref, w_scr, bias_scr):
    step = pl.program_id(0)

    @pl.when(step == 0)
    def _():
        attention_setup(meta_ref[1], meta_ref[2], own_ref, mate_ref, diag_ref, w_scr, bias_scr)

    lengths = [len_ref[meta_ref[0] + step * seqs + s] for s in range(seqs)]
    rows = tok_ref[...].reshape(seqs * L, D).astype(jnp.float32)
    attention_block(lengths, rows, gain_ref[0:1, :], w_scr, bias_scr, ctx_ref)


def near_part(meta, lengths, tokens, gains, own, mate, diag, own_seqs, seqs):
    width = 2 * own.shape[1]
    fixed = lambda *dims: pl.BlockSpec(dims, lambda i, m, n: (0,) * len(dims))
    return pl.pallas_call(
        functools.partial(near_kernel, seqs),
        name="near",
        grid_spec=pltpu.PrefetchScalarGridSpec(
            num_scalar_prefetch=2,
            grid=(own_seqs // seqs,),
            in_specs=[
                pl.BlockSpec((seqs, L, D), lambda i, m, n: (m[0] // seqs + i, 0, 0)),
                fixed(2, D),
                fixed(*own.shape),
                fixed(*mate.shape),
                fixed(*diag.shape),
            ],
            out_specs=pl.BlockSpec((width, seqs * L), lambda i, m, n: (0, i)),
            scratch_shapes=[
                pltpu.VMEM((3 * width, D), jnp.bfloat16),
                pltpu.VMEM((width // HD * L, L), jnp.float32),
            ],
        ),
        out_shape=jax.ShapeDtypeStruct((width, own_seqs * L), jnp.bfloat16),
        compiler_params=pltpu.CompilerParams(
            dimension_semantics=("arbitrary",), vmem_limit_bytes=56 * MIB
        ),
        cost_estimate=pl.CostEstimate(
            flops=2 * own_seqs * L * width * (3 * D + 2 * L),
            bytes_accessed=own_seqs * L * (D + width) * 2 + 6 * D * width,
            transcendentals=own_seqs * width // HD * L * L,
        ),
    )(meta, lengths, tokens, gains, own, mate, diag)


def feed_block(chunk, rows, near, far, gain, wo_scr, up_scr, down_scr, taps_scr):
    width = near.shape[0]
    middle = rows + mm(near, wo_scr[0:width, :], TN) + mm(far, wo_scr[width:, :], TN)
    normed = (middle * rms_scale(middle) * gain).astype(jnp.bfloat16)
    total = jnp.zeros_like(middle)
    for c in range(0, up_scr.shape[1], chunk):
        hidden = gelu(mm(normed, up_scr[:, c : c + chunk])).astype(jnp.bfloat16)
        total = total + mm(hidden, down_scr[c : c + chunk, :])
    taps_scr[...] = (middle + total).astype(jnp.bfloat16)


def pick_rows(step, phase, count):
    row = lax.broadcasted_iota(jnp.int32, (count, step * count), 0)
    column = lax.broadcasted_iota(jnp.int32, (count, step * count), 1)
    return (column == step * row + phase).astype(jnp.bfloat16)


def by_head_rows(block):
    head = lax.broadcasted_iota(jnp.int32, block.shape, 1) // SHD
    zero = jnp.zeros_like(block)
    return jnp.concatenate([jnp.where(head == h, block, zero) for h in range(SH)], axis=0)


def by_head_lanes(block):
    head = lax.broadcasted_iota(jnp.int32, block.shape, 0) // SHD
    zero = jnp.zeros_like(block)
    return jnp.concatenate([jnp.where(head == h, block, zero) for h in range(SH)], axis=1)


def lanes_of(stacked):
    return jnp.concatenate([stacked[h * L : (h + 1) * L] for h in range(SH)], axis=1)


def norm_back(unit, scale, gain, grad):
    scaled = grad * gain
    return scale * (scaled - unit * jnp.mean(scaled * unit, axis=0, keepdims=True))


def two_by_head(turned, first):
    blocks = [by_head_rows(turned[:, s * L : (s + 1) * L].T) for s in (first, first + 1)]
    return jnp.concatenate(blocks, axis=1)


def two_apart(turned, first):
    zero = jnp.zeros((L, L), turned.dtype)
    one, two = turned[:, first * L : (first + 1) * L], turned[:, (first + 1) * L : (first + 2) * L]
    return jnp.concatenate(
        [jnp.concatenate([one, zero], axis=1), jnp.concatenate([zero, two], axis=1)], axis=0
    )


def column_scale(values):
    return lax.rsqrt(jnp.mean(values * values, axis=0, keepdims=True) + NORM_EPS)


def fold_lanes(values):
    total = values[:, 0:L]
    for s in range(1, values.shape[1] // L):
        total = total + values[:, s * L : (s + 1) * L]
    return total


AT_QKV, AT_OUT, AT_UP, AT_BACK, AT_END = D, D + 3 * DS, D + 4 * DS, D + 8 * DS, D + 8 * DS + SFF


def low(values):
    return values.astype(jnp.bfloat16)


def side_setup(gain_ref, w_ref, diag_ref, scratch):
    (
        gain_scr,
        wdown_scr,
        wqkv_scr,
        wqkv_turn_scr,
        wout_turn_scr,
        wup_scr,
        wup_turn_scr,
        wback_turn_scr,
        bias_scr,
        gbias_scr,
        elow_scr,
        gdown_scr,
        gqkv_scr,
        gproj_scr,
        gup_scr,
        gback_scr,
        ggain_scr,
    ) = scratch
    wdown_scr[...] = w_ref[0:D, :].T
    for t in range(3):
        part = mm(pick_rows(3, t, DS), w_ref[AT_QKV:AT_OUT, :])
        wqkv_scr[t] = low(part)
        wqkv_turn_scr[t * L : t * L + DS, :] = low(part.T)
        wqkv_turn_scr[t * L + DS : (t + 1) * L, :] = jnp.zeros((L - DS, DS), jnp.bfloat16)
    wout_turn_scr[...] = w_ref[AT_OUT:AT_UP, :].T
    for t in range(4):
        part = mm(pick_rows(4, t, DS), w_ref[AT_UP:AT_BACK, :])
        wup_scr[:, t * DS : (t + 1) * DS] = low(part)
        wup_turn_scr[t * DS : (t + 1) * DS, :] = low(part.T)
    wback_turn_scr[...] = w_ref[AT_BACK : AT_END, :].T
    for row in range(3):
        wide = jnp.broadcast_to(gain_ref[row : row + 1, :], (L, DS)).T
        gain_scr[row] = jax.nn.sigmoid(wide) if row == 2 else wide
    for head in range(SH):
        bias_scr[head * L : (head + 1) * L, :] = spread_bias(diag_ref[head : head + 1, :])
    for ref in (gbias_scr, gdown_scr, gqkv_scr, gproj_scr, gup_scr, gback_scr, ggain_scr):
        ref[...] = jnp.zeros_like(ref)


def side_block(lengths, taps_scr, x_ref, go_ref, w_ref, out_ref, ig_ref, scratch):
    (
        gain_scr,
        wdown_scr,
        wqkv_scr,
        wqkv_turn_scr,
        wout_turn_scr,
        wup_scr,
        wup_turn_scr,
        wback_turn_scr,
        bias_scr,
        gbias_scr,
        elow_scr,
        gdown_scr,
        gqkv_scr,
        gproj_scr,
        gup_scr,
        gback_scr,
        ggain_scr,
    ) = scratch
    seqs = len(lengths)
    wide = lambda row: jnp.concatenate([gain_scr[row]] * seqs, axis=1)
    gain_one, gain_two, gate = wide(0), wide(1), wide(2)
    w_out = w_ref[AT_OUT:AT_UP, :]
    w_back = w_ref[AT_BACK : AT_END, :]
    key_row = lax.broadcasted_iota(jnp.int32, (SH, L, L), 1)
    token = lax.broadcasted_iota(jnp.int32, (DS, L), 1)
    taps = taps_scr[...]
    x = jnp.concatenate([x_ref[s] for s in range(seqs)], axis=1)
    grad_out = jnp.concatenate(
        [jnp.where(token < lengths[s], go_ref[s], 0.0) for s in range(seqs)], axis=1
    )

    tapped = mm(wdown_scr[...], taps, NT)
    mixed = gate * x + (1.0 - gate) * tapped
    scale_one = column_scale(mixed)
    unit_one = mixed * scale_one
    normed_one = low(unit_one * gain_one)
    qkv = low(mm(wqkv_turn_scr[...], normed_one))

    query, key, value = qkv[0:L], qkv[L : 2 * L], qkv[2 * L :]
    context, inverse = [], []
    for s in range(0, seqs, 2):
        score_two = mm(two_by_head(key, s), two_apart(query, s))
        for side in range(2):
            at = slice((s + side) * L, (s + side + 1) * L)
            scores = score_two[:, side * L : (side + 1) * L] + bias_scr[...]
            scores = jnp.where(key_row < lengths[s + side], scores.reshape(SH, L, L), MASKED)
            shifted = jnp.exp(scores - jnp.max(scores, axis=1, keepdims=True))
            e_low = low(shifted).reshape(SH * L, L)
            elow_scr[s + side] = e_low
            total = 1.0 / jnp.sum(shifted, axis=1, keepdims=True)
            inverse.append(jnp.broadcast_to(total, (SH, SHD, L)).reshape(DS, L))
            context.append(mm(by_head_lanes(value[0:DS, at]), e_low) * inverse[-1])
    context = jnp.concatenate(context, axis=1)
    inverse = jnp.concatenate(inverse, axis=1)
    context_low = low(context)

    middle = mixed + mm(wout_turn_scr[...], context_low)
    scale_two = column_scale(middle)
    unit_two = middle * scale_two
    normed_two = low(unit_two * gain_two)
    pre = mm(wup_turn_scr[...], normed_two)
    square = pre * pre
    bend = jnp.tanh(GELU_RATE * pre * (1.0 + GELU_CUBE * square))
    half = 0.5 * (1.0 + bend)
    hidden = low(pre * half)
    slope = half + (0.5 * GELU_RATE) * pre * (1.0 - bend * bend) * (1.0 + 3.0 * GELU_CUBE * square)
    side_out = middle + mm(wback_turn_scr[...], hidden)

    grad_low = low(grad_out)
    gback_scr[...] += mm(hidden, grad_low, NT)
    grad_pre = low(mm(w_back, grad_low) * slope)
    gup_scr[...] += mm(normed_two, grad_pre, NT)
    grad_normed_two = mm(wup_scr[...], grad_pre)
    ggain_scr[1] += fold_lanes(grad_normed_two * unit_two)
    grad_middle = grad_out + norm_back(unit_two, scale_two, gain_two, grad_normed_two)
    grad_attended = low(grad_middle)
    gproj_scr[...] += mm(context_low, grad_attended, NT)
    grad_context = low(mm(w_out, grad_attended) * inverse)
    pad = jnp.zeros((L - DS, seqs * L), jnp.bfloat16)
    dots = (grad_context.astype(jnp.float32) * context).reshape(SH, SHD, seqs * L)
    dots = jnp.sum(dots, axis=1, keepdims=True)

    grad_context = jnp.concatenate([grad_context, pad], axis=0)
    grad_query, grad_key, grad_value = [], [], []
    for s in range(0, seqs, 2):
        prob_two = mm(two_by_head(value, s), two_apart(grad_context, s))
        for side in range(2):
            at = slice((s + side) * L, (s + side + 1) * L)
            grad_probs = prob_two[:, side * L : (side + 1) * L].reshape(SH, L, L)
            grad_scores = elow_scr[s + side].astype(jnp.float32).reshape(SH, L, L) * (
                grad_probs - dots[:, :, at]
            )
            gbias_scr[...] += grad_scores.reshape(SH * L, L)
            grad_scores = low(grad_scores).reshape(SH * L, L)
            grad_query.append(low(mm(by_head_lanes(key[0:DS, at]), grad_scores)))
            grad_key.append(low(mm(lanes_of(grad_scores), by_head_rows(query[0:DS, at].T))))
            grad_value.append(
                low(mm(lanes_of(elow_scr[s + side]), by_head_rows(grad_context[0:DS, at].T)))
            )
    grad_query = jnp.concatenate(grad_query, axis=1)
    grad_key = jnp.concatenate(grad_key, axis=0)
    grad_value = jnp.concatenate(grad_value, axis=0)

    grad_normed = mm(wqkv_scr[0], grad_query)
    grad_normed += mm(wqkv_scr[1], grad_key, NT)
    grad_normed += mm(wqkv_scr[2], grad_value, NT)
    gqkv_scr[0] += mm(normed_one, grad_query, NT)
    gqkv_scr[1] += mm(normed_one, grad_key)
    gqkv_scr[2] += mm(normed_one, grad_value)
    ggain_scr[0] += fold_lanes(grad_normed * unit_one)
    grad_mixed = grad_middle + norm_back(unit_one, scale_one, gain_one, grad_normed)
    input_grad = gate * grad_mixed
    grad_tap = low((1.0 - gate) * grad_mixed)
    gdown_scr[...] += mm(grad_tap, taps)
    ggain_scr[2] += fold_lanes(grad_mixed * (x - tapped))
    for s in range(seqs):
        out_ref[s] = side_out[:, s * L : (s + 1) * L]
        ig_ref[s] = input_grad[:, s * L : (s + 1) * L]


def side_finish(onehot_ref, send_ref, grow_scr, scratch):
    (
        gain_scr,
        wdown_scr,
        wqkv_scr,
        wqkv_turn_scr,
        wout_turn_scr,
        wup_scr,
        wup_turn_scr,
        wback_turn_scr,
        bias_scr,
        gbias_scr,
        elow_scr,
        gdown_scr,
        gqkv_scr,
        gproj_scr,
        gup_scr,
        gback_scr,
        ggain_scr,
    ) = scratch
    grow_scr[:, DS:] = jnp.zeros((grow_scr.shape[0], grow_scr.shape[1] - DS), jnp.bfloat16)
    grow_scr[0:D, 0:DS] = low(gdown_scr[...].T)
    spread = mm(pick_rows(3, 0, DS), low(gqkv_scr[0]), TN)
    for t in range(1, 3):
        spread = spread + mm(pick_rows(3, t, DS), low(gqkv_scr[t]), TN)
    grow_scr[AT_QKV:AT_OUT, 0:DS] = low(spread)
    grow_scr[AT_OUT:AT_UP, 0:DS] = low(gproj_scr[...])
    spread = mm(pick_rows(4, 0, DS), low(gup_scr[:, 0:DS]), TN)
    for t in range(1, 4):
        spread = spread + mm(pick_rows(4, t, DS), low(gup_scr[:, t * DS : (t + 1) * DS]), TN)
    grow_scr[AT_UP:AT_BACK, 0:DS] = low(spread)
    grow_scr[AT_BACK : AT_END, 0:DS] = low(gback_scr[...])
    flip_row = lax.broadcasted_iota(jnp.int32, (L, L), 0)
    flip_column = lax.broadcasted_iota(jnp.int32, (L, L), 1)
    flip = (flip_row + flip_column == L - 1).astype(jnp.float32)
    diagonals = []
    for head in range(SH):
        square = lax.dot_general(
            flip,
            gbias_scr[head * L : (head + 1) * L, :],
            NN,
            precision=PRECISE,
            preferred_element_type=jnp.float32,
        )
        full = jnp.concatenate([square, jnp.zeros_like(square)], axis=1)
        rolled = pltpu.roll(full, 0, 1, stride=1, stride_axis=0)
        diagonals.append(jnp.sum(rolled, axis=0, keepdims=True))
    diagonals = jnp.concatenate(diagonals, axis=0)
    shard_rows = AT_END // send_ref.shape[0]
    small = shard_rows + SH
    for device in range(send_ref.shape[0]):
        send_ref[device, 0:shard_rows, :] = grow_scr[
            device * shard_rows : (device + 1) * shard_rows, :
        ]
    gains = []
    for row in range(3):
        total = ggain_scr[row]
        if row == 2:
            total = total * (gain_scr[2] * (1.0 - gain_scr[2]))
        gains.append(jnp.sum(total.T, axis=0, keepdims=True))
    gains.append(jnp.zeros((SH - 3, DS), jnp.float32))
    table = lax.dot_general(
        diagonals, onehot_ref[...], NT, precision=PRECISE, preferred_element_type=jnp.float32
    )
    extra = low(jnp.concatenate([jnp.concatenate(gains, axis=0), table], axis=1))
    blank = jnp.zeros((send_ref.shape[1] - small, L), jnp.bfloat16)
    for device in range(send_ref.shape[0]):
        send_ref[device, shard_rows:small, :] = extra
        if small < send_ref.shape[1]:
            send_ref[device, small:, :] = blank


def main_kernel(
    seqs,
    chunk,
    meta_ref,
    len_ref,
    tok_ref,
    gain_ref,
    far_ref,
    mate_ref,
    diag_ref,
    near_ref,
    x_ref,
    go_ref,
    side_gain_ref,
    side_diag_ref,
    onehot_ref,
    wo_hbm,
    up_hbm,
    down_hbm,
    w_hbm,
    out_ref,
    ig_ref,
    send_ref,
    w_scr,
    bias_scr,
    ctx_scr,
    taps_scr,
    wo_scr,
    up_scr,
    down_scr,
    wrow_scr,
    grow_scr,
    sems,
    *scratch,
):
    step = pl.program_id(0)
    group = meta_ref[2]
    width = near_ref.shape[0]
    copies = [
        pltpu.make_async_copy(
            wo_hbm.at[pl.ds(group * width, width), :], wo_scr.at[pl.ds(0, width), :], sems.at[0]
        ),
        pltpu.make_async_copy(
            wo_hbm.at[pl.ds((1 - group) * width, width), :],
            wo_scr.at[pl.ds(width, width), :],
            sems.at[1],
        ),
        pltpu.make_async_copy(up_hbm, up_scr, sems.at[2]),
        pltpu.make_async_copy(down_hbm, down_scr, sems.at[3]),
        pltpu.make_async_copy(w_hbm, wrow_scr, sems.at[4]),
    ]

    @pl.when(step == 0)
    def _():
        for copy in copies:
            copy.start()
        attention_setup(meta_ref[1], 1 - group, far_ref, mate_ref, diag_ref, w_scr, bias_scr)

    lengths = [len_ref[meta_ref[0] + step * seqs + s] for s in range(seqs)]
    rows = tok_ref[...].reshape(seqs * L, D).astype(jnp.float32)
    attention_block(lengths, rows, gain_ref[0:1, :], w_scr, bias_scr, ctx_scr)

    @pl.when(step == 0)
    def _():
        for copy in copies:
            copy.wait()
        side_setup(side_gain_ref, wrow_scr, side_diag_ref, scratch)

    rows = tok_ref[...].reshape(seqs * L, D).astype(jnp.float32)
    feed_block(
        chunk, rows, near_ref[...], ctx_scr[...], gain_ref[1:2, :], wo_scr, up_scr, down_scr, taps_scr
    )
    side_block(lengths, taps_scr, x_ref, go_ref, wrow_scr, out_ref, ig_ref, scratch)

    @pl.when(step == pl.num_programs(0) - 1)
    def _():
        side_finish(onehot_ref, send_ref, grow_scr, scratch)


def main_part(
    meta,
    lengths,
    tokens,
    gains,
    far,
    mate,
    diag,
    ctx_near,
    side_input,
    output_grad,
    side_gains,
    side_diag,
    onehot,
    w_out,
    w_up,
    w_down,
    w_rows,
    devices,
    seqs,
    chunk,
):
    own_seqs = side_input.shape[0]
    width = ctx_near.shape[0]
    ff = w_up.shape[1]
    send_rows = -(-(w_rows.shape[0] // devices + SH) // 8) * 8
    fixed = lambda *dims: pl.BlockSpec(dims, lambda i, m, n: (0,) * len(dims))
    block = pl.BlockSpec((seqs, DS, L), lambda i, m, n: (i, 0, 0))
    hbm = pl.BlockSpec(memory_space=pl.ANY)
    f32, bf16 = jnp.float32, jnp.bfloat16
    return pl.pallas_call(
        functools.partial(main_kernel, seqs, chunk),
        name="main",
        grid_spec=pltpu.PrefetchScalarGridSpec(
            num_scalar_prefetch=2,
            grid=(own_seqs // seqs,),
            in_specs=[
                pl.BlockSpec((seqs, L, D), lambda i, m, n: (m[0] // seqs + i, 0, 0)),
                fixed(2, D),
                fixed(*far.shape),
                fixed(*mate.shape),
                fixed(*diag.shape),
                pl.BlockSpec((width, seqs * L), lambda i, m, n: (0, i)),
                block,
                block,
                fixed(*side_gains.shape),
                fixed(*side_diag.shape),
                fixed(*onehot.shape),
                hbm,
                hbm,
                hbm,
                hbm,
            ],
            out_specs=[block, block, fixed(devices, send_rows, L)],
            scratch_shapes=[
                pltpu.VMEM((3 * width, D), bf16),
                pltpu.VMEM((width // HD * L, L), f32),
                pltpu.VMEM((width, seqs * L), bf16),
                pltpu.VMEM((seqs * L, D), bf16),
                pltpu.VMEM(w_out.shape, bf16),
                pltpu.VMEM(w_up.shape, bf16),
                pltpu.VMEM(w_down.shape, bf16),
                pltpu.VMEM(w_rows.shape, bf16),
                pltpu.VMEM((w_rows.shape[0], L), bf16),
                pltpu.SemaphoreType.DMA((5,)),
                pltpu.VMEM((3, DS, L), f32),
                pltpu.VMEM((DS, D), bf16),
                pltpu.VMEM((3, DS, DS), bf16),
                pltpu.VMEM((3 * L, DS), bf16),
                pltpu.VMEM((DS, DS), bf16),
                pltpu.VMEM((DS, SFF), bf16),
                pltpu.VMEM((SFF, DS), bf16),
                pltpu.VMEM((DS, SFF), bf16),
                pltpu.VMEM((SH * L, L), f32),
                pltpu.VMEM((SH * L, L), f32),
                pltpu.VMEM((seqs, SH * L, L), bf16),
                pltpu.VMEM((DS, D), f32),
                pltpu.VMEM((3, DS, DS), f32),
                pltpu.VMEM((DS, DS), f32),
                pltpu.VMEM((DS, SFF), f32),
                pltpu.VMEM((SFF, DS), f32),
                pltpu.VMEM((3, DS, L), f32),
            ],
        ),
        out_shape=[
            jax.ShapeDtypeStruct(side_input.shape, f32),
            jax.ShapeDtypeStruct(side_input.shape, f32),
            jax.ShapeDtypeStruct((devices, send_rows, L), bf16),
        ],
        compiler_params=pltpu.CompilerParams(
            dimension_semantics=("arbitrary",), vmem_limit_bytes=VMEM_MAIN * MIB
        ),
        cost_estimate=pl.CostEstimate(
            flops=2 * own_seqs * L * (D * (D + 2 * ff) + width * (3 * D + 2 * L))
            + own_seqs * 300_000_000,
            bytes_accessed=own_seqs * L * (3 * D + 16 * DS) + 2 * D * (D + 2 * ff),
            transcendentals=own_seqs * L * (ff + 2 * SH * L + SFF),
        ),
    )(
        meta,
        lengths,
        tokens,
        gains,
        far,
        mate,
        diag,
        ctx_near,
        side_input,
        output_grad,
        side_gains,
        side_diag,
        onehot,
        w_out,
        w_up,
        w_down,
        w_rows,
    )


def adamw_update(weight_now, first_now, second_now, gradient, rate, decay_rate):
    first_new = BETA_ONE * first_now + (1.0 - BETA_ONE) * gradient
    second_new = BETA_TWO * second_now + (1.0 - BETA_TWO) * gradient * gradient
    first_hat = first_new / (1.0 - BETA_ONE**ADAM_STEP)
    second_hat = second_new / (1.0 - BETA_TWO**ADAM_STEP)
    weight_new = weight_now - rate * (
        first_hat / (jnp.sqrt(second_hat) + ADAM_EPS) + decay_rate * weight_now
    )
    return (first_new, second_new, weight_new)


def swap(values, distance):
    size = lax.axis_size("mp")
    return lax.ppermute(values, "mp", [(i, i ^ distance) for i in range(size)])


def exchange(values):
    return lax.all_to_all(values, ("batch", "mp"), split_axis=0, concat_axis=0, tiled=True)


def on_device(
    tokens,
    lengths,
    base_gains,
    base_qkv,
    base_out,
    base_up,
    base_down,
    base_table,
    side_input,
    output_grad,
    side_weights,
    weights_first,
    weights_second,
    side_gains,
    gains_first,
    gains_second,
    side_table,
    table_first,
    table_second,
):
    devices = lax.axis_size(("batch", "mp"))
    model_index = lax.axis_index("mp")
    own_seqs = side_input.shape[0]
    shard_rows = side_weights.shape[0] // DS
    buckets = side_table.shape[0]
    meta = jnp.stack([model_index * own_seqs, model_index % 2, model_index // 2]).astype(jnp.int32)

    turn = lambda values: jnp.transpose(values, (0, 2, 1))
    qkv_own = turn(base_qkv)
    qkv_far = swap(qkv_own, 2)
    qkv_mate = swap(qkv_own, 1)
    low_rows = side_weights.astype(jnp.bfloat16).reshape(1, shard_rows, DS)
    w_rows = exchange(jnp.broadcast_to(low_rows, (devices, shard_rows, DS)))

    onehot = jnp.asarray(diagonal_onehot(buckets))
    base_diag = jnp.dot(base_table.T, onehot, precision=PRECISE)
    side_diag = jnp.dot(side_table.T, onehot, precision=PRECISE)

    ctx_near = near_part(
        meta, lengths, tokens, base_gains, qkv_own, qkv_mate, base_diag, own_seqs, 8
    )
    ctx_near, qkv_far, w_rows = lax.optimization_barrier((ctx_near, qkv_far, w_rows))
    side_output, input_grad, outgoing = main_part(
        meta,
        lengths,
        tokens,
        base_gains,
        qkv_far,
        swap(qkv_far, 1),
        base_diag,
        ctx_near,
        turn(side_input),
        turn(output_grad),
        side_gains,
        side_diag,
        jnp.asarray(gradient_onehot(buckets)),
        base_out,
        base_up,
        base_down,
        w_rows.reshape(devices * shard_rows, DS),
        devices,
        8,
        1024,
    )

    summed = jnp.sum(exchange(outgoing).astype(jnp.float32), axis=0)
    grad_shard = lax.optimization_barrier(summed[:shard_rows, :DS].reshape(-1))
    small_total = summed[shard_rows : shard_rows + SH]
    gains_total = small_total[0:3, :DS]
    table_total = small_total[:, DS : DS + buckets].T
    square = jnp.sum(grad_shard * grad_shard)
    squares = exchange(jnp.broadcast_to(square, (devices, L)))
    grad_norm = jnp.sqrt(
        jnp.sum(squares[:, 0])
        + jnp.sum(gains_total * gains_total)
        + jnp.sum(table_total * table_total)
    )
    factor = CLIP_NORM / jnp.maximum(grad_norm, CLIP_NORM)
    weights_moment, weights_square, weights_new = adamw_update(
        side_weights,
        weights_first,
        weights_second,
        factor * grad_shard,
        RATE_MATRIX,
        WEIGHT_DECAY,
    )
    gains_moment, gains_square, gains_new = adamw_update(
        side_gains, gains_first, gains_second, factor * gains_total, RATE_SMALL, 0.0
    )
    table_moment, table_square, table_new = adamw_update(
        side_table, table_first, table_second, factor * table_total, RATE_SMALL, 0.0
    )
    return (
        turn(side_output),
        turn(input_grad),
        grad_norm,
        weights_moment,
        weights_square,
        weights_new,
        weights_new.astype(jnp.bfloat16),
        gains_moment,
        gains_square,
        gains_new,
        table_moment,
        table_square,
        table_new,
    )


def solution(mesh):
    return jax.shard_map(
        on_device,
        mesh=mesh,
        in_specs=(
            P("batch", None, None),
            P("batch"),
            P(),
            P(None, None, "mp"),
            P(),
            P(),
            P(),
            P(),
            P(("batch", "mp"), None, None),
            P(("batch", "mp"), None, None),
            P(("batch", "mp")),
            P(("batch", "mp")),
            P(("batch", "mp")),
            P(),
            P(),
            P(),
            P(),
            P(),
            P(),
        ),
        out_specs=(
            P(("batch", "mp"), None, None),
            P(("batch", "mp"), None, None),
            P(),
            P(("batch", "mp")),
            P(("batch", "mp")),
            P(("batch", "mp")),
            P(("batch", "mp")),
            P(),
            P(),
            P(),
            P(),
            P(),
            P(),
        ),
        check_vma=False,
    )
```

```python
import functools
import math
import jax
import jax.numpy as jnp
import numpy as np
from jax import lax
from jax.experimental import pallas as pl
from jax.experimental.pallas import tpu as pltpu
from jax.sharding import PartitionSpec as P

D = 768
HD = 64
DS = 96
SH = 12
SHD = 8
SFF = 384
MAXD = 128
L = 128
ADAM_STEP = 10
PAIR = 2 * HD
SPAN = 2 * L

NORM_EPS = 1e-06
CLIP_NORM = 1.0
BETA_ONE = 0.9
BETA_TWO = 0.999
ADAM_EPS = 1e-08
RATE_MATRIX = 0.1
RATE_SMALL = 0.5
WEIGHT_DECAY = 0.01
MASKED = -1e30
PRECISE = lax.Precision.HIGHEST
MIB = 1 << 20
VMEM_MAIN = 60
GELU_RATE = math.sqrt(2.0 / math.pi)
GELU_CUBE = 0.044715

NN = (((1,), (0,)), ((), ()))
NT = (((1,), (1,)), ((), ()))
TN = (((0,), (0,)), ((), ()))


def mm(left, right, dims=NN):
    return lax.dot_general(left, right, dims, preferred_element_type=jnp.float32)


def bucket_of(offset, buckets, reach):
    half_count = buckets // 2
    exact_count = half_count // 2
    distance = np.abs(offset)
    spread_part = (
        np.log(np.maximum(distance, 1) / exact_count)
        / np.log(reach / exact_count)
        * (half_count - exact_count)
    )
    far_bucket = np.minimum(exact_count + np.floor(spread_part).astype(np.int32), half_count - 1)
    near_side = np.where(distance < exact_count, distance, far_bucket)
    return (near_side + (offset > 0) * half_count).astype(np.int32)


def diagonal_onehot(buckets):
    column = np.arange(SPAN)
    offset = np.where(column < L, -column, SPAN - column)
    onehot = bucket_of(offset, buckets, MAXD)[None, :] == np.arange(buckets)[:, None]
    onehot = onehot & (column != L)[None, :]
    return onehot.astype(np.float32)


def gradient_onehot(buckets):
    column = np.arange(SPAN)
    onehot = bucket_of(L - 1 - column, buckets, MAXD)[None, :] == np.arange(buckets)[:, None]
    onehot = onehot & (column != SPAN - 1)[None, :]
    return onehot.astype(np.float32)


def rms_scale(values):
    return lax.rsqrt(jnp.mean(values * values, axis=-1, keepdims=True) + NORM_EPS)


def gelu(v):
    return 0.5 * v * (1.0 + jnp.tanh(GELU_RATE * (v + GELU_CUBE * (v * v * v))))


def diagonals_of(table_ref, onehot_ref):
    return lax.dot_general(
        table_ref[...],
        onehot_ref[...],
        NN,
        precision=PRECISE,
        preferred_element_type=jnp.float32,
    )


def spread_bias(row):
    full = jnp.broadcast_to(row, (L, SPAN))
    return pltpu.roll(full, 0, 1, stride=1, stride_axis=0)[:, :L]


def attention_setup(
    parity, group, own_ref, mate_ref, table_ref, onehot_ref, diag_scr, w_scr, bias_scr
):
    third = own_ref.shape[1]
    width = 2 * third
    heads = width // HD

    def place(low_ref, high_ref):
        for part in range(3):
            w_scr[part * width : part * width + third, :] = low_ref[part]
            w_scr[part * width + third : (part + 1) * width, :] = high_ref[part]

    @pl.when(parity == 0)
    def _():
        place(own_ref, mate_ref)

    @pl.when(parity == 1)
    def _():
        place(mate_ref, own_ref)

    diag_scr[...] = diagonals_of(table_ref, onehot_ref)
    for head in range(heads):
        bias_scr[head * L : (head + 1) * L, :] = spread_bias(
            diag_scr[pl.ds(group * heads + head, 1), :]
        )


def attention_block(lengths, rows, gain, w_scr, bias_scr, ctx_ref):
    width = w_scr.shape[0] // 3
    normed = (rows * rms_scale(rows) * gain).astype(jnp.bfloat16)
    turned = mm(w_scr[...], normed, NT).astype(jnp.bfloat16)
    query, key, value = turned[0:width], turned[width : 2 * width], turned[2 * width :]
    low_lane = lax.broadcasted_iota(jnp.int32, (L, PAIR), 1) < HD
    low_row = lax.broadcasted_iota(jnp.int32, (PAIR, L), 0) < HD
    key_row = lax.broadcasted_iota(jnp.int32, (2, L, L), 1)
    for s, length in enumerate(lengths):
        at = slice(s * L, (s + 1) * L)
        seen = key_row < length
        for p in range(width // PAIR):
            head = slice(p * PAIR, (p + 1) * PAIR)
            k_one, v_one = key[head, at].T, value[head, at]
            zero = jnp.zeros_like(k_one)
            k_two = jnp.concatenate(
                [jnp.where(low_lane, k_one, zero), jnp.where(low_lane, zero, k_one)], axis=0
            )
            v_two = jnp.concatenate(
                [jnp.where(low_row, v_one, zero), jnp.where(low_row, zero, v_one)], axis=1
            )
            scores = mm(k_two, query[head, at]) + bias_scr[p * 2 * L : (p + 1) * 2 * L, :]
            scores = jnp.where(seen, scores.reshape(2, L, L), MASKED)
            shifted = jnp.exp(scores - jnp.max(scores, axis=1, keepdims=True))
            scale = 1.0 / jnp.sum(shifted, axis=1, keepdims=True)
            scale = jnp.broadcast_to(scale, (2, HD, L)).reshape(PAIR, L)
            probs = shifted.astype(jnp.bfloat16).reshape(2 * L, L)
            ctx_ref[head, at] = (mm(v_two, probs) * scale).astype(jnp.bfloat16)


def near_kernel(
    seqs,
    meta_ref,
    len_ref,
    tok_ref,
    gain_ref,
    own_ref,
    mate_ref,
    table_ref,
    onehot_ref,
    ctx_ref,
    diag_scr,
    w_scr,
    bias_scr,
):
    step = pl.program_id(0)

    @pl.when(step == 0)
    def _():
        attention_setup(
            meta_ref[1],
            meta_ref[2],
            own_ref,
            mate_ref,
            table_ref,
            onehot_ref,
            diag_scr,
            w_scr,
            bias_scr,
        )

    lengths = [len_ref[meta_ref[0] + step * seqs + s] for s in range(seqs)]
    rows = tok_ref[...].reshape(seqs * L, D).astype(jnp.float32)
    attention_block(lengths, rows, gain_ref[0:1, :], w_scr, bias_scr, ctx_ref)


def near_part(meta, lengths, tokens, gains, own, mate, table, onehot, own_seqs, seqs):
    width = 2 * own.shape[1]
    fixed = lambda *dims: pl.BlockSpec(dims, lambda i, m, n: (0,) * len(dims))
    return pl.pallas_call(
        functools.partial(near_kernel, seqs),
        name="near",
        grid_spec=pltpu.PrefetchScalarGridSpec(
            num_scalar_prefetch=2,
            grid=(own_seqs // seqs,),
            in_specs=[
                pl.BlockSpec((seqs, L, D), lambda i, m, n: (m[0] // seqs + i, 0, 0)),
                fixed(2, D),
                fixed(*own.shape),
                fixed(*mate.shape),
                fixed(*table.shape),
                fixed(*onehot.shape),
            ],
            out_specs=pl.BlockSpec((width, seqs * L), lambda i, m, n: (0, i)),
            scratch_shapes=[
                pltpu.VMEM((table.shape[0], SPAN), jnp.float32),
                pltpu.VMEM((3 * width, D), jnp.bfloat16),
                pltpu.VMEM((width // HD * L, L), jnp.float32),
            ],
        ),
        out_shape=jax.ShapeDtypeStruct((width, own_seqs * L), jnp.bfloat16),
        compiler_params=pltpu.CompilerParams(
            dimension_semantics=("arbitrary",), vmem_limit_bytes=56 * MIB
        ),
        cost_estimate=pl.CostEstimate(
            flops=2 * own_seqs * L * width * (3 * D + 2 * L),
            bytes_accessed=own_seqs * L * (D + width) * 2 + 6 * D * width,
            transcendentals=own_seqs * width // HD * L * L,
        ),
    )(meta, lengths, tokens, gains, own, mate, table, onehot)


def feed_block(chunk, rows, near, far, gain, wo_scr, up_scr, down_scr, taps_scr):
    width = near.shape[0]
    size = rows.shape[0] // 2
    halves = [slice(0, size), slice(size, 2 * size)]
    middle = [
        rows[at]
        + mm(near[:, at], wo_scr[0:width, :], TN)
        + mm(far[:, at], wo_scr[width:, :], TN)
        for at in halves
    ]
    normed = [(part * rms_scale(part) * gain).astype(jnp.bfloat16) for part in middle]
    for at, part, unit in zip(halves, middle, normed):
        total = jnp.zeros_like(part)
        for c in range(0, up_scr.shape[1], chunk):
            hidden = gelu(mm(unit, up_scr[:, c : c + chunk])).astype(jnp.bfloat16)
            total = total + mm(hidden, down_scr[c : c + chunk, :])
        taps_scr[at, :] = (part + total).astype(jnp.bfloat16)


def pick_rows(step, phase, count):
    row = lax.broadcasted_iota(jnp.int32, (count, step * count), 0)
    column = lax.broadcasted_iota(jnp.int32, (count, step * count), 1)
    return (column == step * row + phase).astype(jnp.bfloat16)


def by_head_rows(block):
    head = lax.broadcasted_iota(jnp.int32, block.shape, 1) // SHD
    zero = jnp.zeros_like(block)
    return jnp.concatenate([jnp.where(head == h, block, zero) for h in range(SH)], axis=0)


def by_head_lanes(block):
    head = lax.broadcasted_iota(jnp.int32, block.shape, 0) // SHD
    zero = jnp.zeros_like(block)
    return jnp.concatenate([jnp.where(head == h, block, zero) for h in range(SH)], axis=1)


def lanes_of(stacked):
    return jnp.concatenate([stacked[h * L : (h + 1) * L] for h in range(SH)], axis=1)


def norm_back(unit, scale, gain, grad):
    scaled = grad * gain
    return scale * (scaled - unit * jnp.mean(scaled * unit, axis=0, keepdims=True))


def two_by_head(turned, first):
    blocks = [by_head_rows(turned[:, s * L : (s + 1) * L].T) for s in (first, first + 1)]
    return jnp.concatenate(blocks, axis=1)


def two_apart(turned, first):
    zero = jnp.zeros((L, L), turned.dtype)
    one, two = turned[:, first * L : (first + 1) * L], turned[:, (first + 1) * L : (first + 2) * L]
    return jnp.concatenate(
        [jnp.concatenate([one, zero], axis=1), jnp.concatenate([zero, two], axis=1)], axis=0
    )


def column_scale(values):
    return lax.rsqrt(jnp.mean(values * values, axis=0, keepdims=True) + NORM_EPS)


def fold_lanes(values):
    total = values[:, 0:L]
    for s in range(1, values.shape[1] // L):
        total = total + values[:, s * L : (s + 1) * L]
    return total


AT_QKV, AT_OUT, AT_UP, AT_BACK, AT_END = D, D + 3 * DS, D + 4 * DS, D + 8 * DS, D + 8 * DS + SFF


def low(values):
    return values.astype(jnp.bfloat16)


def side_setup(gain_ref, w_ref, table_ref, onehot_ref, scratch):
    (
        gain_scr,
        wdown_scr,
        wqkv_scr,
        wqkv_turn_scr,
        wout_turn_scr,
        wup_scr,
        wup_turn_scr,
        wback_turn_scr,
        bias_scr,
        gbias_scr,
        elow_scr,
        gdown_scr,
        gqkv_scr,
        gproj_scr,
        gup_scr,
        gback_scr,
        ggain_scr,
    ) = scratch
    wdown_scr[...] = w_ref[0:D, :].T
    for t in range(3):
        part = mm(pick_rows(3, t, DS), w_ref[AT_QKV:AT_OUT, :])
        wqkv_scr[t] = low(part)
        wqkv_turn_scr[t * L : t * L + DS, :] = low(part.T)
        wqkv_turn_scr[t * L + DS : (t + 1) * L, :] = jnp.zeros((L - DS, DS), jnp.bfloat16)
    wout_turn_scr[...] = w_ref[AT_OUT:AT_UP, :].T
    for t in range(4):
        part = mm(pick_rows(4, t, DS), w_ref[AT_UP:AT_BACK, :])
        wup_scr[:, t * DS : (t + 1) * DS] = low(part)
        wup_turn_scr[t * DS : (t + 1) * DS, :] = low(part.T)
    wback_turn_scr[...] = w_ref[AT_BACK : AT_END, :].T
    for row in range(3):
        wide = jnp.broadcast_to(gain_ref[row : row + 1, :], (L, DS)).T
        gain_scr[row] = jax.nn.sigmoid(wide) if row == 2 else wide
    diagonals = diagonals_of(table_ref, onehot_ref)
    for head in range(SH):
        bias_scr[head * L : (head + 1) * L, :] = spread_bias(diagonals[head : head + 1, :])
    for ref in (gbias_scr, gdown_scr, gqkv_scr, gproj_scr, gup_scr, gback_scr, ggain_scr):
        ref[...] = jnp.zeros_like(ref)


def side_block(lengths, taps_scr, x_ref, go_ref, w_ref, out_ref, ig_ref, scratch):
    (
        gain_scr,
        wdown_scr,
        wqkv_scr,
        wqkv_turn_scr,
        wout_turn_scr,
        wup_scr,
        wup_turn_scr,
        wback_turn_scr,
        bias_scr,
        gbias_scr,
        elow_scr,
        gdown_scr,
        gqkv_scr,
        gproj_scr,
        gup_scr,
        gback_scr,
        ggain_scr,
    ) = scratch
    seqs = len(lengths)
    wide = lambda row: jnp.concatenate([gain_scr[row]] * seqs, axis=1)
    gain_one, gain_two, gate = wide(0), wide(1), wide(2)
    w_out = w_ref[AT_OUT:AT_UP, :]
    w_back = w_ref[AT_BACK : AT_END, :]
    key_row = lax.broadcasted_iota(jnp.int32, (SH, L, L), 1)
    token = lax.broadcasted_iota(jnp.int32, (DS, L), 1)
    taps = taps_scr[...]
    x = jnp.concatenate([x_ref[s] for s in range(seqs)], axis=1)
    grad_out = jnp.concatenate(
        [jnp.where(token < lengths[s], go_ref[s], 0.0) for s in range(seqs)], axis=1
    )

    tapped = mm(wdown_scr[...], taps, NT)
    mixed = gate * x + (1.0 - gate) * tapped
    scale_one = column_scale(mixed)
    unit_one = mixed * scale_one
    normed_one = low(unit_one * gain_one)
    qkv = low(mm(wqkv_turn_scr[...], normed_one))

    query, key, value = qkv[0:L], qkv[L : 2 * L], qkv[2 * L :]
    context, inverse = [], []
    for s in range(0, seqs, 2):
        score_two = mm(two_by_head(key, s), two_apart(query, s))
        for side in range(2):
            at = slice((s + side) * L, (s + side + 1) * L)
            scores = score_two[:, side * L : (side + 1) * L] + bias_scr[...]
            scores = jnp.where(key_row < lengths[s + side], scores.reshape(SH, L, L), MASKED)
            shifted = jnp.exp(scores - jnp.max(scores, axis=1, keepdims=True))
            e_low = low(shifted).reshape(SH * L, L)
            elow_scr[s + side] = e_low
            total = 1.0 / jnp.sum(shifted, axis=1, keepdims=True)
            inverse.append(jnp.broadcast_to(total, (SH, SHD, L)).reshape(DS, L))
            context.append(mm(by_head_lanes(value[0:DS, at]), e_low) * inverse[-1])
    context = jnp.concatenate(context, axis=1)
    inverse = jnp.concatenate(inverse, axis=1)
    context_low = low(context)

    middle = mixed + mm(wout_turn_scr[...], context_low)
    scale_two = column_scale(middle)
    unit_two = middle * scale_two
    normed_two = low(unit_two * gain_two)
    pre = mm(wup_turn_scr[...], normed_two)
    square = pre * pre
    bend = jnp.tanh(GELU_RATE * pre * (1.0 + GELU_CUBE * square))
    half = 0.5 * (1.0 + bend)
    hidden = low(pre * half)
    slope = half + (0.5 * GELU_RATE) * pre * (1.0 - bend * bend) * (1.0 + 3.0 * GELU_CUBE * square)
    side_out = middle + mm(wback_turn_scr[...], hidden)

    grad_low = low(grad_out)
    gback_scr[...] += mm(hidden, grad_low, NT)
    grad_pre = low(mm(w_back, grad_low) * slope)
    gup_scr[...] += mm(normed_two, grad_pre, NT)
    grad_normed_two = mm(wup_scr[...], grad_pre)
    ggain_scr[1] += fold_lanes(grad_normed_two * unit_two)
    grad_middle = grad_out + norm_back(unit_two, scale_two, gain_two, grad_normed_two)
    grad_attended = low(grad_middle)
    gproj_scr[...] += mm(context_low, grad_attended, NT)
    grad_context = low(mm(w_out, grad_attended) * inverse)
    pad = jnp.zeros((L - DS, seqs * L), jnp.bfloat16)
    dots = (grad_context.astype(jnp.float32) * context).reshape(SH, SHD, seqs * L)
    dots = jnp.sum(dots, axis=1, keepdims=True)

    grad_context = jnp.concatenate([grad_context, pad], axis=0)
    grad_query, grad_key, grad_value = [], [], []
    for s in range(0, seqs, 2):
        prob_two = mm(two_by_head(value, s), two_apart(grad_context, s))
        for side in range(2):
            at = slice((s + side) * L, (s + side + 1) * L)
            grad_probs = prob_two[:, side * L : (side + 1) * L].reshape(SH, L, L)
            grad_scores = elow_scr[s + side].astype(jnp.float32).reshape(SH, L, L) * (
                grad_probs - dots[:, :, at]
            )
            gbias_scr[...] += grad_scores.reshape(SH * L, L)
            grad_scores = low(grad_scores).reshape(SH * L, L)
            grad_query.append(low(mm(by_head_lanes(key[0:DS, at]), grad_scores)))
            grad_key.append(low(mm(lanes_of(grad_scores), by_head_rows(query[0:DS, at].T))))
            grad_value.append(
                low(mm(lanes_of(elow_scr[s + side]), by_head_rows(grad_context[0:DS, at].T)))
            )
    grad_query = jnp.concatenate(grad_query, axis=1)
    grad_key = jnp.concatenate(grad_key, axis=0)
    grad_value = jnp.concatenate(grad_value, axis=0)

    grad_normed = mm(wqkv_scr[0], grad_query)
    grad_normed += mm(wqkv_scr[1], grad_key, NT)
    grad_normed += mm(wqkv_scr[2], grad_value, NT)
    gqkv_scr[0] += mm(normed_one, grad_query, NT)
    gqkv_scr[1] += mm(normed_one, grad_key)
    gqkv_scr[2] += mm(normed_one, grad_value)
    ggain_scr[0] += fold_lanes(grad_normed * unit_one)
    grad_mixed = grad_middle + norm_back(unit_one, scale_one, gain_one, grad_normed)
    input_grad = gate * grad_mixed
    grad_tap = low((1.0 - gate) * grad_mixed)
    gdown_scr[...] += mm(grad_tap, taps)
    ggain_scr[2] += fold_lanes(grad_mixed * (x - tapped))
    for s in range(seqs):
        out_ref[s] = side_out[:, s * L : (s + 1) * L]
        ig_ref[s] = input_grad[:, s * L : (s + 1) * L]


def side_finish(onehot_ref, send_ref, grow_scr, scratch):
    (
        gain_scr,
        wdown_scr,
        wqkv_scr,
        wqkv_turn_scr,
        wout_turn_scr,
        wup_scr,
        wup_turn_scr,
        wback_turn_scr,
        bias_scr,
        gbias_scr,
        elow_scr,
        gdown_scr,
        gqkv_scr,
        gproj_scr,
        gup_scr,
        gback_scr,
        ggain_scr,
    ) = scratch
    grow_scr[:, DS:] = jnp.zeros((grow_scr.shape[0], grow_scr.shape[1] - DS), jnp.bfloat16)
    grow_scr[0:D, 0:DS] = low(gdown_scr[...].T)
    spread = mm(pick_rows(3, 0, DS), low(gqkv_scr[0]), TN)
    for t in range(1, 3):
        spread = spread + mm(pick_rows(3, t, DS), low(gqkv_scr[t]), TN)
    grow_scr[AT_QKV:AT_OUT, 0:DS] = low(spread)
    grow_scr[AT_OUT:AT_UP, 0:DS] = low(gproj_scr[...])
    spread = mm(pick_rows(4, 0, DS), low(gup_scr[:, 0:DS]), TN)
    for t in range(1, 4):
        spread = spread + mm(pick_rows(4, t, DS), low(gup_scr[:, t * DS : (t + 1) * DS]), TN)
    grow_scr[AT_UP:AT_BACK, 0:DS] = low(spread)
    grow_scr[AT_BACK : AT_END, 0:DS] = low(gback_scr[...])
    flip_row = lax.broadcasted_iota(jnp.int32, (L, L), 0)
    flip_column = lax.broadcasted_iota(jnp.int32, (L, L), 1)
    flip = (flip_row + flip_column == L - 1).astype(jnp.float32)
    diagonals = []
    for head in range(SH):
        square = lax.dot_general(
            flip,
            gbias_scr[head * L : (head + 1) * L, :],
            NN,
            precision=PRECISE,
            preferred_element_type=jnp.float32,
        )
        full = jnp.concatenate([square, jnp.zeros_like(square)], axis=1)
        rolled = pltpu.roll(full, 0, 1, stride=1, stride_axis=0)
        diagonals.append(jnp.sum(rolled, axis=0, keepdims=True))
    diagonals = jnp.concatenate(diagonals, axis=0)
    shard_rows = AT_END // send_ref.shape[0]
    small = shard_rows + SH
    for device in range(send_ref.shape[0]):
        send_ref[device, 0:shard_rows, :] = grow_scr[
            device * shard_rows : (device + 1) * shard_rows, :
        ]
    gains = []
    for row in range(3):
        total = ggain_scr[row]
        if row == 2:
            total = total * (gain_scr[2] * (1.0 - gain_scr[2]))
        gains.append(jnp.sum(total.T, axis=0, keepdims=True))
    gains.append(jnp.zeros((SH - 3, DS), jnp.float32))
    table = lax.dot_general(
        diagonals, onehot_ref[...], NT, precision=PRECISE, preferred_element_type=jnp.float32
    )
    extra = low(jnp.concatenate([jnp.concatenate(gains, axis=0), table], axis=1))
    blank = jnp.zeros((send_ref.shape[1] - small, L), jnp.bfloat16)
    for device in range(send_ref.shape[0]):
        send_ref[device, shard_rows:small, :] = extra
        if small < send_ref.shape[1]:
            send_ref[device, small:, :] = blank


def main_kernel(
    seqs,
    chunk,
    meta_ref,
    len_ref,
    tok_ref,
    gain_ref,
    far_ref,
    mate_ref,
    table_ref,
    near_ref,
    x_ref,
    go_ref,
    side_gain_ref,
    side_table_ref,
    onehot_ref,
    turn_onehot_ref,
    wo_hbm,
    up_hbm,
    down_hbm,
    w_hbm,
    out_ref,
    ig_ref,
    send_ref,
    diag_scr,
    w_scr,
    bias_scr,
    ctx_scr,
    taps_scr,
    wo_scr,
    up_scr,
    down_scr,
    wrow_scr,
    grow_scr,
    sems,
    *scratch,
):
    step = pl.program_id(0)
    group = meta_ref[2]
    width = near_ref.shape[0]
    copies = [
        pltpu.make_async_copy(
            wo_hbm.at[pl.ds(group * width, width), :], wo_scr.at[pl.ds(0, width), :], sems.at[0]
        ),
        pltpu.make_async_copy(
            wo_hbm.at[pl.ds((1 - group) * width, width), :],
            wo_scr.at[pl.ds(width, width), :],
            sems.at[1],
        ),
        pltpu.make_async_copy(up_hbm, up_scr, sems.at[2]),
        pltpu.make_async_copy(down_hbm, down_scr, sems.at[3]),
        pltpu.make_async_copy(w_hbm, wrow_scr, sems.at[4]),
    ]

    @pl.when(step == 0)
    def _():
        for copy in copies:
            copy.start()
        attention_setup(
            meta_ref[1],
            1 - group,
            far_ref,
            mate_ref,
            table_ref,
            onehot_ref,
            diag_scr,
            w_scr,
            bias_scr,
        )

    lengths = [len_ref[meta_ref[0] + step * seqs + s] for s in range(seqs)]
    rows = tok_ref[...].reshape(seqs * L, D).astype(jnp.float32)
    attention_block(lengths, rows, gain_ref[0:1, :], w_scr, bias_scr, ctx_scr)

    @pl.when(step == 0)
    def _():
        for copy in copies:
            copy.wait()
        side_setup(side_gain_ref, wrow_scr, side_table_ref, onehot_ref, scratch)

    rows = tok_ref[...].reshape(seqs * L, D).astype(jnp.float32)
    feed_block(
        chunk, rows, near_ref[...], ctx_scr[...], gain_ref[1:2, :], wo_scr, up_scr, down_scr, taps_scr
    )
    side_block(lengths, taps_scr, x_ref, go_ref, wrow_scr, out_ref, ig_ref, scratch)

    @pl.when(step == pl.num_programs(0) - 1)
    def _():
        side_finish(turn_onehot_ref, send_ref, grow_scr, scratch)


def main_part(
    meta,
    lengths,
    tokens,
    gains,
    far,
    mate,
    table,
    ctx_near,
    side_input,
    output_grad,
    side_gains,
    side_table,
    onehot,
    turn_onehot,
    w_out,
    w_up,
    w_down,
    w_rows,
    devices,
    seqs,
    chunk,
):
    own_seqs = side_input.shape[0]
    width = ctx_near.shape[0]
    ff = w_up.shape[1]
    send_rows = -(-(w_rows.shape[0] // devices + SH) // 8) * 8
    fixed = lambda *dims: pl.BlockSpec(dims, lambda i, m, n: (0,) * len(dims))
    block = pl.BlockSpec((seqs, DS, L), lambda i, m, n: (i, 0, 0))
    hbm = pl.BlockSpec(memory_space=pl.ANY)
    f32, bf16 = jnp.float32, jnp.bfloat16
    return pl.pallas_call(
        functools.partial(main_kernel, seqs, chunk),
        name="main",
        grid_spec=pltpu.PrefetchScalarGridSpec(
            num_scalar_prefetch=2,
            grid=(own_seqs // seqs,),
            in_specs=[
                pl.BlockSpec((seqs, L, D), lambda i, m, n: (m[0] // seqs + i, 0, 0)),
                fixed(2, D),
                fixed(*far.shape),
                fixed(*mate.shape),
                fixed(*table.shape),
                pl.BlockSpec((width, seqs * L), lambda i, m, n: (0, i)),
                block,
                block,
                fixed(*side_gains.shape),
                fixed(*side_table.shape),
                fixed(*onehot.shape),
                fixed(*turn_onehot.shape),
                hbm,
                hbm,
                hbm,
                hbm,
            ],
            out_specs=[block, block, fixed(devices, send_rows, L)],
            scratch_shapes=[
                pltpu.VMEM((table.shape[0], SPAN), f32),
                pltpu.VMEM((3 * width, D), bf16),
                pltpu.VMEM((width // HD * L, L), f32),
                pltpu.VMEM((width, seqs * L), bf16),
                pltpu.VMEM((seqs * L, D), bf16),
                pltpu.VMEM(w_out.shape, bf16),
                pltpu.VMEM(w_up.shape, bf16),
                pltpu.VMEM(w_down.shape, bf16),
                pltpu.VMEM(w_rows.shape, bf16),
                pltpu.VMEM((w_rows.shape[0], L), bf16),
                pltpu.SemaphoreType.DMA((5,)),
                pltpu.VMEM((3, DS, L), f32),
                pltpu.VMEM((DS, D), bf16),
                pltpu.VMEM((3, DS, DS), bf16),
                pltpu.VMEM((3 * L, DS), bf16),
                pltpu.VMEM((DS, DS), bf16),
                pltpu.VMEM((DS, SFF), bf16),
                pltpu.VMEM((SFF, DS), bf16),
                pltpu.VMEM((DS, SFF), bf16),
                pltpu.VMEM((SH * L, L), f32),
                pltpu.VMEM((SH * L, L), f32),
                pltpu.VMEM((seqs, SH * L, L), bf16),
                pltpu.VMEM((DS, D), f32),
                pltpu.VMEM((3, DS, DS), f32),
                pltpu.VMEM((DS, DS), f32),
                pltpu.VMEM((DS, SFF), f32),
                pltpu.VMEM((SFF, DS), f32),
                pltpu.VMEM((3, DS, L), f32),
            ],
        ),
        out_shape=[
            jax.ShapeDtypeStruct(side_input.shape, f32),
            jax.ShapeDtypeStruct(side_input.shape, f32),
            jax.ShapeDtypeStruct((devices, send_rows, L), bf16),
        ],
        compiler_params=pltpu.CompilerParams(
            dimension_semantics=("arbitrary",), vmem_limit_bytes=VMEM_MAIN * MIB
        ),
        cost_estimate=pl.CostEstimate(
            flops=2 * own_seqs * L * (D * (D + 2 * ff) + width * (3 * D + 2 * L))
            + own_seqs * 300_000_000,
            bytes_accessed=own_seqs * L * (3 * D + 16 * DS) + 2 * D * (D + 2 * ff),
            transcendentals=own_seqs * L * (ff + 2 * SH * L + SFF),
        ),
    )(
        meta,
        lengths,
        tokens,
        gains,
        far,
        mate,
        table,
        ctx_near,
        side_input,
        output_grad,
        side_gains,
        side_table,
        onehot,
        turn_onehot,
        w_out,
        w_up,
        w_down,
        w_rows,
    )


def adamw_update(weight_now, first_now, second_now, gradient, rate, decay_rate):
    first_new = BETA_ONE * first_now + (1.0 - BETA_ONE) * gradient
    second_new = BETA_TWO * second_now + (1.0 - BETA_TWO) * gradient * gradient
    first_hat = first_new / (1.0 - BETA_ONE**ADAM_STEP)
    second_hat = second_new / (1.0 - BETA_TWO**ADAM_STEP)
    weight_new = weight_now - rate * (
        first_hat / (jnp.sqrt(second_hat) + ADAM_EPS) + decay_rate * weight_now
    )
    return (first_new, second_new, weight_new)


def collect_kernel(shard_rows, got_ref, shard_ref, small_ref, square_ref):
    total = got_ref[0].astype(jnp.float32)
    for device in range(1, got_ref.shape[0]):
        total = total + got_ref[device].astype(jnp.float32)
    shard = total[0:shard_rows, 0:DS]
    shard_ref[...] = shard
    small_ref[...] = total[shard_rows : shard_rows + SH, :]
    square = jnp.sum(jnp.sum(shard * shard, axis=1, keepdims=True), axis=0, keepdims=True)
    square_ref[...] = jnp.broadcast_to(square, square_ref.shape)


def collect_part(got, shard_rows):
    devices = got.shape[0]
    return pl.pallas_call(
        functools.partial(collect_kernel, shard_rows),
        name="collect",
        out_shape=[
            jax.ShapeDtypeStruct((shard_rows, DS), jnp.float32),
            jax.ShapeDtypeStruct((SH, L), jnp.float32),
            jax.ShapeDtypeStruct((devices, L), jnp.float32),
        ],
        in_specs=[pl.BlockSpec(memory_space=pltpu.VMEM)],
        out_specs=[pl.BlockSpec(memory_space=pltpu.VMEM)] * 3,
    )(got)


def update_kernel(square_ref, small_ref, shard_ref, *refs):
    weights, gains, table = refs[0:3], refs[3:6], refs[6:9]
    norm_ref, copy_ref = refs[9], refs[13]
    gains_total = small_ref[0:3, 0:DS]
    table_total = small_ref[:, DS:]
    whole = lambda values: jnp.sum(
        jnp.sum(values, axis=1, keepdims=True), axis=0, keepdims=True
    )
    norm = jnp.sqrt(
        jnp.sum(square_ref[:, 0:1], axis=0, keepdims=True)
        + whole(gains_total * gains_total)
        + whole(table_total * table_total)
    )
    norm_ref[...] = norm
    factor = CLIP_NORM / jnp.maximum(norm, CLIP_NORM)

    def update(state, gradient, outs, rate, decay):
        results = adamw_update(*[ref[...] for ref in state], factor * gradient, rate, decay)
        for ref, value in zip(outs, results):
            ref[...] = value
        return results[2]

    new = update(weights, shard_ref[...], refs[10:13], RATE_MATRIX, WEIGHT_DECAY)
    copy_ref[...] = new.astype(jnp.bfloat16)
    update(gains, gains_total, refs[14:17], RATE_SMALL, 0.0)
    update(table, table_total, refs[17:20], RATE_SMALL, 0.0)


def update_part(squares, small, shard, weights, gains, table):
    f32 = jnp.float32
    like = lambda values, dtype=f32: jax.ShapeDtypeStruct(values.shape, dtype)
    operands = (squares, small, shard, *weights, *gains, *table)
    return pl.pallas_call(
        update_kernel,
        name="update",
        out_shape=[
            jax.ShapeDtypeStruct((1, 1), f32),
            *[like(values) for values in weights],
            like(shard, jnp.bfloat16),
            *[like(values) for values in gains],
            *[like(values) for values in table],
        ],
        in_specs=[pl.BlockSpec(memory_space=pltpu.VMEM)] * len(operands),
        out_specs=[pl.BlockSpec(memory_space=pltpu.VMEM)] * 11,
    )(*operands)


def swap(values, distance):
    size = lax.axis_size("mp")
    return lax.ppermute(values, "mp", [(i, i ^ distance) for i in range(size)])


def exchange(values):
    return lax.all_to_all(values, ("batch", "mp"), split_axis=0, concat_axis=0, tiled=True)


def on_device(
    tokens,
    lengths,
    base_gains,
    base_qkv,
    base_out,
    base_up,
    base_down,
    base_table,
    side_input,
    output_grad,
    side_weights,
    weights_first,
    weights_second,
    side_gains,
    gains_first,
    gains_second,
    side_table,
    table_first,
    table_second,
):
    devices = lax.axis_size(("batch", "mp"))
    model_index = lax.axis_index("mp")
    own_seqs = side_input.shape[0]
    shard_rows = side_weights.shape[0] // DS
    buckets = side_table.shape[0]
    meta = jnp.stack([model_index * own_seqs, model_index % 2, model_index // 2]).astype(jnp.int32)

    turn = lambda values: jnp.transpose(values, (0, 2, 1))
    qkv_own = turn(base_qkv)
    qkv_far = swap(qkv_own, 2)
    lanes = L if side_weights.shape[0] % L == 0 else DS
    flat = lambda values: values.reshape(-1, lanes)
    low_rows = flat(side_weights.astype(jnp.bfloat16))
    low_rows = jnp.broadcast_to(low_rows[None], (devices,) + low_rows.shape)
    w_rows = exchange(low_rows)
    qkv_mate = swap(qkv_own, 1)

    onehot = jnp.asarray(diagonal_onehot(buckets))
    ctx_near = near_part(
        meta, lengths, tokens, base_gains, qkv_own, qkv_mate, base_table.T, onehot, own_seqs, 8
    )
    ctx_near, qkv_far, w_rows = lax.optimization_barrier((ctx_near, qkv_far, w_rows))
    qkv_far_mate = swap(qkv_far, 1)
    side_output, input_grad, outgoing = main_part(
        meta,
        lengths,
        tokens,
        base_gains,
        qkv_far,
        qkv_far_mate,
        base_table.T,
        ctx_near,
        turn(side_input),
        turn(output_grad),
        side_gains,
        side_table.T,
        onehot,
        jnp.asarray(gradient_onehot(buckets)),
        base_out,
        base_up,
        base_down,
        w_rows.reshape(devices * shard_rows, DS),
        devices,
        8,
        1024,
    )

    grad_shard, small, squares = collect_part(exchange(outgoing), shard_rows)
    (
        grad_norm,
        weights_moment,
        weights_square,
        weights_new,
        weights_copy,
        gains_moment,
        gains_square,
        gains_new,
        table_moment,
        table_square,
        table_new,
    ) = update_part(
        exchange(squares),
        small,
        flat(grad_shard),
        [flat(side_weights), flat(weights_first), flat(weights_second)],
        [side_gains, gains_first, gains_second],
        [side_table.T, table_first.T, table_second.T],
    )
    return (
        turn(side_output),
        turn(input_grad),
        grad_norm.reshape(()),
        weights_moment.reshape(-1),
        weights_square.reshape(-1),
        weights_new.reshape(-1),
        weights_copy.reshape(-1),
        gains_moment,
        gains_square,
        gains_new,
        table_moment.T,
        table_square.T,
        table_new.T,
    )


def solution(mesh):
    return jax.shard_map(
        on_device,
        mesh=mesh,
        in_specs=(
            P("batch", None, None),
            P("batch"),
            P(),
            P(None, None, "mp"),
            P(),
            P(),
            P(),
            P(),
            P(("batch", "mp"), None, None),
            P(("batch", "mp"), None, None),
            P(("batch", "mp")),
            P(("batch", "mp")),
            P(("batch", "mp")),
            P(),
            P(),
            P(),
            P(),
            P(),
            P(),
        ),
        out_specs=(
            P(("batch", "mp"), None, None),
            P(("batch", "mp"), None, None),
            P(),
            P(("batch", "mp")),
            P(("batch", "mp")),
            P(("batch", "mp")),
            P(("batch", "mp")),
            P(),
            P(),
            P(),
            P(),
            P(),
            P(),
        ),
        check_vma=False,
    )
```

```python
import functools
import math
import jax
import jax.numpy as jnp
import numpy as np
from jax import lax
from jax.experimental import pallas as pl
from jax.experimental.pallas import tpu as pltpu
from jax.sharding import PartitionSpec as P

D = 768
HD = 64
DS = 96
SH = 12
SHD = 8
SFF = 384
MAXD = 128
L = 128
ADAM_STEP = 10
PAIR = 2 * HD
SPAN = 2 * L
NARROW = L - DS
SMALL_ROWS = SH + 9

NORM_EPS = 1e-06
CLIP_NORM = 1.0
BETA_ONE = 0.9
BETA_TWO = 0.999
ADAM_EPS = 1e-08
RATE_MATRIX = 0.1
RATE_SMALL = 0.5
WEIGHT_DECAY = 0.01
MASKED = -1e30
PRECISE = lax.Precision.HIGHEST
MIB = 1 << 20
VMEM_MAIN = 60
GELU_RATE = math.sqrt(2.0 / math.pi)
GELU_CUBE = 0.044715

NN = (((1,), (0,)), ((), ()))
NT = (((1,), (1,)), ((), ()))
TN = (((0,), (0,)), ((), ()))


def mm(left, right, dims=NN):
    return lax.dot_general(left, right, dims, preferred_element_type=jnp.float32)


def bucket_of(offset, buckets, reach):
    half_count = buckets // 2
    exact_count = half_count // 2
    distance = np.abs(offset)
    spread_part = (
        np.log(np.maximum(distance, 1) / exact_count)
        / np.log(reach / exact_count)
        * (half_count - exact_count)
    )
    far_bucket = np.minimum(exact_count + np.floor(spread_part).astype(np.int32), half_count - 1)
    near_side = np.where(distance < exact_count, distance, far_bucket)
    return (near_side + (offset > 0) * half_count).astype(np.int32)


def diagonal_onehot(buckets):
    column = np.arange(SPAN)
    offset = np.where(column < L, -column, SPAN - column)
    onehot = bucket_of(offset, buckets, MAXD)[None, :] == np.arange(buckets)[:, None]
    onehot = onehot & (column != L)[None, :]
    return onehot.astype(np.float32)


def gradient_onehot(buckets):
    column = np.arange(SPAN)
    onehot = bucket_of(L - 1 - column, buckets, MAXD)[None, :] == np.arange(buckets)[:, None]
    onehot = onehot & (column != SPAN - 1)[None, :]
    return onehot.astype(np.float32)


def rms_scale(values):
    return lax.rsqrt(jnp.mean(values * values, axis=-1, keepdims=True) + NORM_EPS)


def gelu(v):
    return 0.5 * v * (1.0 + jnp.tanh(GELU_RATE * (v + GELU_CUBE * (v * v * v))))


def diagonals_of(table_ref, onehot_ref):
    return lax.dot_general(
        table_ref[...],
        onehot_ref[...],
        NN,
        precision=PRECISE,
        preferred_element_type=jnp.float32,
    )


def spread_bias(row):
    full = jnp.broadcast_to(row, (L, SPAN))
    return pltpu.roll(full, 0, 1, stride=1, stride_axis=0)[:, :L]


def attention_setup(
    parity, group, own_ref, mate_ref, table_ref, onehot_ref, diag_scr, w_scr, bias_scr
):
    third = own_ref.shape[1]
    width = 2 * third
    heads = width // HD

    def place(low_ref, high_ref):
        for part in range(3):
            w_scr[part * width : part * width + third, :] = low_ref[part]
            w_scr[part * width + third : (part + 1) * width, :] = high_ref[part]

    @pl.when(parity == 0)
    def _():
        place(own_ref, mate_ref)

    @pl.when(parity == 1)
    def _():
        place(mate_ref, own_ref)

    diag_scr[...] = diagonals_of(table_ref, onehot_ref)
    for head in range(heads):
        bias_scr[head * L : (head + 1) * L, :] = spread_bias(
            diag_scr[pl.ds(group * heads + head, 1), :]
        )


def together(*steps):
    waiting = list(steps)
    while waiting:
        for stage in list(waiting):
            if next(stage, StopIteration) is StopIteration:
                waiting.remove(stage)


def attention_steps(lengths, rows, gain, w_scr, bias_scr, ctx_ref, base):
    width = w_scr.shape[0] // 3
    normed = (rows * rms_scale(rows) * gain).astype(jnp.bfloat16)
    turned = mm(w_scr[...], normed, NT).astype(jnp.bfloat16)
    query, key, value = turned[0:width], turned[width : 2 * width], turned[2 * width :]
    yield
    low_lane = lax.broadcasted_iota(jnp.int32, (L, PAIR), 1) < HD
    low_row = lax.broadcasted_iota(jnp.int32, (PAIR, L), 0) < HD
    key_row = lax.broadcasted_iota(jnp.int32, (2, L, L), 1)
    for s, length in enumerate(lengths):
        at = slice(s * L, (s + 1) * L)
        seen = key_row < length
        for p in range(width // PAIR):
            head = slice(p * PAIR, (p + 1) * PAIR)
            k_one, v_one = key[head, at].T, value[head, at]
            zero = jnp.zeros_like(k_one)
            k_two = jnp.concatenate(
                [jnp.where(low_lane, k_one, zero), jnp.where(low_lane, zero, k_one)], axis=0
            )
            v_two = jnp.concatenate(
                [jnp.where(low_row, v_one, zero), jnp.where(low_row, zero, v_one)], axis=1
            )
            scores = mm(k_two, query[head, at]) + bias_scr[p * 2 * L : (p + 1) * 2 * L, :]
            scores = jnp.where(seen, scores.reshape(2, L, L), MASKED)
            shifted = jnp.exp(scores - jnp.max(scores, axis=1, keepdims=True))
            scale = 1.0 / jnp.sum(shifted, axis=1, keepdims=True)
            scale = jnp.broadcast_to(scale, (2, HD, L)).reshape(PAIR, L)
            probs = shifted.astype(jnp.bfloat16).reshape(2 * L, L)
            into = slice(base + s * L, base + (s + 1) * L)
            ctx_ref[head, into] = (mm(v_two, probs) * scale).astype(jnp.bfloat16)
        yield


def near_kernel(
    seqs,
    meta_ref,
    len_ref,
    tok_ref,
    gain_ref,
    own_ref,
    mate_ref,
    table_ref,
    onehot_ref,
    ctx_ref,
    diag_scr,
    w_scr,
    bias_scr,
):
    step = pl.program_id(0)

    @pl.when(step == 0)
    def _():
        attention_setup(
            meta_ref[1],
            meta_ref[2],
            own_ref,
            mate_ref,
            table_ref,
            onehot_ref,
            diag_scr,
            w_scr,
            bias_scr,
        )

    lengths = [len_ref[meta_ref[0] + step * seqs + s] for s in range(seqs)]
    rows = tok_ref[...].reshape(seqs * L, D).astype(jnp.float32)
    together(attention_steps(lengths, rows, gain_ref[0:1, :], w_scr, bias_scr, ctx_ref, 0))


def near_part(meta, lengths, tokens, gains, own, mate, table, onehot, own_seqs, seqs):
    width = 2 * own.shape[1]
    fixed = lambda *dims: pl.BlockSpec(dims, lambda i, m, n: (0,) * len(dims))
    return pl.pallas_call(
        functools.partial(near_kernel, seqs),
        name="near",
        grid_spec=pltpu.PrefetchScalarGridSpec(
            num_scalar_prefetch=2,
            grid=(own_seqs // seqs,),
            in_specs=[
                pl.BlockSpec((seqs, L, D), lambda i, m, n: (m[0] // seqs + i, 0, 0)),
                fixed(2, D),
                fixed(*own.shape),
                fixed(*mate.shape),
                fixed(*table.shape),
                fixed(*onehot.shape),
            ],
            out_specs=pl.BlockSpec((width, seqs * L), lambda i, m, n: (0, i)),
            scratch_shapes=[
                pltpu.VMEM((table.shape[0], SPAN), jnp.float32),
                pltpu.VMEM((3 * width, D), jnp.bfloat16),
                pltpu.VMEM((width // HD * L, L), jnp.float32),
            ],
        ),
        out_shape=jax.ShapeDtypeStruct((width, own_seqs * L), jnp.bfloat16),
        compiler_params=pltpu.CompilerParams(
            dimension_semantics=("arbitrary",), vmem_limit_bytes=56 * MIB
        ),
        cost_estimate=pl.CostEstimate(
            flops=2 * own_seqs * L * width * (3 * D + 2 * L),
            bytes_accessed=own_seqs * L * (D + width) * 2 + 6 * D * width,
            transcendentals=own_seqs * width // HD * L * L,
        ),
    )(meta, lengths, tokens, gains, own, mate, table, onehot)


def feed_steps(chunk, rows, near, far, gain, wo_scr, up_scr, down_scr, taps_scr, at):
    width = near.shape[0]
    middle = rows + mm(near, wo_scr[0:width, :], TN) + mm(far, wo_scr[width:, :], TN)
    normed = (middle * rms_scale(middle) * gain).astype(jnp.bfloat16)
    total = jnp.zeros_like(middle)
    yield
    for c in range(0, up_scr.shape[1], chunk):
        hidden = gelu(mm(normed, up_scr[:, c : c + chunk])).astype(jnp.bfloat16)
        yield
        total = total + mm(hidden, down_scr[c : c + chunk, :])
        yield
    taps_scr[at, :] = (middle + total).astype(jnp.bfloat16)


def pick_rows(step, phase, count):
    row = lax.broadcasted_iota(jnp.int32, (count, step * count), 0)
    column = lax.broadcasted_iota(jnp.int32, (count, step * count), 1)
    return (column == step * row + phase).astype(jnp.bfloat16)


def by_head_rows(block):
    head = lax.broadcasted_iota(jnp.int32, block.shape, 1) // SHD
    zero = jnp.zeros_like(block)
    return jnp.concatenate([jnp.where(head == h, block, zero) for h in range(SH)], axis=0)


def by_head_lanes(block):
    head = lax.broadcasted_iota(jnp.int32, block.shape, 0) // SHD
    zero = jnp.zeros_like(block)
    return jnp.concatenate([jnp.where(head == h, block, zero) for h in range(SH)], axis=1)


def lanes_of(stacked):
    return jnp.concatenate([stacked[h * L : (h + 1) * L] for h in range(SH)], axis=1)


def norm_back(unit, scale, gain, grad):
    scaled = grad * gain
    return scale * (scaled - unit * jnp.mean(scaled * unit, axis=0, keepdims=True))


def two_by_head(turned, first):
    blocks = [by_head_rows(turned[:, s * L : (s + 1) * L].T) for s in (first, first + 1)]
    return jnp.concatenate(blocks, axis=1)


def two_apart(turned, first):
    zero = jnp.zeros((L, L), turned.dtype)
    one, two = turned[:, first * L : (first + 1) * L], turned[:, (first + 1) * L : (first + 2) * L]
    return jnp.concatenate(
        [jnp.concatenate([one, zero], axis=1), jnp.concatenate([zero, two], axis=1)], axis=0
    )


def column_scale(values):
    return lax.rsqrt(jnp.mean(values * values, axis=0, keepdims=True) + NORM_EPS)


def fold_lanes(values):
    total = values[:, 0:L]
    for s in range(1, values.shape[1] // L):
        total = total + values[:, s * L : (s + 1) * L]
    return total


AT_QKV, AT_OUT, AT_UP, AT_BACK, AT_END = D, D + 3 * DS, D + 4 * DS, D + 8 * DS, D + 8 * DS + SFF


def low(values):
    return values.astype(jnp.bfloat16)


def side_setup(gain_ref, w_ref, table_ref, onehot_ref, scratch):
    (
        gain_scr,
        wdown_scr,
        wqkv_scr,
        wqkv_turn_scr,
        wout_turn_scr,
        wup_scr,
        wup_turn_scr,
        wback_turn_scr,
        bias_scr,
        gbias_scr,
        elow_scr,
        gdown_scr,
        gqkv_scr,
        gproj_scr,
        gup_scr,
        gback_scr,
        ggain_scr,
    ) = scratch
    wdown_scr[...] = w_ref[0:D, :].T
    for t in range(3):
        part = mm(pick_rows(3, t, DS), w_ref[AT_QKV:AT_OUT, :])
        wqkv_scr[t] = low(part)
        wqkv_turn_scr[t * L : t * L + DS, :] = low(part.T)
        wqkv_turn_scr[t * L + DS : (t + 1) * L, :] = jnp.zeros((L - DS, DS), jnp.bfloat16)
    wout_turn_scr[...] = w_ref[AT_OUT:AT_UP, :].T
    for t in range(4):
        part = mm(pick_rows(4, t, DS), w_ref[AT_UP:AT_BACK, :])
        wup_scr[:, t * DS : (t + 1) * DS] = low(part)
        wup_turn_scr[t * DS : (t + 1) * DS, :] = low(part.T)
    wback_turn_scr[...] = w_ref[AT_BACK : AT_END, :].T
    for row in range(3):
        wide = jnp.broadcast_to(gain_ref[row : row + 1, :], (L, DS)).T
        gain_scr[row] = jax.nn.sigmoid(wide) if row == 2 else wide
    diagonals = diagonals_of(table_ref, onehot_ref)
    for head in range(SH):
        bias_scr[head * L : (head + 1) * L, :] = spread_bias(diagonals[head : head + 1, :])
    for ref in (gbias_scr, gdown_scr, gqkv_scr, gproj_scr, gup_scr, gback_scr, ggain_scr):
        ref[...] = jnp.zeros_like(ref)


def side_steps(lengths, base, taps, x_ref, go_ref, w_ref, out_ref, ig_ref, scratch):
    (
        gain_scr,
        wdown_scr,
        wqkv_scr,
        wqkv_turn_scr,
        wout_turn_scr,
        wup_scr,
        wup_turn_scr,
        wback_turn_scr,
        bias_scr,
        gbias_scr,
        elow_scr,
        gdown_scr,
        gqkv_scr,
        gproj_scr,
        gup_scr,
        gback_scr,
        ggain_scr,
    ) = scratch
    seqs = len(lengths)
    wide = lambda row: jnp.concatenate([gain_scr[row]] * seqs, axis=1)
    gain_one, gain_two, gate = wide(0), wide(1), wide(2)
    w_out = w_ref[AT_OUT:AT_UP, :]
    w_back = w_ref[AT_BACK : AT_END, :]
    key_row = lax.broadcasted_iota(jnp.int32, (SH, L, L), 1)
    token = lax.broadcasted_iota(jnp.int32, (DS, L), 1)
    x = jnp.concatenate([x_ref[base + s] for s in range(seqs)], axis=1)
    grad_out = jnp.concatenate(
        [jnp.where(token < lengths[s], go_ref[base + s], 0.0) for s in range(seqs)], axis=1
    )

    tapped = mm(wdown_scr[...], taps, NT)
    mixed = gate * x + (1.0 - gate) * tapped
    scale_one = column_scale(mixed)
    unit_one = mixed * scale_one
    normed_one = low(unit_one * gain_one)
    qkv = low(mm(wqkv_turn_scr[...], normed_one))

    query, key, value = qkv[0:L], qkv[L : 2 * L], qkv[2 * L :]
    context, inverse = [], []
    yield
    for s in range(0, seqs, 2):
        score_two = mm(two_by_head(key, s), two_apart(query, s))
        for side in range(2):
            at = slice((s + side) * L, (s + side + 1) * L)
            scores = score_two[:, side * L : (side + 1) * L] + bias_scr[...]
            scores = jnp.where(key_row < lengths[s + side], scores.reshape(SH, L, L), MASKED)
            shifted = jnp.exp(scores - jnp.max(scores, axis=1, keepdims=True))
            e_low = low(shifted).reshape(SH * L, L)
            elow_scr[base + s + side] = e_low
            total = 1.0 / jnp.sum(shifted, axis=1, keepdims=True)
            inverse.append(jnp.broadcast_to(total, (SH, SHD, L)).reshape(DS, L))
            context.append(mm(by_head_lanes(value[0:DS, at]), e_low) * inverse[-1])
        yield
    context = jnp.concatenate(context, axis=1)
    inverse = jnp.concatenate(inverse, axis=1)
    context_low = low(context)

    middle = mixed + mm(wout_turn_scr[...], context_low)
    scale_two = column_scale(middle)
    unit_two = middle * scale_two
    normed_two = low(unit_two * gain_two)
    pre = mm(wup_turn_scr[...], normed_two)
    square = pre * pre
    bend = jnp.tanh(GELU_RATE * pre * (1.0 + GELU_CUBE * square))
    half = 0.5 * (1.0 + bend)
    hidden = low(pre * half)
    slope = half + (0.5 * GELU_RATE) * pre * (1.0 - bend * bend) * (1.0 + 3.0 * GELU_CUBE * square)
    side_out = middle + mm(wback_turn_scr[...], hidden)
    yield

    grad_low = low(grad_out)
    gback_scr[...] += mm(hidden, grad_low, NT)
    grad_pre = low(mm(w_back, grad_low) * slope)
    gup_scr[...] += mm(normed_two, grad_pre, NT)
    grad_normed_two = mm(wup_scr[...], grad_pre)
    ggain_scr[1] += fold_lanes(grad_normed_two * unit_two)
    grad_middle = grad_out + norm_back(unit_two, scale_two, gain_two, grad_normed_two)
    grad_attended = low(grad_middle)
    gproj_scr[...] += mm(context_low, grad_attended, NT)
    grad_context = low(mm(w_out, grad_attended) * inverse)
    pad = jnp.zeros((L - DS, seqs * L), jnp.bfloat16)
    dots = (grad_context.astype(jnp.float32) * context).reshape(SH, SHD, seqs * L)
    dots = jnp.sum(dots, axis=1, keepdims=True)

    grad_context = jnp.concatenate([grad_context, pad], axis=0)
    grad_query, grad_key, grad_value = [], [], []
    yield
    for s in range(0, seqs, 2):
        prob_two = mm(two_by_head(value, s), two_apart(grad_context, s))
        for side in range(2):
            at = slice((s + side) * L, (s + side + 1) * L)
            grad_probs = prob_two[:, side * L : (side + 1) * L].reshape(SH, L, L)
            grad_scores = elow_scr[base + s + side].astype(jnp.float32).reshape(SH, L, L) * (
                grad_probs - dots[:, :, at]
            )
            gbias_scr[...] += grad_scores.reshape(SH * L, L)
            grad_scores = low(grad_scores).reshape(SH * L, L)
            grad_query.append(low(mm(by_head_lanes(key[0:DS, at]), grad_scores)))
            grad_key.append(low(mm(lanes_of(grad_scores), by_head_rows(query[0:DS, at].T))))
            grad_value.append(
                low(mm(lanes_of(elow_scr[base + s + side]), by_head_rows(grad_context[0:DS, at].T)))
            )
        yield
    grad_query = jnp.concatenate(grad_query, axis=1)
    grad_key = jnp.concatenate(grad_key, axis=0)
    grad_value = jnp.concatenate(grad_value, axis=0)

    grad_normed = mm(wqkv_scr[0], grad_query)
    grad_normed += mm(wqkv_scr[1], grad_key, NT)
    grad_normed += mm(wqkv_scr[2], grad_value, NT)
    gqkv_scr[0] += mm(normed_one, grad_query, NT)
    gqkv_scr[1] += mm(normed_one, grad_key)
    gqkv_scr[2] += mm(normed_one, grad_value)
    ggain_scr[0] += fold_lanes(grad_normed * unit_one)
    grad_mixed = grad_middle + norm_back(unit_one, scale_one, gain_one, grad_normed)
    input_grad = gate * grad_mixed
    grad_tap = low((1.0 - gate) * grad_mixed)
    gdown_scr[...] += mm(grad_tap, taps)
    ggain_scr[2] += fold_lanes(grad_mixed * (x - tapped))
    for s in range(seqs):
        out_ref[base + s] = side_out[:, s * L : (s + 1) * L]
        ig_ref[base + s] = input_grad[:, s * L : (s + 1) * L]


def side_finish(parity, onehot_ref, mine_ref, other_ref, grow_scr, scratch):
    (
        gain_scr,
        wdown_scr,
        wqkv_scr,
        wqkv_turn_scr,
        wout_turn_scr,
        wup_scr,
        wup_turn_scr,
        wback_turn_scr,
        bias_scr,
        gbias_scr,
        elow_scr,
        gdown_scr,
        gqkv_scr,
        gproj_scr,
        gup_scr,
        gback_scr,
        ggain_scr,
    ) = scratch
    grow_scr[:, DS:] = jnp.zeros((grow_scr.shape[0], grow_scr.shape[1] - DS), jnp.bfloat16)
    grow_scr[0:D, 0:DS] = low(gdown_scr[...].T)
    spread = mm(pick_rows(3, 0, DS), low(gqkv_scr[0]), TN)
    for t in range(1, 3):
        spread = spread + mm(pick_rows(3, t, DS), low(gqkv_scr[t]), TN)
    grow_scr[AT_QKV:AT_OUT, 0:DS] = low(spread)
    grow_scr[AT_OUT:AT_UP, 0:DS] = low(gproj_scr[...])
    spread = mm(pick_rows(4, 0, DS), low(gup_scr[:, 0:DS]), TN)
    for t in range(1, 4):
        spread = spread + mm(pick_rows(4, t, DS), low(gup_scr[:, t * DS : (t + 1) * DS]), TN)
    grow_scr[AT_UP:AT_BACK, 0:DS] = low(spread)
    grow_scr[AT_BACK : AT_END, 0:DS] = low(gback_scr[...])
    flip_row = lax.broadcasted_iota(jnp.int32, (L, L), 0)
    flip_column = lax.broadcasted_iota(jnp.int32, (L, L), 1)
    flip = (flip_row + flip_column == L - 1).astype(jnp.float32)
    diagonals = []
    for head in range(SH):
        square = lax.dot_general(
            flip,
            gbias_scr[head * L : (head + 1) * L, :],
            NN,
            precision=PRECISE,
            preferred_element_type=jnp.float32,
        )
        full = jnp.concatenate([square, jnp.zeros_like(square)], axis=1)
        rolled = pltpu.roll(full, 0, 1, stride=1, stride_axis=0)
        diagonals.append(jnp.sum(rolled, axis=0, keepdims=True))
    diagonals = jnp.concatenate(diagonals, axis=0)
    gains = []
    for row in range(3):
        total = ggain_scr[row]
        if row == 2:
            total = total * (gain_scr[2] * (1.0 - gain_scr[2]))
        total = jnp.sum(total.T, axis=0, keepdims=True)
        gains += [total[:, part * NARROW : (part + 1) * NARROW] for part in range(3)]
    table = lax.dot_general(
        diagonals, onehot_ref[...], NT, precision=PRECISE, preferred_element_type=jnp.float32
    )
    small = low(jnp.concatenate([table] + gains, axis=0))
    pairs = mine_ref.shape[0]
    shard_rows = AT_END // (2 * pairs)
    blank = jnp.zeros((mine_ref.shape[1] - shard_rows, L), jnp.bfloat16)

    def place(even_ref, odd_ref):
        for device in range(2 * pairs):
            ref, slot = (even_ref, odd_ref)[device % 2], device // 2
            ref[slot, 0:shard_rows, :] = grow_scr[device * shard_rows : (device + 1) * shard_rows, :]
            if blank.shape[0]:
                ref[slot, shard_rows:, :] = blank
            ref[slot, 0 : small.shape[0], DS:] = small

    @pl.when(parity == 0)
    def _():
        place(mine_ref, other_ref)

    @pl.when(parity == 1)
    def _():
        place(other_ref, mine_ref)


def main_kernel(
    seqs,
    chunk,
    meta_ref,
    len_ref,
    tok_ref,
    gain_ref,
    far_ref,
    mate_ref,
    table_ref,
    near_ref,
    x_ref,
    go_ref,
    side_gain_ref,
    side_table_ref,
    onehot_ref,
    turn_onehot_ref,
    wo_hbm,
    up_hbm,
    down_hbm,
    w_hbm,
    out_ref,
    ig_ref,
    mine_ref,
    other_ref,
    diag_scr,
    w_scr,
    bias_scr,
    ctx_scr,
    taps_scr,
    wo_scr,
    up_scr,
    down_scr,
    wrow_scr,
    grow_scr,
    sems,
    *scratch,
):
    step = pl.program_id(0)
    group = meta_ref[2]
    width = near_ref.shape[0]
    copies = [
        pltpu.make_async_copy(
            wo_hbm.at[pl.ds(group * width, width), :], wo_scr.at[pl.ds(0, width), :], sems.at[0]
        ),
        pltpu.make_async_copy(
            wo_hbm.at[pl.ds((1 - group) * width, width), :],
            wo_scr.at[pl.ds(width, width), :],
            sems.at[1],
        ),
        pltpu.make_async_copy(up_hbm, up_scr, sems.at[2]),
        pltpu.make_async_copy(down_hbm, down_scr, sems.at[3]),
        pltpu.make_async_copy(w_hbm, wrow_scr, sems.at[4]),
    ]

    @pl.when(step == 0)
    def _():
        for copy in copies:
            copy.start()
        attention_setup(
            meta_ref[1],
            1 - group,
            far_ref,
            mate_ref,
            table_ref,
            onehot_ref,
            diag_scr,
            w_scr,
            bias_scr,
        )

    lengths = [len_ref[meta_ref[0] + step * seqs + s] for s in range(seqs)]
    half = seqs // 2
    at = [slice(h * half * L, (h + 1) * half * L) for h in range(2)]

    def rows(h):
        return tok_ref[h * half : (h + 1) * half].reshape(half * L, D).astype(jnp.float32)

    def attend(h):
        return attention_steps(
            lengths[h * half : (h + 1) * half],
            rows(h),
            gain_ref[0:1, :],
            w_scr,
            bias_scr,
            ctx_scr,
            h * half * L,
        )

    def feed(h):
        return feed_steps(
            chunk,
            rows(h),
            near_ref[:, at[h]],
            ctx_scr[:, at[h]],
            gain_ref[1:2, :],
            wo_scr,
            up_scr,
            down_scr,
            taps_scr,
            at[h],
        )

    def side(h):
        return side_steps(
            lengths[h * half : (h + 1) * half],
            h * half,
            taps_scr[at[h], :],
            x_ref,
            go_ref,
            wrow_scr,
            out_ref,
            ig_ref,
            scratch,
        )

    together(attend(0), attend(1))
    @pl.when(step == 0)
    def _():
        for copy in copies:
            copy.wait()
        side_setup(side_gain_ref, wrow_scr, side_table_ref, onehot_ref, scratch)

    together(feed(0), feed(1))
    together(side(0), side(1))

    @pl.when(step == pl.num_programs(0) - 1)
    def _():
        side_finish(meta_ref[1], turn_onehot_ref, mine_ref, other_ref, grow_scr, scratch)


def main_part(
    meta,
    lengths,
    tokens,
    gains,
    far,
    mate,
    table,
    ctx_near,
    side_input,
    output_grad,
    side_gains,
    side_table,
    onehot,
    turn_onehot,
    w_out,
    w_up,
    w_down,
    w_rows,
    devices,
    seqs,
    chunk,
):
    own_seqs = side_input.shape[0]
    width = ctx_near.shape[0]
    ff = w_up.shape[1]
    send_rows = -(-max(w_rows.shape[0] // devices, SMALL_ROWS) // 8) * 8
    send_shape = (devices // 2, send_rows, L)
    fixed = lambda *dims: pl.BlockSpec(dims, lambda i, m, n: (0,) * len(dims))
    block = pl.BlockSpec((seqs, DS, L), lambda i, m, n: (i, 0, 0))
    hbm = pl.BlockSpec(memory_space=pl.ANY)
    f32, bf16 = jnp.float32, jnp.bfloat16
    return pl.pallas_call(
        functools.partial(main_kernel, seqs, chunk),
        name="main",
        grid_spec=pltpu.PrefetchScalarGridSpec(
            num_scalar_prefetch=2,
            grid=(own_seqs // seqs,),
            in_specs=[
                pl.BlockSpec((seqs, L, D), lambda i, m, n: (m[0] // seqs + i, 0, 0)),
                fixed(2, D),
                fixed(*far.shape),
                fixed(*mate.shape),
                fixed(*table.shape),
                pl.BlockSpec((width, seqs * L), lambda i, m, n: (0, i)),
                block,
                block,
                fixed(*side_gains.shape),
                fixed(*side_table.shape),
                fixed(*onehot.shape),
                fixed(*turn_onehot.shape),
                hbm,
                hbm,
                hbm,
                hbm,
            ],
            out_specs=[block, block, fixed(*send_shape), fixed(*send_shape)],
            scratch_shapes=[
                pltpu.VMEM((table.shape[0], SPAN), f32),
                pltpu.VMEM((3 * width, D), bf16),
                pltpu.VMEM((width // HD * L, L), f32),
                pltpu.VMEM((width, seqs * L), bf16),
                pltpu.VMEM((seqs * L, D), bf16),
                pltpu.VMEM(w_out.shape, bf16),
                pltpu.VMEM(w_up.shape, bf16),
                pltpu.VMEM(w_down.shape, bf16),
                pltpu.VMEM(w_rows.shape, bf16),
                pltpu.VMEM((w_rows.shape[0], L), bf16),
                pltpu.SemaphoreType.DMA((5,)),
                pltpu.VMEM((3, DS, L), f32),
                pltpu.VMEM((DS, D), bf16),
                pltpu.VMEM((3, DS, DS), bf16),
                pltpu.VMEM((3 * L, DS), bf16),
                pltpu.VMEM((DS, DS), bf16),
                pltpu.VMEM((DS, SFF), bf16),
                pltpu.VMEM((SFF, DS), bf16),
                pltpu.VMEM((DS, SFF), bf16),
                pltpu.VMEM((SH * L, L), f32),
                pltpu.VMEM((SH * L, L), f32),
                pltpu.VMEM((seqs, SH * L, L), bf16),
                pltpu.VMEM((DS, D), f32),
                pltpu.VMEM((3, DS, DS), f32),
                pltpu.VMEM((DS, DS), f32),
                pltpu.VMEM((DS, SFF), f32),
                pltpu.VMEM((SFF, DS), f32),
                pltpu.VMEM((3, DS, L), f32),
            ],
        ),
        out_shape=[
            jax.ShapeDtypeStruct(side_input.shape, f32),
            jax.ShapeDtypeStruct(side_input.shape, f32),
            jax.ShapeDtypeStruct(send_shape, bf16),
            jax.ShapeDtypeStruct(send_shape, bf16),
        ],
        compiler_params=pltpu.CompilerParams(
            dimension_semantics=("arbitrary",), vmem_limit_bytes=VMEM_MAIN * MIB
        ),
        cost_estimate=pl.CostEstimate(
            flops=2 * own_seqs * L * (D * (D + 2 * ff) + width * (3 * D + 2 * L))
            + own_seqs * 300_000_000,
            bytes_accessed=own_seqs * L * (3 * D + 16 * DS) + 2 * D * (D + 2 * ff),
            transcendentals=own_seqs * L * (ff + 2 * SH * L + SFF),
        ),
    )(
        meta,
        lengths,
        tokens,
        gains,
        far,
        mate,
        table,
        ctx_near,
        side_input,
        output_grad,
        side_gains,
        side_table,
        onehot,
        turn_onehot,
        w_out,
        w_up,
        w_down,
        w_rows,
    )


def adamw_update(weight_now, first_now, second_now, gradient, rate, decay_rate):
    first_new = BETA_ONE * first_now + (1.0 - BETA_ONE) * gradient
    second_new = BETA_TWO * second_now + (1.0 - BETA_TWO) * gradient * gradient
    first_hat = first_new / (1.0 - BETA_ONE**ADAM_STEP)
    second_hat = second_new / (1.0 - BETA_TWO**ADAM_STEP)
    weight_new = weight_now - rate * (
        first_hat / (jnp.sqrt(second_hat) + ADAM_EPS) + decay_rate * weight_now
    )
    return (first_new, second_new, weight_new)


def collect_kernel(got_ref, shard_ref, gains_ref, table_ref, square_ref):
    total = got_ref[0].astype(jnp.float32)
    for device in range(1, got_ref.shape[0]):
        total = total + got_ref[device].astype(jnp.float32)
    shard = total[0 : shard_ref.shape[0], 0:DS]
    shard_ref[...] = shard
    table_ref[...] = total[0:SH, DS:]
    for row in range(3):
        for part in range(3):
            at = SH + 3 * row + part
            gains_ref[row : row + 1, part * NARROW : (part + 1) * NARROW] = total[at : at + 1, DS:]
    square = jnp.sum(jnp.sum(shard * shard, axis=1, keepdims=True), axis=0, keepdims=True)
    square_ref[...] = jnp.broadcast_to(square, square_ref.shape)


def collect_part(got, shard_rows):
    return pl.pallas_call(
        collect_kernel,
        name="collect",
        out_shape=[
            jax.ShapeDtypeStruct((shard_rows, DS), jnp.float32),
            jax.ShapeDtypeStruct((3, DS), jnp.float32),
            jax.ShapeDtypeStruct((SH, NARROW), jnp.float32),
            jax.ShapeDtypeStruct((2 * got.shape[0], L), jnp.float32),
        ],
        in_specs=[pl.BlockSpec(memory_space=pltpu.VMEM)],
        out_specs=[pl.BlockSpec(memory_space=pltpu.VMEM)] * 4,
    )(got)


def update_kernel(square_ref, gains_sum_ref, table_sum_ref, shard_ref, *refs):
    weights, gains, table = refs[0:3], refs[3:6], refs[6:9]
    norm_ref, copy_ref = refs[9], refs[13]
    gains_total = gains_sum_ref[...]
    table_total = table_sum_ref[...]
    whole = lambda values: jnp.sum(
        jnp.sum(values, axis=1, keepdims=True), axis=0, keepdims=True
    )
    norm = jnp.sqrt(
        jnp.sum(square_ref[:, 0:1], axis=0, keepdims=True)
        + whole(gains_total * gains_total)
        + whole(table_total * table_total)
    )
    norm_ref[...] = norm
    factor = CLIP_NORM / jnp.maximum(norm, CLIP_NORM)

    def update(state, gradient, outs, rate, decay):
        results = adamw_update(*[ref[...] for ref in state], factor * gradient, rate, decay)
        for ref, value in zip(outs, results):
            ref[...] = value
        return results[2]

    new = update(weights, shard_ref[...], refs[10:13], RATE_MATRIX, WEIGHT_DECAY)
    copy_ref[...] = new.astype(jnp.bfloat16)
    update(gains, gains_total, refs[14:17], RATE_SMALL, 0.0)
    update(table, table_total, refs[17:20], RATE_SMALL, 0.0)


def update_part(squares, gains_sum, table_sum, shard, weights, gains, table):
    f32 = jnp.float32
    like = lambda values, dtype=f32: jax.ShapeDtypeStruct(values.shape, dtype)
    operands = (squares, gains_sum, table_sum, shard, *weights, *gains, *table)
    return pl.pallas_call(
        update_kernel,
        name="update",
        out_shape=[
            jax.ShapeDtypeStruct((1, 1), f32),
            *[like(values) for values in weights],
            like(shard, jnp.bfloat16),
            *[like(values) for values in gains],
            *[like(values) for values in table],
        ],
        in_specs=[pl.BlockSpec(memory_space=pltpu.VMEM)] * len(operands),
        out_specs=[pl.BlockSpec(memory_space=pltpu.VMEM)] * 11,
    )(*operands)


def swap(values, distance):
    size = lax.axis_size("mp")
    return lax.ppermute(values, "mp", [(i, i ^ distance) for i in range(size)])


def exchange(values):
    return lax.all_to_all(values, ("batch", "mp"), split_axis=0, concat_axis=0, tiled=True)


def exchange_alike(values):
    groups = [[2 * i + parity for i in range(values.shape[0])] for parity in range(2)]
    return lax.all_to_all(
        values,
        ("batch", "mp"),
        split_axis=0,
        concat_axis=0,
        axis_index_groups=groups,
        tiled=True,
    )


def on_device(
    tokens,
    lengths,
    base_gains,
    base_qkv,
    base_out,
    base_up,
    base_down,
    base_table,
    side_input,
    output_grad,
    side_weights,
    weights_first,
    weights_second,
    side_gains,
    gains_first,
    gains_second,
    side_table,
    table_first,
    table_second,
):
    devices = lax.axis_size(("batch", "mp"))
    model_index = lax.axis_index("mp")
    own_seqs = side_input.shape[0]
    shard_rows = side_weights.shape[0] // DS
    buckets = side_table.shape[0]
    meta = jnp.stack([model_index * own_seqs, model_index % 2, model_index // 2]).astype(jnp.int32)

    turn = lambda values: jnp.transpose(values, (0, 2, 1))
    qkv_own = turn(base_qkv)
    qkv_far = swap(qkv_own, 2)
    lanes = L if side_weights.shape[0] % L == 0 else DS
    flat = lambda values: values.reshape(-1, lanes)
    low_rows = flat(side_weights.astype(jnp.bfloat16))
    low_rows = jnp.broadcast_to(low_rows[None], (devices,) + low_rows.shape)
    w_rows = exchange(low_rows)
    qkv_mate = swap(qkv_own, 1)

    onehot = jnp.asarray(diagonal_onehot(buckets))
    ctx_near = near_part(
        meta, lengths, tokens, base_gains, qkv_own, qkv_mate, base_table.T, onehot, own_seqs, 8
    )
    ctx_near, qkv_far, w_rows = lax.optimization_barrier((ctx_near, qkv_far, w_rows))
    qkv_far_mate = swap(qkv_far, 1)
    side_output, input_grad, mine, other = main_part(
        meta,
        lengths,
        tokens,
        base_gains,
        qkv_far,
        qkv_far_mate,
        base_table.T,
        ctx_near,
        turn(side_input),
        turn(output_grad),
        side_gains,
        side_table.T,
        onehot,
        jnp.asarray(gradient_onehot(buckets)),
        base_out,
        base_up,
        base_down,
        w_rows.reshape(devices * shard_rows, DS),
        devices,
        8,
        1024,
    )

    paired = mine.astype(jnp.float32) + swap(other, 1).astype(jnp.float32)
    grad_shard, gains_sum, table_sum, squares = collect_part(
        exchange_alike(paired.astype(jnp.bfloat16)), shard_rows
    )
    (
        grad_norm,
        weights_moment,
        weights_square,
        weights_new,
        weights_copy,
        gains_moment,
        gains_square,
        gains_new,
        table_moment,
        table_square,
        table_new,
    ) = update_part(
        exchange(squares),
        gains_sum,
        table_sum,
        flat(grad_shard),
        [flat(side_weights), flat(weights_first), flat(weights_second)],
        [side_gains, gains_first, gains_second],
        [side_table.T, table_first.T, table_second.T],
    )
    return (
        turn(side_output),
        turn(input_grad),
        grad_norm.reshape(()),
        weights_moment.reshape(-1),
        weights_square.reshape(-1),
        weights_new.reshape(-1),
        weights_copy.reshape(-1),
        gains_moment,
        gains_square,
        gains_new,
        table_moment.T,
        table_square.T,
        table_new.T,
    )


def solution(mesh):
    return jax.shard_map(
        on_device,
        mesh=mesh,
        in_specs=(
            P("batch", None, None),
            P("batch"),
            P(),
            P(None, None, "mp"),
            P(),
            P(),
            P(),
            P(),
            P(("batch", "mp"), None, None),
            P(("batch", "mp"), None, None),
            P(("batch", "mp")),
            P(("batch", "mp")),
            P(("batch", "mp")),
            P(),
            P(),
            P(),
            P(),
            P(),
            P(),
        ),
        out_specs=(
            P(("batch", "mp"), None, None),
            P(("batch", "mp"), None, None),
            P(),
            P(("batch", "mp")),
            P(("batch", "mp")),
            P(("batch", "mp")),
            P(("batch", "mp")),
            P(),
            P(),
            P(),
            P(),
            P(),
            P(),
        ),
        check_vma=False,
    )
```

```python
import functools
import math
import jax
import jax.numpy as jnp
import numpy as np
from jax import lax
from jax.experimental import pallas as pl
from jax.experimental.pallas import tpu as pltpu
from jax.sharding import PartitionSpec as P

D = 768
HD = 64
DS = 96
SH = 12
SHD = 8
SFF = 384
MAXD = 128
L = 128
ADAM_STEP = 10
PAIR = 2 * HD
SPAN = 2 * L
NARROW = L - DS
SMALL_ROWS = SH + 9

NORM_EPS = 1e-06
CLIP_NORM = 1.0
BETA_ONE = 0.9
BETA_TWO = 0.999
ADAM_EPS = 1e-08
RATE_MATRIX = 0.1
RATE_SMALL = 0.5
WEIGHT_DECAY = 0.01
MASKED = -1e30
PRECISE = lax.Precision.HIGHEST
MIB = 1 << 20
VMEM_MAIN = 60
GELU_RATE = math.sqrt(2.0 / math.pi)
GELU_CUBE = 0.044715

NN = (((1,), (0,)), ((), ()))
NT = (((1,), (1,)), ((), ()))
TN = (((0,), (0,)), ((), ()))


def mm(left, right, dims=NN):
    return lax.dot_general(left, right, dims, preferred_element_type=jnp.float32)


def bucket_of(offset, buckets, reach):
    half_count = buckets // 2
    exact_count = half_count // 2
    distance = np.abs(offset)
    spread_part = (
        np.log(np.maximum(distance, 1) / exact_count)
        / np.log(reach / exact_count)
        * (half_count - exact_count)
    )
    far_bucket = np.minimum(exact_count + np.floor(spread_part).astype(np.int32), half_count - 1)
    near_side = np.where(distance < exact_count, distance, far_bucket)
    return (near_side + (offset > 0) * half_count).astype(np.int32)


def diagonal_onehot(buckets):
    column = np.arange(SPAN)
    offset = np.where(column < L, -column, SPAN - column)
    onehot = bucket_of(offset, buckets, MAXD)[None, :] == np.arange(buckets)[:, None]
    onehot = onehot & (column != L)[None, :]
    return onehot.astype(np.float32)


def gradient_onehot(buckets):
    column = np.arange(SPAN)
    onehot = bucket_of(L - 1 - column, buckets, MAXD)[None, :] == np.arange(buckets)[:, None]
    onehot = onehot & (column != SPAN - 1)[None, :]
    return onehot.astype(np.float32)


def rms_scale(values):
    return lax.rsqrt(jnp.mean(values * values, axis=-1, keepdims=True) + NORM_EPS)


def gelu(v):
    return 0.5 * v * (1.0 + jnp.tanh(GELU_RATE * (v + GELU_CUBE * (v * v * v))))


def diagonals_of(table_ref, onehot_ref):
    return lax.dot_general(
        table_ref[...],
        onehot_ref[...],
        NN,
        precision=PRECISE,
        preferred_element_type=jnp.float32,
    )


def spread_bias(row):
    full = jnp.broadcast_to(row, (L, SPAN))
    return pltpu.roll(full, 0, 1, stride=1, stride_axis=0)[:, :L]


def attention_setup(
    parity, group, own_ref, mate_ref, table_ref, onehot_ref, diag_scr, w_scr, bias_scr
):
    third = own_ref.shape[1]
    width = 2 * third
    heads = width // HD

    def place(low_ref, high_ref):
        for part in range(3):
            w_scr[part * width : part * width + third, :] = low_ref[part]
            w_scr[part * width + third : (part + 1) * width, :] = high_ref[part]

    @pl.when(parity == 0)
    def _():
        place(own_ref, mate_ref)

    @pl.when(parity == 1)
    def _():
        place(mate_ref, own_ref)

    diag_scr[...] = diagonals_of(table_ref, onehot_ref)
    for head in range(heads):
        bias_scr[head * L : (head + 1) * L, :] = spread_bias(
            diag_scr[pl.ds(group * heads + head, 1), :]
        )


def together(*steps):
    waiting = list(steps)
    while waiting:
        for stage in list(waiting):
            if next(stage, StopIteration) is StopIteration:
                waiting.remove(stage)


def attention_steps(lengths, normed, w_scr, bias_scr, ctx_ref, base):
    width = w_scr.shape[0] // 3
    turned = mm(w_scr[...], normed, NT).astype(jnp.bfloat16)
    query, key, value = turned[0:width], turned[width : 2 * width], turned[2 * width :]
    yield
    low_lane = lax.broadcasted_iota(jnp.int32, (L, PAIR), 1) < HD
    low_row = lax.broadcasted_iota(jnp.int32, (PAIR, L), 0) < HD
    key_row = lax.broadcasted_iota(jnp.int32, (2, L, L), 1)
    for s, length in enumerate(lengths):
        at = slice(s * L, (s + 1) * L)
        seen = key_row < length
        for p in range(width // PAIR):
            head = slice(p * PAIR, (p + 1) * PAIR)
            k_one, v_one = key[head, at].T, value[head, at]
            zero = jnp.zeros_like(k_one)
            k_two = jnp.concatenate(
                [jnp.where(low_lane, k_one, zero), jnp.where(low_lane, zero, k_one)], axis=0
            )
            v_two = jnp.concatenate(
                [jnp.where(low_row, v_one, zero), jnp.where(low_row, zero, v_one)], axis=1
            )
            scores = mm(k_two, query[head, at]) + bias_scr[p * 2 * L : (p + 1) * 2 * L, :]
            scores = jnp.where(seen, scores.reshape(2, L, L), MASKED)
            shifted = jnp.exp(scores - jnp.max(scores, axis=1, keepdims=True))
            scale = 1.0 / jnp.sum(shifted, axis=1, keepdims=True)
            scale = jnp.broadcast_to(scale, (2, HD, L)).reshape(PAIR, L)
            probs = shifted.astype(jnp.bfloat16).reshape(2 * L, L)
            into = slice(base + s * L, base + (s + 1) * L)
            ctx_ref[head, into] = (mm(v_two, probs) * scale).astype(jnp.bfloat16)
        yield


def near_kernel(
    seqs,
    meta_ref,
    len_ref,
    tok_ref,
    gain_ref,
    own_ref,
    mate_ref,
    table_ref,
    onehot_ref,
    wo_ref,
    normed_ref,
    partial_ref,
    ctx_scr,
    diag_scr,
    w_scr,
    bias_scr,
):
    step = pl.program_id(0)

    @pl.when(step == 0)
    def _():
        attention_setup(
            meta_ref[1],
            meta_ref[2],
            own_ref,
            mate_ref,
            table_ref,
            onehot_ref,
            diag_scr,
            w_scr,
            bias_scr,
        )

    lengths = [len_ref[meta_ref[0] + step * seqs + s] for s in range(seqs)]
    rows = tok_ref[...].reshape(seqs * L, D).astype(jnp.float32)
    normed = (rows * rms_scale(rows) * gain_ref[0:1, :]).astype(jnp.bfloat16)
    normed_ref[...] = normed
    together(attention_steps(lengths, normed, w_scr, bias_scr, ctx_scr, 0))
    partial_ref[...] = (rows + mm(ctx_scr[...], wo_ref[...], TN)).astype(jnp.bfloat16)


def near_part(meta, lengths, tokens, gains, own, mate, table, onehot, w_out, own_seqs, seqs):
    width = 2 * own.shape[1]
    fixed = lambda *dims: pl.BlockSpec(dims, lambda i, m, n: (0,) * len(dims))
    return pl.pallas_call(
        functools.partial(near_kernel, seqs),
        name="near",
        grid_spec=pltpu.PrefetchScalarGridSpec(
            num_scalar_prefetch=2,
            grid=(own_seqs // seqs,),
            in_specs=[
                pl.BlockSpec((seqs, L, D), lambda i, m, n: (m[0] // seqs + i, 0, 0)),
                fixed(2, D),
                fixed(*own.shape),
                fixed(*mate.shape),
                fixed(*table.shape),
                fixed(*onehot.shape),
                pl.BlockSpec((width, D), lambda i, m, n: (m[2], 0)),
            ],
            out_specs=[pl.BlockSpec((seqs * L, D), lambda i, m, n: (i, 0))] * 2,
            scratch_shapes=[
                pltpu.VMEM((width, seqs * L), jnp.bfloat16),
                pltpu.VMEM((table.shape[0], SPAN), jnp.float32),
                pltpu.VMEM((3 * width, D), jnp.bfloat16),
                pltpu.VMEM((width // HD * L, L), jnp.float32),
            ],
        ),
        out_shape=[jax.ShapeDtypeStruct((own_seqs * L, D), jnp.bfloat16)] * 2,
        compiler_params=pltpu.CompilerParams(
            dimension_semantics=("arbitrary",), vmem_limit_bytes=56 * MIB
        ),
        cost_estimate=pl.CostEstimate(
            flops=2 * own_seqs * L * width * (4 * D + 2 * L),
            bytes_accessed=own_seqs * L * 3 * D * 2 + 6 * D * width,
            transcendentals=own_seqs * width // HD * L * L,
        ),
    )(meta, lengths, tokens, gains, own, mate, table, onehot, w_out)


def feed_steps(chunk, rows, far, gain, wo_scr, up_scr, down_scr, taps_scr, at):
    middle = rows + mm(far, wo_scr[...], TN)
    normed = (middle * rms_scale(middle) * gain).astype(jnp.bfloat16)
    total = jnp.zeros_like(middle)
    yield
    for c in range(0, up_scr.shape[1], chunk):
        hidden = gelu(mm(normed, up_scr[:, c : c + chunk])).astype(jnp.bfloat16)
        yield
        total = total + mm(hidden, down_scr[c : c + chunk, :])
        yield
    taps_scr[at, :] = (middle + total).astype(jnp.bfloat16)


def pick_rows(step, phase, count):
    row = lax.broadcasted_iota(jnp.int32, (count, step * count), 0)
    column = lax.broadcasted_iota(jnp.int32, (count, step * count), 1)
    return (column == step * row + phase).astype(jnp.bfloat16)


def by_head_rows(block):
    head = lax.broadcasted_iota(jnp.int32, block.shape, 1) // SHD
    zero = jnp.zeros_like(block)
    return jnp.concatenate([jnp.where(head == h, block, zero) for h in range(SH)], axis=0)


def by_head_lanes(block):
    head = lax.broadcasted_iota(jnp.int32, block.shape, 0) // SHD
    zero = jnp.zeros_like(block)
    return jnp.concatenate([jnp.where(head == h, block, zero) for h in range(SH)], axis=1)


def lanes_of(stacked):
    return jnp.concatenate([stacked[h * L : (h + 1) * L] for h in range(SH)], axis=1)


def norm_back(unit, scale, gain, grad):
    scaled = grad * gain
    return scale * (scaled - unit * jnp.mean(scaled * unit, axis=0, keepdims=True))


def two_by_head(turned, first):
    blocks = [by_head_rows(turned[:, s * L : (s + 1) * L].T) for s in (first, first + 1)]
    return jnp.concatenate(blocks, axis=1)


def two_apart(turned, first):
    zero = jnp.zeros((L, L), turned.dtype)
    one, two = turned[:, first * L : (first + 1) * L], turned[:, (first + 1) * L : (first + 2) * L]
    return jnp.concatenate(
        [jnp.concatenate([one, zero], axis=1), jnp.concatenate([zero, two], axis=1)], axis=0
    )


def column_scale(values):
    return lax.rsqrt(jnp.mean(values * values, axis=0, keepdims=True) + NORM_EPS)


def fold_lanes(values):
    total = values[:, 0:L]
    for s in range(1, values.shape[1] // L):
        total = total + values[:, s * L : (s + 1) * L]
    return total


AT_QKV, AT_OUT, AT_UP, AT_BACK, AT_END = D, D + 3 * DS, D + 4 * DS, D + 8 * DS, D + 8 * DS + SFF


def low(values):
    return values.astype(jnp.bfloat16)


def side_setup(gain_ref, w_ref, table_ref, onehot_ref, scratch):
    (
        gain_scr,
        wdown_scr,
        wqkv_scr,
        wqkv_turn_scr,
        wout_turn_scr,
        wup_scr,
        wup_turn_scr,
        wback_turn_scr,
        bias_scr,
        gbias_scr,
        elow_scr,
        gdown_scr,
        gqkv_scr,
        gproj_scr,
        gup_scr,
        gback_scr,
        ggain_scr,
    ) = scratch
    wdown_scr[...] = w_ref[0:D, :].T
    for t in range(3):
        part = mm(pick_rows(3, t, DS), w_ref[AT_QKV:AT_OUT, :])
        wqkv_scr[t] = low(part)
        wqkv_turn_scr[t * L : t * L + DS, :] = low(part.T)
        wqkv_turn_scr[t * L + DS : (t + 1) * L, :] = jnp.zeros((L - DS, DS), jnp.bfloat16)
    wout_turn_scr[...] = w_ref[AT_OUT:AT_UP, :].T
    for t in range(4):
        part = mm(pick_rows(4, t, DS), w_ref[AT_UP:AT_BACK, :])
        wup_scr[:, t * DS : (t + 1) * DS] = low(part)
        wup_turn_scr[t * DS : (t + 1) * DS, :] = low(part.T)
    wback_turn_scr[...] = w_ref[AT_BACK : AT_END, :].T
    for row in range(3):
        wide = jnp.broadcast_to(gain_ref[row : row + 1, :], (L, DS)).T
        gain_scr[row] = jax.nn.sigmoid(wide) if row == 2 else wide
    diagonals = diagonals_of(table_ref, onehot_ref)
    for head in range(SH):
        bias_scr[head * L : (head + 1) * L, :] = spread_bias(diagonals[head : head + 1, :])
    for ref in (gbias_scr, gdown_scr, gqkv_scr, gproj_scr, gup_scr, gback_scr, ggain_scr):
        ref[...] = jnp.zeros_like(ref)


def side_steps(lengths, base, taps, x_ref, go_ref, w_ref, out_ref, ig_ref, scratch):
    (
        gain_scr,
        wdown_scr,
        wqkv_scr,
        wqkv_turn_scr,
        wout_turn_scr,
        wup_scr,
        wup_turn_scr,
        wback_turn_scr,
        bias_scr,
        gbias_scr,
        elow_scr,
        gdown_scr,
        gqkv_scr,
        gproj_scr,
        gup_scr,
        gback_scr,
        ggain_scr,
    ) = scratch
    seqs = len(lengths)
    wide = lambda row: jnp.concatenate([gain_scr[row]] * seqs, axis=1)
    gain_one, gain_two, gate = wide(0), wide(1), wide(2)
    w_out = w_ref[AT_OUT:AT_UP, :]
    w_back = w_ref[AT_BACK : AT_END, :]
    key_row = lax.broadcasted_iota(jnp.int32, (SH, L, L), 1)
    token = lax.broadcasted_iota(jnp.int32, (DS, L), 1)
    x = jnp.concatenate([x_ref[base + s] for s in range(seqs)], axis=1)
    grad_out = jnp.concatenate(
        [jnp.where(token < lengths[s], go_ref[base + s], 0.0) for s in range(seqs)], axis=1
    )

    tapped = mm(wdown_scr[...], taps, NT)
    mixed = gate * x + (1.0 - gate) * tapped
    scale_one = column_scale(mixed)
    unit_one = mixed * scale_one
    normed_one = low(unit_one * gain_one)
    qkv = low(mm(wqkv_turn_scr[...], normed_one))

    query, key, value = qkv[0:L], qkv[L : 2 * L], qkv[2 * L :]
    context, inverse = [], []
    yield
    for s in range(0, seqs, 2):
        score_two = mm(two_by_head(key, s), two_apart(query, s))
        for side in range(2):
            at = slice((s + side) * L, (s + side + 1) * L)
            scores = score_two[:, side * L : (side + 1) * L] + bias_scr[...]
            scores = jnp.where(key_row < lengths[s + side], scores.reshape(SH, L, L), MASKED)
            shifted = jnp.exp(scores - jnp.max(scores, axis=1, keepdims=True))
            e_low = low(shifted).reshape(SH * L, L)
            elow_scr[base + s + side] = e_low
            total = 1.0 / jnp.sum(shifted, axis=1, keepdims=True)
            inverse.append(jnp.broadcast_to(total, (SH, SHD, L)).reshape(DS, L))
            context.append(mm(by_head_lanes(value[0:DS, at]), e_low) * inverse[-1])
        yield
    context = jnp.concatenate(context, axis=1)
    inverse = jnp.concatenate(inverse, axis=1)
    context_low = low(context)

    middle = mixed + mm(wout_turn_scr[...], context_low)
    scale_two = column_scale(middle)
    unit_two = middle * scale_two
    normed_two = low(unit_two * gain_two)
    pre = mm(wup_turn_scr[...], normed_two)
    square = pre * pre
    bend = jnp.tanh(GELU_RATE * pre * (1.0 + GELU_CUBE * square))
    half = 0.5 * (1.0 + bend)
    hidden = low(pre * half)
    slope = half + (0.5 * GELU_RATE) * pre * (1.0 - bend * bend) * (1.0 + 3.0 * GELU_CUBE * square)
    side_out = middle + mm(wback_turn_scr[...], hidden)
    yield

    grad_low = low(grad_out)
    gback_scr[...] += mm(hidden, grad_low, NT)
    grad_pre = low(mm(w_back, grad_low) * slope)
    gup_scr[...] += mm(normed_two, grad_pre, NT)
    grad_normed_two = mm(wup_scr[...], grad_pre)
    ggain_scr[1] += fold_lanes(grad_normed_two * unit_two)
    grad_middle = grad_out + norm_back(unit_two, scale_two, gain_two, grad_normed_two)
    grad_attended = low(grad_middle)
    gproj_scr[...] += mm(context_low, grad_attended, NT)
    grad_context = low(mm(w_out, grad_attended) * inverse)
    pad = jnp.zeros((L - DS, seqs * L), jnp.bfloat16)
    dots = (grad_context.astype(jnp.float32) * context).reshape(SH, SHD, seqs * L)
    dots = jnp.sum(dots, axis=1, keepdims=True)

    grad_context = jnp.concatenate([grad_context, pad], axis=0)
    grad_query, grad_key, grad_value = [], [], []
    yield
    for s in range(0, seqs, 2):
        prob_two = mm(two_by_head(value, s), two_apart(grad_context, s))
        for side in range(2):
            at = slice((s + side) * L, (s + side + 1) * L)
            grad_probs = prob_two[:, side * L : (side + 1) * L].reshape(SH, L, L)
            grad_scores = elow_scr[base + s + side].astype(jnp.float32).reshape(SH, L, L) * (
                grad_probs - dots[:, :, at]
            )
            gbias_scr[...] += grad_scores.reshape(SH * L, L)
            grad_scores = low(grad_scores).reshape(SH * L, L)
            grad_query.append(low(mm(by_head_lanes(key[0:DS, at]), grad_scores)))
            grad_key.append(low(mm(lanes_of(grad_scores), by_head_rows(query[0:DS, at].T))))
            grad_value.append(
                low(mm(lanes_of(elow_scr[base + s + side]), by_head_rows(grad_context[0:DS, at].T)))
            )
        yield
    grad_query = jnp.concatenate(grad_query, axis=1)
    grad_key = jnp.concatenate(grad_key, axis=0)
    grad_value = jnp.concatenate(grad_value, axis=0)

    grad_normed = mm(wqkv_scr[0], grad_query)
    grad_normed += mm(wqkv_scr[1], grad_key, NT)
    grad_normed += mm(wqkv_scr[2], grad_value, NT)
    gqkv_scr[0] += mm(normed_one, grad_query, NT)
    gqkv_scr[1] += mm(normed_one, grad_key)
    gqkv_scr[2] += mm(normed_one, grad_value)
    ggain_scr[0] += fold_lanes(grad_normed * unit_one)
    grad_mixed = grad_middle + norm_back(unit_one, scale_one, gain_one, grad_normed)
    input_grad = gate * grad_mixed
    grad_tap = low((1.0 - gate) * grad_mixed)
    gdown_scr[...] += mm(grad_tap, taps)
    ggain_scr[2] += fold_lanes(grad_mixed * (x - tapped))
    for s in range(seqs):
        out_ref[base + s] = side_out[:, s * L : (s + 1) * L]
        ig_ref[base + s] = input_grad[:, s * L : (s + 1) * L]


def side_finish(parity, onehot_ref, mine_ref, other_ref, grow_scr, scratch):
    (
        gain_scr,
        wdown_scr,
        wqkv_scr,
        wqkv_turn_scr,
        wout_turn_scr,
        wup_scr,
        wup_turn_scr,
        wback_turn_scr,
        bias_scr,
        gbias_scr,
        elow_scr,
        gdown_scr,
        gqkv_scr,
        gproj_scr,
        gup_scr,
        gback_scr,
        ggain_scr,
    ) = scratch
    grow_scr[:, DS:] = jnp.zeros((grow_scr.shape[0], grow_scr.shape[1] - DS), jnp.bfloat16)
    grow_scr[0:D, 0:DS] = low(gdown_scr[...].T)
    spread = mm(pick_rows(3, 0, DS), low(gqkv_scr[0]), TN)
    for t in range(1, 3):
        spread = spread + mm(pick_rows(3, t, DS), low(gqkv_scr[t]), TN)
    grow_scr[AT_QKV:AT_OUT, 0:DS] = low(spread)
    grow_scr[AT_OUT:AT_UP, 0:DS] = low(gproj_scr[...])
    spread = mm(pick_rows(4, 0, DS), low(gup_scr[:, 0:DS]), TN)
    for t in range(1, 4):
        spread = spread + mm(pick_rows(4, t, DS), low(gup_scr[:, t * DS : (t + 1) * DS]), TN)
    grow_scr[AT_UP:AT_BACK, 0:DS] = low(spread)
    grow_scr[AT_BACK : AT_END, 0:DS] = low(gback_scr[...])
    flip_row = lax.broadcasted_iota(jnp.int32, (L, L), 0)
    flip_column = lax.broadcasted_iota(jnp.int32, (L, L), 1)
    flip = low((flip_row + flip_column == L - 1).astype(jnp.float32))
    squares = lanes_of(gbias_scr[...])
    upper = low(squares)
    flipped = mm(flip, upper)
    flipped = flipped + mm(flip, low(squares - upper.astype(jnp.float32)))
    diagonals = []
    for head in range(SH):
        square = flipped[:, head * L : (head + 1) * L]
        full = jnp.concatenate([square, jnp.zeros_like(square)], axis=1)
        rolled = pltpu.roll(full, 0, 1, stride=1, stride_axis=0)
        diagonals.append(jnp.sum(rolled, axis=0, keepdims=True))
    diagonals = jnp.concatenate(diagonals, axis=0)
    gains = []
    for row in range(3):
        total = ggain_scr[row]
        if row == 2:
            total = total * (gain_scr[2] * (1.0 - gain_scr[2]))
        total = jnp.sum(total.T, axis=0, keepdims=True)
        gains += [total[:, part * NARROW : (part + 1) * NARROW] for part in range(3)]
    table = lax.dot_general(
        diagonals, onehot_ref[...], NT, precision=PRECISE, preferred_element_type=jnp.float32
    )
    small = low(jnp.concatenate([table] + gains, axis=0))
    pairs = mine_ref.shape[0]
    shard_rows = AT_END // (2 * pairs)
    blank = jnp.zeros((mine_ref.shape[1] - shard_rows, L), jnp.bfloat16)

    def place(even_ref, odd_ref):
        for device in range(2 * pairs):
            ref, slot = (even_ref, odd_ref)[device % 2], device // 2
            ref[slot, 0:shard_rows, :] = grow_scr[device * shard_rows : (device + 1) * shard_rows, :]
            if blank.shape[0]:
                ref[slot, shard_rows:, :] = blank
            ref[slot, 0 : small.shape[0], DS:] = small

    @pl.when(parity == 0)
    def _():
        place(mine_ref, other_ref)

    @pl.when(parity == 1)
    def _():
        place(other_ref, mine_ref)


def main_kernel(
    seqs,
    chunk,
    meta_ref,
    len_ref,
    normed_ref,
    partial_ref,
    gain_ref,
    far_ref,
    mate_ref,
    table_ref,
    x_ref,
    go_ref,
    side_gain_ref,
    side_table_ref,
    onehot_ref,
    turn_onehot_ref,
    wo_hbm,
    up_hbm,
    down_hbm,
    w_hbm,
    out_ref,
    ig_ref,
    mine_ref,
    other_ref,
    diag_scr,
    w_scr,
    bias_scr,
    ctx_scr,
    taps_scr,
    wo_scr,
    up_scr,
    down_scr,
    wrow_scr,
    grow_scr,
    sems,
    *scratch,
):
    step = pl.program_id(0)
    group = meta_ref[2]
    width = wo_scr.shape[0]
    copies = [
        pltpu.make_async_copy(wo_hbm.at[pl.ds((1 - group) * width, width), :], wo_scr, sems.at[0]),
        pltpu.make_async_copy(up_hbm, up_scr, sems.at[1]),
        pltpu.make_async_copy(down_hbm, down_scr, sems.at[2]),
        pltpu.make_async_copy(w_hbm, wrow_scr, sems.at[3]),
    ]

    @pl.when(step == 0)
    def _():
        for copy in copies:
            copy.start()
        attention_setup(
            meta_ref[1],
            1 - group,
            far_ref,
            mate_ref,
            table_ref,
            onehot_ref,
            diag_scr,
            w_scr,
            bias_scr,
        )

    lengths = [len_ref[meta_ref[0] + step * seqs + s] for s in range(seqs)]
    half = seqs // 2
    at = [slice(h * half * L, (h + 1) * half * L) for h in range(2)]

    def attend(h):
        return attention_steps(
            lengths[h * half : (h + 1) * half],
            normed_ref[at[h], :],
            w_scr,
            bias_scr,
            ctx_scr,
            h * half * L,
        )

    def feed(part):
        size = seqs * L // 4
        at = slice(part * size, (part + 1) * size)
        return feed_steps(
            chunk,
            partial_ref[at, :].astype(jnp.float32),
            ctx_scr[:, at],
            gain_ref[1:2, :],
            wo_scr,
            up_scr,
            down_scr,
            taps_scr,
            at,
        )

    def side(h):
        return side_steps(
            lengths[h * half : (h + 1) * half],
            h * half,
            taps_scr[at[h], :],
            x_ref,
            go_ref,
            wrow_scr,
            out_ref,
            ig_ref,
            scratch,
        )

    together(attend(0), attend(1))
    @pl.when(step == 0)
    def _():
        for copy in copies:
            copy.wait()
        side_setup(side_gain_ref, wrow_scr, side_table_ref, onehot_ref, scratch)

    together(*[feed(part) for part in range(4)])
    together(side(0), side(1))

    @pl.when(step == pl.num_programs(0) - 1)
    def _():
        side_finish(meta_ref[1], turn_onehot_ref, mine_ref, other_ref, grow_scr, scratch)


def main_part(
    meta,
    lengths,
    normed,
    partial,
    gains,
    far,
    mate,
    table,
    side_input,
    output_grad,
    side_gains,
    side_table,
    onehot,
    turn_onehot,
    w_out,
    w_up,
    w_down,
    w_rows,
    devices,
    seqs,
    chunk,
):
    own_seqs = side_input.shape[0]
    width = w_out.shape[0] // 2
    ff = w_up.shape[1]
    send_rows = -(-max(w_rows.shape[0] // devices, SMALL_ROWS) // 8) * 8
    send_shape = (devices // 2, send_rows, L)
    fixed = lambda *dims: pl.BlockSpec(dims, lambda i, m, n: (0,) * len(dims))
    block = pl.BlockSpec((seqs, DS, L), lambda i, m, n: (i, 0, 0))
    hbm = pl.BlockSpec(memory_space=pl.ANY)
    f32, bf16 = jnp.float32, jnp.bfloat16
    return pl.pallas_call(
        functools.partial(main_kernel, seqs, chunk),
        name="main",
        grid_spec=pltpu.PrefetchScalarGridSpec(
            num_scalar_prefetch=2,
            grid=(own_seqs // seqs,),
            in_specs=[
                pl.BlockSpec((seqs * L, D), lambda i, m, n: (i, 0)),
                pl.BlockSpec((seqs * L, D), lambda i, m, n: (i, 0)),
                fixed(2, D),
                fixed(*far.shape),
                fixed(*mate.shape),
                fixed(*table.shape),
                block,
                block,
                fixed(*side_gains.shape),
                fixed(*side_table.shape),
                fixed(*onehot.shape),
                fixed(*turn_onehot.shape),
                hbm,
                hbm,
                hbm,
                hbm,
            ],
            out_specs=[block, block, fixed(*send_shape), fixed(*send_shape)],
            scratch_shapes=[
                pltpu.VMEM((table.shape[0], SPAN), f32),
                pltpu.VMEM((3 * width, D), bf16),
                pltpu.VMEM((width // HD * L, L), f32),
                pltpu.VMEM((width, seqs * L), bf16),
                pltpu.VMEM((seqs * L, D), bf16),
                pltpu.VMEM((width, D), bf16),
                pltpu.VMEM(w_up.shape, bf16),
                pltpu.VMEM(w_down.shape, bf16),
                pltpu.VMEM(w_rows.shape, bf16),
                pltpu.VMEM((w_rows.shape[0], L), bf16),
                pltpu.SemaphoreType.DMA((4,)),
                pltpu.VMEM((3, DS, L), f32),
                pltpu.VMEM((DS, D), bf16),
                pltpu.VMEM((3, DS, DS), bf16),
                pltpu.VMEM((3 * L, DS), bf16),
                pltpu.VMEM((DS, DS), bf16),
                pltpu.VMEM((DS, SFF), bf16),
                pltpu.VMEM((SFF, DS), bf16),
                pltpu.VMEM((DS, SFF), bf16),
                pltpu.VMEM((SH * L, L), f32),
                pltpu.VMEM((SH * L, L), f32),
                pltpu.VMEM((seqs, SH * L, L), bf16),
                pltpu.VMEM((DS, D), f32),
                pltpu.VMEM((3, DS, DS), f32),
                pltpu.VMEM((DS, DS), f32),
                pltpu.VMEM((DS, SFF), f32),
                pltpu.VMEM((SFF, DS), f32),
                pltpu.VMEM((3, DS, L), f32),
            ],
        ),
        out_shape=[
            jax.ShapeDtypeStruct(side_input.shape, f32),
            jax.ShapeDtypeStruct(side_input.shape, f32),
            jax.ShapeDtypeStruct(send_shape, bf16),
            jax.ShapeDtypeStruct(send_shape, bf16),
        ],
        compiler_params=pltpu.CompilerParams(
            dimension_semantics=("arbitrary",), vmem_limit_bytes=VMEM_MAIN * MIB
        ),
        cost_estimate=pl.CostEstimate(
            flops=2 * own_seqs * L * (D * (D + 2 * ff) + width * (3 * D + 2 * L))
            + own_seqs * 300_000_000,
            bytes_accessed=own_seqs * L * (3 * D + 16 * DS) + 2 * D * (D + 2 * ff),
            transcendentals=own_seqs * L * (ff + 2 * SH * L + SFF),
        ),
    )(
        meta,
        lengths,
        normed,
        partial,
        gains,
        far,
        mate,
        table,
        side_input,
        output_grad,
        side_gains,
        side_table,
        onehot,
        turn_onehot,
        w_out,
        w_up,
        w_down,
        w_rows,
    )


def adamw_update(weight_now, first_now, second_now, gradient, rate, decay_rate):
    first_new = BETA_ONE * first_now + (1.0 - BETA_ONE) * gradient
    second_new = BETA_TWO * second_now + (1.0 - BETA_TWO) * gradient * gradient
    first_hat = first_new / (1.0 - BETA_ONE**ADAM_STEP)
    second_hat = second_new / (1.0 - BETA_TWO**ADAM_STEP)
    weight_new = weight_now - rate * (
        first_hat / (jnp.sqrt(second_hat) + ADAM_EPS) + decay_rate * weight_now
    )
    return (first_new, second_new, weight_new)


def collect_kernel(got_ref, shard_ref, gains_ref, table_ref, square_ref):
    total = got_ref[0].astype(jnp.float32)
    for device in range(1, got_ref.shape[0]):
        total = total + got_ref[device].astype(jnp.float32)
    shard = total[0 : shard_ref.shape[0], 0:DS]
    shard_ref[...] = shard
    table_ref[...] = total[0:SH, DS:]
    for row in range(3):
        for part in range(3):
            at = SH + 3 * row + part
            gains_ref[row : row + 1, part * NARROW : (part + 1) * NARROW] = total[at : at + 1, DS:]
    square = jnp.sum(jnp.sum(shard * shard, axis=1, keepdims=True), axis=0, keepdims=True)
    square_ref[...] = jnp.broadcast_to(square, square_ref.shape)


def collect_part(got, shard_rows):
    return pl.pallas_call(
        collect_kernel,
        name="collect",
        out_shape=[
            jax.ShapeDtypeStruct((shard_rows, DS), jnp.float32),
            jax.ShapeDtypeStruct((3, DS), jnp.float32),
            jax.ShapeDtypeStruct((SH, NARROW), jnp.float32),
            jax.ShapeDtypeStruct((2 * got.shape[0], L), jnp.float32),
        ],
        in_specs=[pl.BlockSpec(memory_space=pltpu.VMEM)],
        out_specs=[pl.BlockSpec(memory_space=pltpu.VMEM)] * 4,
    )(got)


def update_kernel(square_ref, gains_sum_ref, table_sum_ref, shard_ref, *refs):
    weights, gains, table = refs[0:3], refs[3:6], refs[6:9]
    norm_ref, copy_ref = refs[9], refs[13]
    gains_total = gains_sum_ref[...]
    table_total = table_sum_ref[...]
    whole = lambda values: jnp.sum(
        jnp.sum(values, axis=1, keepdims=True), axis=0, keepdims=True
    )
    norm = jnp.sqrt(
        jnp.sum(square_ref[:, 0:1], axis=0, keepdims=True)
        + whole(gains_total * gains_total)
        + whole(table_total * table_total)
    )
    norm_ref[...] = norm
    factor = CLIP_NORM / jnp.maximum(norm, CLIP_NORM)

    def update(state, gradient, outs, rate, decay):
        results = adamw_update(*[ref[...] for ref in state], factor * gradient, rate, decay)
        for ref, value in zip(outs, results):
            ref[...] = value
        return results[2]

    new = update(weights, shard_ref[...], refs[10:13], RATE_MATRIX, WEIGHT_DECAY)
    copy_ref[...] = new.astype(jnp.bfloat16)
    update(gains, gains_total, refs[14:17], RATE_SMALL, 0.0)
    update(table, table_total, refs[17:20], RATE_SMALL, 0.0)


def update_part(squares, gains_sum, table_sum, shard, weights, gains, table):
    f32 = jnp.float32
    like = lambda values, dtype=f32: jax.ShapeDtypeStruct(values.shape, dtype)
    operands = (squares, gains_sum, table_sum, shard, *weights, *gains, *table)
    return pl.pallas_call(
        update_kernel,
        name="update",
        out_shape=[
            jax.ShapeDtypeStruct((1, 1), f32),
            *[like(values) for values in weights],
            like(shard, jnp.bfloat16),
            *[like(values) for values in gains],
            *[like(values) for values in table],
        ],
        in_specs=[pl.BlockSpec(memory_space=pltpu.VMEM)] * len(operands),
        out_specs=[pl.BlockSpec(memory_space=pltpu.VMEM)] * 11,
    )(*operands)


def swap(values, distance):
    size = lax.axis_size("mp")
    return lax.ppermute(values, "mp", [(i, i ^ distance) for i in range(size)])


def exchange(values):
    return lax.all_to_all(values, ("batch", "mp"), split_axis=0, concat_axis=0, tiled=True)


def exchange_alike(values):
    groups = [[2 * i + parity for i in range(values.shape[0])] for parity in range(2)]
    return lax.all_to_all(
        values,
        ("batch", "mp"),
        split_axis=0,
        concat_axis=0,
        axis_index_groups=groups,
        tiled=True,
    )


def on_device(
    tokens,
    lengths,
    base_gains,
    base_qkv,
    base_out,
    base_up,
    base_down,
    base_table,
    side_input,
    output_grad,
    side_weights,
    weights_first,
    weights_second,
    side_gains,
    gains_first,
    gains_second,
    side_table,
    table_first,
    table_second,
):
    devices = lax.axis_size(("batch", "mp"))
    model_index = lax.axis_index("mp")
    own_seqs = side_input.shape[0]
    shard_rows = side_weights.shape[0] // DS
    buckets = side_table.shape[0]
    meta = jnp.stack([model_index * own_seqs, model_index % 2, model_index // 2]).astype(jnp.int32)

    turn = lambda values: jnp.transpose(values, (0, 2, 1))
    qkv_own = turn(base_qkv)
    qkv_far = swap(qkv_own, 2)
    lanes = L if side_weights.shape[0] % L == 0 else DS
    flat = lambda values: values.reshape(-1, lanes)
    low_rows = flat(side_weights.astype(jnp.bfloat16))
    low_rows = jnp.broadcast_to(low_rows[None], (devices,) + low_rows.shape)
    w_rows = exchange(low_rows)
    qkv_mate = swap(qkv_own, 1)

    onehot = jnp.asarray(diagonal_onehot(buckets))
    normed, partial = near_part(
        meta,
        lengths,
        tokens,
        base_gains,
        qkv_own,
        qkv_mate,
        base_table.T,
        onehot,
        base_out,
        own_seqs,
        8,
    )
    normed, partial, qkv_far, w_rows = lax.optimization_barrier((normed, partial, qkv_far, w_rows))
    qkv_far_mate = swap(qkv_far, 1)
    side_output, input_grad, mine, other = main_part(
        meta,
        lengths,
        normed,
        partial,
        base_gains,
        qkv_far,
        qkv_far_mate,
        base_table.T,
        turn(side_input),
        turn(output_grad),
        side_gains,
        side_table.T,
        onehot,
        jnp.asarray(gradient_onehot(buckets)),
        base_out,
        base_up,
        base_down,
        w_rows.reshape(devices * shard_rows, DS),
        devices,
        8,
        1024,
    )

    paired = mine.astype(jnp.float32) + swap(other, 1).astype(jnp.float32)
    grad_shard, gains_sum, table_sum, squares = collect_part(
        exchange_alike(paired.astype(jnp.bfloat16)), shard_rows
    )
    (
        grad_norm,
        weights_moment,
        weights_square,
        weights_new,
        weights_copy,
        gains_moment,
        gains_square,
        gains_new,
        table_moment,
        table_square,
        table_new,
    ) = update_part(
        exchange(squares),
        gains_sum,
        table_sum,
        flat(grad_shard),
        [flat(side_weights), flat(weights_first), flat(weights_second)],
        [side_gains, gains_first, gains_second],
        [side_table.T, table_first.T, table_second.T],
    )
    return (
        turn(side_output),
        turn(input_grad),
        grad_norm.reshape(()),
        weights_moment.reshape(-1),
        weights_square.reshape(-1),
        weights_new.reshape(-1),
        weights_copy.reshape(-1),
        gains_moment,
        gains_square,
        gains_new,
        table_moment.T,
        table_square.T,
        table_new.T,
    )


def solution(mesh):
    return jax.shard_map(
        on_device,
        mesh=mesh,
        in_specs=(
            P("batch", None, None),
            P("batch"),
            P(),
            P(None, None, "mp"),
            P(),
            P(),
            P(),
            P(),
            P(("batch", "mp"), None, None),
            P(("batch", "mp"), None, None),
            P(("batch", "mp")),
            P(("batch", "mp")),
            P(("batch", "mp")),
            P(),
            P(),
            P(),
            P(),
            P(),
            P(),
        ),
        out_specs=(
            P(("batch", "mp"), None, None),
            P(("batch", "mp"), None, None),
            P(),
            P(("batch", "mp")),
            P(("batch", "mp")),
            P(("batch", "mp")),
            P(("batch", "mp")),
            P(),
            P(),
            P(),
            P(),
            P(),
            P(),
        ),
        check_vma=False,
    )
```

```python
import functools
import math
import jax
import jax.numpy as jnp
import numpy as np
from jax import lax
from jax.experimental import pallas as pl
from jax.experimental.pallas import tpu as pltpu
from jax.sharding import PartitionSpec as P

D = 768
HD = 64
DS = 96
SH = 12
SHD = 8
SFF = 384
MAXD = 128
L = 128
ADAM_STEP = 10
PAIR = 2 * HD
SPAN = 2 * L
NARROW = L - DS
SMALL_ROWS = SH + 9

NORM_EPS = 1e-06
CLIP_NORM = 1.0
BETA_ONE = 0.9
BETA_TWO = 0.999
ADAM_EPS = 1e-08
RATE_MATRIX = 0.1
RATE_SMALL = 0.5
WEIGHT_DECAY = 0.01
MASKED = -1e30
PRECISE = lax.Precision.HIGHEST
MIB = 1 << 20
VMEM_MAIN = 60
GELU_RATE = math.sqrt(2.0 / math.pi)
GELU_CUBE = 0.044715

NN = (((1,), (0,)), ((), ()))
NT = (((1,), (1,)), ((), ()))
TN = (((0,), (0,)), ((), ()))


def mm(left, right, dims=NN):
    return lax.dot_general(left, right, dims, preferred_element_type=jnp.float32)


def bucket_of(offset, buckets, reach):
    half_count = buckets // 2
    exact_count = half_count // 2
    distance = np.abs(offset)
    spread_part = (
        np.log(np.maximum(distance, 1) / exact_count)
        / np.log(reach / exact_count)
        * (half_count - exact_count)
    )
    far_bucket = np.minimum(exact_count + np.floor(spread_part).astype(np.int32), half_count - 1)
    near_side = np.where(distance < exact_count, distance, far_bucket)
    return (near_side + (offset > 0) * half_count).astype(np.int32)


def diagonal_onehot(buckets):
    column = np.arange(SPAN)
    offset = np.where(column < L, -column, SPAN - column)
    onehot = bucket_of(offset, buckets, MAXD)[None, :] == np.arange(buckets)[:, None]
    onehot = onehot & (column != L)[None, :]
    return onehot.astype(np.float32)


def gradient_onehot(buckets):
    column = np.arange(SPAN)
    onehot = bucket_of(L - 1 - column, buckets, MAXD)[None, :] == np.arange(buckets)[:, None]
    onehot = onehot & (column != SPAN - 1)[None, :]
    return onehot.astype(np.float32)


def rms_scale(values):
    return lax.rsqrt(jnp.mean(values * values, axis=-1, keepdims=True) + NORM_EPS)


def gelu(v):
    return 0.5 * v * (1.0 + jnp.tanh(GELU_RATE * (v + GELU_CUBE * (v * v * v))))


def diagonals_of(table_ref, onehot_ref):
    return lax.dot_general(
        table_ref[...],
        onehot_ref[...],
        NN,
        precision=PRECISE,
        preferred_element_type=jnp.float32,
    )


def spread_bias(row):
    full = jnp.broadcast_to(row, (L, SPAN))
    return pltpu.roll(full, 0, 1, stride=1, stride_axis=0)[:, :L]


def attention_setup(
    parity, group, own_ref, mate_ref, table_ref, onehot_ref, diag_scr, w_scr, bias_scr
):
    third = own_ref.shape[1]
    width = 2 * third
    heads = width // HD

    def place(low_ref, high_ref):
        for part in range(3):
            w_scr[part * width : part * width + third, :] = low_ref[part]
            w_scr[part * width + third : (part + 1) * width, :] = high_ref[part]

    @pl.when(parity == 0)
    def _():
        place(own_ref, mate_ref)

    @pl.when(parity == 1)
    def _():
        place(mate_ref, own_ref)

    diag_scr[...] = diagonals_of(table_ref, onehot_ref)
    for head in range(heads):
        bias_scr[head * L : (head + 1) * L, :] = spread_bias(
            diag_scr[pl.ds(group * heads + head, 1), :]
        )


def together(*steps):
    waiting = list(steps)
    while waiting:
        for stage in list(waiting):
            if next(stage, StopIteration) is StopIteration:
                waiting.remove(stage)


def attention_steps(lengths, normed, w_scr, bias_scr, ctx_ref, base):
    width = w_scr.shape[0] // 3
    turned = mm(w_scr[...], normed, NT).astype(jnp.bfloat16)
    query, key, value = turned[0:width], turned[width : 2 * width], turned[2 * width :]
    yield
    low_lane = lax.broadcasted_iota(jnp.int32, (L, PAIR), 1) < HD
    low_row = lax.broadcasted_iota(jnp.int32, (PAIR, L), 0) < HD
    key_row = lax.broadcasted_iota(jnp.int32, (2, L, L), 1)
    for s, length in enumerate(lengths):
        at = slice(s * L, (s + 1) * L)
        seen = key_row < length
        for p in range(width // PAIR):
            head = slice(p * PAIR, (p + 1) * PAIR)
            k_one, v_one = key[head, at].T, value[head, at]
            zero = jnp.zeros_like(k_one)
            k_two = jnp.concatenate(
                [jnp.where(low_lane, k_one, zero), jnp.where(low_lane, zero, k_one)], axis=0
            )
            v_two = jnp.concatenate(
                [jnp.where(low_row, v_one, zero), jnp.where(low_row, zero, v_one)], axis=1
            )
            scores = mm(k_two, query[head, at]) + bias_scr[p * 2 * L : (p + 1) * 2 * L, :]
            scores = jnp.where(seen, scores.reshape(2, L, L), MASKED)
            shifted = jnp.exp(scores - jnp.max(scores, axis=1, keepdims=True))
            scale = 1.0 / jnp.sum(shifted, axis=1, keepdims=True)
            scale = jnp.broadcast_to(scale, (2, HD, L)).reshape(PAIR, L)
            probs = shifted.astype(jnp.bfloat16).reshape(2 * L, L)
            into = slice(base + s * L, base + (s + 1) * L)
            ctx_ref[head, into] = (mm(v_two, probs) * scale).astype(jnp.bfloat16)
        yield


def near_kernel(
    seqs,
    meta_ref,
    len_ref,
    tok_ref,
    gain_ref,
    own_ref,
    mate_ref,
    table_ref,
    onehot_ref,
    wo_ref,
    normed_ref,
    partial_ref,
    ctx_scr,
    diag_scr,
    w_scr,
    bias_scr,
):
    step = pl.program_id(0)

    @pl.when(step == 0)
    def _():
        attention_setup(
            meta_ref[1],
            meta_ref[2],
            own_ref,
            mate_ref,
            table_ref,
            onehot_ref,
            diag_scr,
            w_scr,
            bias_scr,
        )

    lengths = [len_ref[meta_ref[0] + step * seqs + s] for s in range(seqs)]
    rows = tok_ref[...].reshape(seqs * L, D).astype(jnp.float32)
    normed = (rows * rms_scale(rows) * gain_ref[0:1, :]).astype(jnp.bfloat16)
    normed_ref[...] = normed
    together(attention_steps(lengths, normed, w_scr, bias_scr, ctx_scr, 0))
    partial_ref[...] = (rows + mm(ctx_scr[...], wo_ref[...], TN)).astype(jnp.bfloat16)


def near_part(meta, lengths, tokens, gains, own, mate, table, onehot, w_out, own_seqs, seqs):
    width = 2 * own.shape[1]
    fixed = lambda *dims: pl.BlockSpec(dims, lambda i, m, n: (0,) * len(dims))
    return pl.pallas_call(
        functools.partial(near_kernel, seqs),
        name="near",
        grid_spec=pltpu.PrefetchScalarGridSpec(
            num_scalar_prefetch=2,
            grid=(own_seqs // seqs,),
            in_specs=[
                pl.BlockSpec((seqs, L, D), lambda i, m, n: (m[0] // seqs + i, 0, 0)),
                fixed(2, D),
                fixed(*own.shape),
                fixed(*mate.shape),
                fixed(*table.shape),
                fixed(*onehot.shape),
                pl.BlockSpec((width, D), lambda i, m, n: (m[2], 0)),
            ],
            out_specs=[pl.BlockSpec((seqs * L, D), lambda i, m, n: (i, 0))] * 2,
            scratch_shapes=[
                pltpu.VMEM((width, seqs * L), jnp.bfloat16),
                pltpu.VMEM((table.shape[0], SPAN), jnp.float32),
                pltpu.VMEM((3 * width, D), jnp.bfloat16),
                pltpu.VMEM((width // HD * L, L), jnp.float32),
            ],
        ),
        out_shape=[jax.ShapeDtypeStruct((own_seqs * L, D), jnp.bfloat16)] * 2,
        compiler_params=pltpu.CompilerParams(
            dimension_semantics=("arbitrary",), vmem_limit_bytes=56 * MIB
        ),
        cost_estimate=pl.CostEstimate(
            flops=2 * own_seqs * L * width * (4 * D + 2 * L),
            bytes_accessed=own_seqs * L * 3 * D * 2 + 6 * D * width,
            transcendentals=own_seqs * width // HD * L * L,
        ),
    )(meta, lengths, tokens, gains, own, mate, table, onehot, w_out)


def feed_steps(chunk, rows, far, gain, wo_scr, up_scr, down_scr, taps_scr, at):
    middle = rows + mm(far, wo_scr[...], TN)
    normed = (middle * rms_scale(middle) * gain).astype(jnp.bfloat16)
    total = jnp.zeros_like(middle)
    yield
    for c in range(0, up_scr.shape[1], chunk):
        hidden = gelu(mm(normed, up_scr[:, c : c + chunk])).astype(jnp.bfloat16)
        yield
        total = total + mm(hidden, down_scr[c : c + chunk, :])
        yield
    taps_scr[at, :] = (middle + total).astype(jnp.bfloat16)


def pick_rows(step, phase, count):
    row = lax.broadcasted_iota(jnp.int32, (count, step * count), 0)
    column = lax.broadcasted_iota(jnp.int32, (count, step * count), 1)
    return (column == step * row + phase).astype(jnp.bfloat16)


def by_head_rows(block):
    head = lax.broadcasted_iota(jnp.int32, block.shape, 1) // SHD
    zero = jnp.zeros_like(block)
    return jnp.concatenate([jnp.where(head == h, block, zero) for h in range(SH)], axis=0)


def by_head_lanes(block):
    head = lax.broadcasted_iota(jnp.int32, block.shape, 0) // SHD
    zero = jnp.zeros_like(block)
    return jnp.concatenate([jnp.where(head == h, block, zero) for h in range(SH)], axis=1)


def lanes_of(stacked):
    return jnp.concatenate([stacked[h * L : (h + 1) * L] for h in range(SH)], axis=1)


def norm_back(unit, scale, gain, grad):
    scaled = grad * gain
    return scale * (scaled - unit * jnp.mean(scaled * unit, axis=0, keepdims=True))


def two_by_head(turned, first):
    blocks = [by_head_rows(turned[:, s * L : (s + 1) * L].T) for s in (first, first + 1)]
    return jnp.concatenate(blocks, axis=1)


def two_apart(turned, first):
    zero = jnp.zeros((L, L), turned.dtype)
    one, two = turned[:, first * L : (first + 1) * L], turned[:, (first + 1) * L : (first + 2) * L]
    return jnp.concatenate(
        [jnp.concatenate([one, zero], axis=1), jnp.concatenate([zero, two], axis=1)], axis=0
    )


def column_scale(values):
    return lax.rsqrt(jnp.mean(values * values, axis=0, keepdims=True) + NORM_EPS)


def fold_lanes(values):
    total = values[:, 0:L]
    for s in range(1, values.shape[1] // L):
        total = total + values[:, s * L : (s + 1) * L]
    return total


AT_QKV, AT_OUT, AT_UP, AT_BACK, AT_END = D, D + 3 * DS, D + 4 * DS, D + 8 * DS, D + 8 * DS + SFF


def low(values):
    return values.astype(jnp.bfloat16)


def side_setup(gain_ref, w_ref, table_ref, onehot_ref, scratch):
    (
        gain_scr,
        wdown_scr,
        wqkv_scr,
        wqkv_turn_scr,
        wout_turn_scr,
        wup_scr,
        wup_turn_scr,
        wback_turn_scr,
        bias_scr,
        gbias_scr,
        elow_scr,
        gdown_scr,
        gqkv_scr,
        gproj_scr,
        gup_scr,
        gback_scr,
        ggain_scr,
    ) = scratch
    wdown_scr[...] = w_ref[0:D, :].T
    for t in range(3):
        part = mm(pick_rows(3, t, DS), w_ref[AT_QKV:AT_OUT, :])
        wqkv_scr[t] = low(part)
        wqkv_turn_scr[t * L : t * L + DS, :] = low(part.T)
        wqkv_turn_scr[t * L + DS : (t + 1) * L, :] = jnp.zeros((L - DS, DS), jnp.bfloat16)
    wout_turn_scr[...] = w_ref[AT_OUT:AT_UP, :].T
    for t in range(4):
        part = mm(pick_rows(4, t, DS), w_ref[AT_UP:AT_BACK, :])
        wup_scr[:, t * DS : (t + 1) * DS] = low(part)
        wup_turn_scr[t * DS : (t + 1) * DS, :] = low(part.T)
    wback_turn_scr[...] = w_ref[AT_BACK : AT_END, :].T
    for row in range(3):
        wide = jnp.broadcast_to(gain_ref[row : row + 1, :], (L, DS)).T
        gain_scr[row] = jax.nn.sigmoid(wide) if row == 2 else wide
    diagonals = diagonals_of(table_ref, onehot_ref)
    for head in range(SH):
        bias_scr[head * L : (head + 1) * L, :] = spread_bias(diagonals[head : head + 1, :])
    for ref in (gbias_scr, gdown_scr, gqkv_scr, gproj_scr, gup_scr, gback_scr, ggain_scr):
        ref[...] = jnp.zeros_like(ref)


def side_steps(lengths, base, taps, x_ref, go_ref, w_ref, out_ref, ig_ref, scratch):
    (
        gain_scr,
        wdown_scr,
        wqkv_scr,
        wqkv_turn_scr,
        wout_turn_scr,
        wup_scr,
        wup_turn_scr,
        wback_turn_scr,
        bias_scr,
        gbias_scr,
        elow_scr,
        gdown_scr,
        gqkv_scr,
        gproj_scr,
        gup_scr,
        gback_scr,
        ggain_scr,
    ) = scratch
    seqs = len(lengths)
    wide = lambda row: jnp.concatenate([gain_scr[row]] * seqs, axis=1)
    gain_one, gain_two, gate = wide(0), wide(1), wide(2)
    w_out = w_ref[AT_OUT:AT_UP, :]
    w_back = w_ref[AT_BACK : AT_END, :]
    key_row = lax.broadcasted_iota(jnp.int32, (SH, L, L), 1)
    token = lax.broadcasted_iota(jnp.int32, (DS, L), 1)
    x = jnp.concatenate([x_ref[base + s] for s in range(seqs)], axis=1)
    grad_out = jnp.concatenate(
        [jnp.where(token < lengths[s], go_ref[base + s], 0.0) for s in range(seqs)], axis=1
    )

    tapped = mm(wdown_scr[...], taps, NT)
    mixed = gate * x + (1.0 - gate) * tapped
    scale_one = column_scale(mixed)
    unit_one = mixed * scale_one
    normed_one = low(unit_one * gain_one)
    qkv = low(mm(wqkv_turn_scr[...], normed_one))

    query, key, value = qkv[0:L], qkv[L : 2 * L], qkv[2 * L :]
    context, inverse = [], []
    yield
    for s in range(0, seqs, 2):
        score_two = mm(two_by_head(key, s), two_apart(query, s))
        for side in range(2):
            at = slice((s + side) * L, (s + side + 1) * L)
            scores = score_two[:, side * L : (side + 1) * L] + bias_scr[...]
            scores = jnp.where(key_row < lengths[s + side], scores.reshape(SH, L, L), MASKED)
            shifted = jnp.exp(scores - jnp.max(scores, axis=1, keepdims=True))
            e_low = low(shifted).reshape(SH * L, L)
            elow_scr[base + s + side] = e_low
            total = 1.0 / jnp.sum(shifted, axis=1, keepdims=True)
            inverse.append(jnp.broadcast_to(total, (SH, SHD, L)).reshape(DS, L))
            context.append(mm(by_head_lanes(value[0:DS, at]), e_low) * inverse[-1])
        yield
    context = jnp.concatenate(context, axis=1)
    inverse = jnp.concatenate(inverse, axis=1)
    context_low = low(context)

    middle = mixed + mm(wout_turn_scr[...], context_low)
    scale_two = column_scale(middle)
    unit_two = middle * scale_two
    normed_two = low(unit_two * gain_two)
    pre = mm(wup_turn_scr[...], normed_two)
    square = pre * pre
    bend = jnp.tanh(GELU_RATE * pre * (1.0 + GELU_CUBE * square))
    half = 0.5 * (1.0 + bend)
    hidden = low(pre * half)
    slope = half + (0.5 * GELU_RATE) * pre * (1.0 - bend * bend) * (1.0 + 3.0 * GELU_CUBE * square)
    side_out = middle + mm(wback_turn_scr[...], hidden)
    yield

    grad_low = low(grad_out)
    gback_scr[...] += mm(hidden, grad_low, NT)
    grad_pre = low(mm(w_back, grad_low) * slope)
    gup_scr[...] += mm(normed_two, grad_pre, NT)
    grad_normed_two = mm(wup_scr[...], grad_pre)
    ggain_scr[1] += fold_lanes(grad_normed_two * unit_two)
    grad_middle = grad_out + norm_back(unit_two, scale_two, gain_two, grad_normed_two)
    grad_attended = low(grad_middle)
    gproj_scr[...] += mm(context_low, grad_attended, NT)
    grad_context = low(mm(w_out, grad_attended) * inverse)
    pad = jnp.zeros((L - DS, seqs * L), jnp.bfloat16)
    dots = (grad_context.astype(jnp.float32) * context).reshape(SH, SHD, seqs * L)
    dots = jnp.sum(dots, axis=1, keepdims=True)

    grad_context = jnp.concatenate([grad_context, pad], axis=0)
    grad_query, grad_key, grad_value = [], [], []
    yield
    for s in range(0, seqs, 2):
        prob_two = mm(two_by_head(value, s), two_apart(grad_context, s))
        for side in range(2):
            at = slice((s + side) * L, (s + side + 1) * L)
            grad_probs = prob_two[:, side * L : (side + 1) * L].reshape(SH, L, L)
            grad_scores = elow_scr[base + s + side].astype(jnp.float32).reshape(SH, L, L) * (
                grad_probs - dots[:, :, at]
            )
            gbias_scr[...] += grad_scores.reshape(SH * L, L)
            grad_scores = low(grad_scores).reshape(SH * L, L)
            grad_query.append(low(mm(by_head_lanes(key[0:DS, at]), grad_scores)))
            grad_key.append(low(mm(lanes_of(grad_scores), by_head_rows(query[0:DS, at].T))))
            grad_value.append(
                low(mm(lanes_of(elow_scr[base + s + side]), by_head_rows(grad_context[0:DS, at].T)))
            )
        yield
    grad_query = jnp.concatenate(grad_query, axis=1)
    grad_key = jnp.concatenate(grad_key, axis=0)
    grad_value = jnp.concatenate(grad_value, axis=0)

    grad_normed = mm(wqkv_scr[0], grad_query)
    grad_normed += mm(wqkv_scr[1], grad_key, NT)
    grad_normed += mm(wqkv_scr[2], grad_value, NT)
    gqkv_scr[0] += mm(normed_one, grad_query, NT)
    gqkv_scr[1] += mm(normed_one, grad_key)
    gqkv_scr[2] += mm(normed_one, grad_value)
    ggain_scr[0] += fold_lanes(grad_normed * unit_one)
    grad_mixed = grad_middle + norm_back(unit_one, scale_one, gain_one, grad_normed)
    input_grad = gate * grad_mixed
    grad_tap = low((1.0 - gate) * grad_mixed)
    gdown_scr[...] += mm(grad_tap, taps)
    ggain_scr[2] += fold_lanes(grad_mixed * (x - tapped))
    for s in range(seqs):
        out_ref[base + s] = side_out[:, s * L : (s + 1) * L]
        ig_ref[base + s] = input_grad[:, s * L : (s + 1) * L]


def side_finish(parity, onehot_ref, mine_ref, other_ref, grow_scr, scratch):
    (
        gain_scr,
        wdown_scr,
        wqkv_scr,
        wqkv_turn_scr,
        wout_turn_scr,
        wup_scr,
        wup_turn_scr,
        wback_turn_scr,
        bias_scr,
        gbias_scr,
        elow_scr,
        gdown_scr,
        gqkv_scr,
        gproj_scr,
        gup_scr,
        gback_scr,
        ggain_scr,
    ) = scratch
    grow_scr[:, DS:] = jnp.zeros((grow_scr.shape[0], grow_scr.shape[1] - DS), jnp.bfloat16)
    grow_scr[0:D, 0:DS] = low(gdown_scr[...].T)
    spread = mm(pick_rows(3, 0, DS), low(gqkv_scr[0]), TN)
    for t in range(1, 3):
        spread = spread + mm(pick_rows(3, t, DS), low(gqkv_scr[t]), TN)
    grow_scr[AT_QKV:AT_OUT, 0:DS] = low(spread)
    grow_scr[AT_OUT:AT_UP, 0:DS] = low(gproj_scr[...])
    spread = mm(pick_rows(4, 0, DS), low(gup_scr[:, 0:DS]), TN)
    for t in range(1, 4):
        spread = spread + mm(pick_rows(4, t, DS), low(gup_scr[:, t * DS : (t + 1) * DS]), TN)
    grow_scr[AT_UP:AT_BACK, 0:DS] = low(spread)
    grow_scr[AT_BACK : AT_END, 0:DS] = low(gback_scr[...])
    flip_row = lax.broadcasted_iota(jnp.int32, (L, L), 0)
    flip_column = lax.broadcasted_iota(jnp.int32, (L, L), 1)
    flip = low((flip_row + flip_column == L - 1).astype(jnp.float32))
    squares = lanes_of(gbias_scr[...])
    upper = low(squares)
    flipped = mm(flip, upper)
    flipped = flipped + mm(flip, low(squares - upper.astype(jnp.float32)))
    diagonals = []
    for head in range(SH):
        square = flipped[:, head * L : (head + 1) * L]
        full = jnp.concatenate([square, jnp.zeros_like(square)], axis=1)
        rolled = pltpu.roll(full, 0, 1, stride=1, stride_axis=0)
        diagonals.append(jnp.sum(rolled, axis=0, keepdims=True))
    diagonals = jnp.concatenate(diagonals, axis=0)
    gains = []
    for row in range(3):
        total = ggain_scr[row]
        if row == 2:
            total = total * (gain_scr[2] * (1.0 - gain_scr[2]))
        total = jnp.sum(total.T, axis=0, keepdims=True)
        gains += [total[:, part * NARROW : (part + 1) * NARROW] for part in range(3)]
    table = lax.dot_general(
        diagonals, onehot_ref[...], NT, precision=PRECISE, preferred_element_type=jnp.float32
    )
    small = low(jnp.concatenate([table] + gains, axis=0))
    pairs = mine_ref.shape[0]
    shard_rows = AT_END // (2 * pairs)
    blank = jnp.zeros((mine_ref.shape[1] - shard_rows, L), jnp.bfloat16)

    def place(even_ref, odd_ref):
        for device in range(2 * pairs):
            ref, slot = (even_ref, odd_ref)[device % 2], device // 2
            ref[slot, 0:shard_rows, :] = grow_scr[device * shard_rows : (device + 1) * shard_rows, :]
            if blank.shape[0]:
                ref[slot, shard_rows:, :] = blank
            ref[slot, 0 : small.shape[0], DS:] = small

    @pl.when(parity == 0)
    def _():
        place(mine_ref, other_ref)

    @pl.when(parity == 1)
    def _():
        place(other_ref, mine_ref)


def main_kernel(
    seqs,
    chunk,
    meta_ref,
    len_ref,
    normed_ref,
    partial_ref,
    gain_ref,
    far_ref,
    mate_ref,
    table_ref,
    x_ref,
    go_ref,
    side_gain_ref,
    side_table_ref,
    onehot_ref,
    turn_onehot_ref,
    wo_hbm,
    up_hbm,
    down_hbm,
    w_hbm,
    out_ref,
    ig_ref,
    mine_ref,
    other_ref,
    diag_scr,
    w_scr,
    bias_scr,
    ctx_scr,
    taps_scr,
    wo_scr,
    up_scr,
    down_scr,
    wrow_scr,
    grow_scr,
    sems,
    *scratch,
):
    step = pl.program_id(0)
    group = meta_ref[2]
    width = wo_scr.shape[0]
    copies = [
        pltpu.make_async_copy(wo_hbm.at[pl.ds((1 - group) * width, width), :], wo_scr, sems.at[0]),
        pltpu.make_async_copy(up_hbm, up_scr, sems.at[1]),
        pltpu.make_async_copy(down_hbm, down_scr, sems.at[2]),
        pltpu.make_async_copy(w_hbm, wrow_scr, sems.at[3]),
    ]

    @pl.when(step == 0)
    def _():
        for copy in copies:
            copy.start()
        attention_setup(
            meta_ref[1],
            1 - group,
            far_ref,
            mate_ref,
            table_ref,
            onehot_ref,
            diag_scr,
            w_scr,
            bias_scr,
        )

    lengths = [len_ref[meta_ref[0] + step * seqs + s] for s in range(seqs)]
    half = seqs // 2
    at = [slice(h * half * L, (h + 1) * half * L) for h in range(2)]

    def attend(h):
        return attention_steps(
            lengths[h * half : (h + 1) * half],
            normed_ref[at[h], :],
            w_scr,
            bias_scr,
            ctx_scr,
            h * half * L,
        )

    def feed(part):
        size = seqs * L // 4
        at = slice(part * size, (part + 1) * size)
        return feed_steps(
            chunk,
            partial_ref[at, :].astype(jnp.float32),
            ctx_scr[:, at],
            gain_ref[1:2, :],
            wo_scr,
            up_scr,
            down_scr,
            taps_scr,
            at,
        )

    def side(h):
        return side_steps(
            lengths[h * half : (h + 1) * half],
            h * half,
            taps_scr[at[h], :],
            x_ref,
            go_ref,
            wrow_scr,
            out_ref,
            ig_ref,
            scratch,
        )

    together(attend(0), attend(1))
    @pl.when(step == 0)
    def _():
        for copy in copies:
            copy.wait()
        side_setup(side_gain_ref, wrow_scr, side_table_ref, onehot_ref, scratch)

    together(*[feed(part) for part in range(4)])
    together(side(0), side(1))

    @pl.when(step == pl.num_programs(0) - 1)
    def _():
        side_finish(meta_ref[1], turn_onehot_ref, mine_ref, other_ref, grow_scr, scratch)


def main_part(
    meta,
    lengths,
    normed,
    partial,
    gains,
    far,
    mate,
    table,
    side_input,
    output_grad,
    side_gains,
    side_table,
    onehot,
    turn_onehot,
    w_out,
    w_up,
    w_down,
    w_rows,
    devices,
    seqs,
    chunk,
):
    own_seqs = side_input.shape[0]
    width = w_out.shape[0] // 2
    ff = w_up.shape[1]
    send_rows = -(-max(w_rows.shape[0] // devices, SMALL_ROWS) // 8) * 8
    send_shape = (devices // 2, send_rows, L)
    fixed = lambda *dims: pl.BlockSpec(dims, lambda i, m, n: (0,) * len(dims))
    block = pl.BlockSpec((seqs, DS, L), lambda i, m, n: (i, 0, 0))
    hbm = pl.BlockSpec(memory_space=pl.ANY)
    f32, bf16 = jnp.float32, jnp.bfloat16
    return pl.pallas_call(
        functools.partial(main_kernel, seqs, chunk),
        name="main",
        grid_spec=pltpu.PrefetchScalarGridSpec(
            num_scalar_prefetch=2,
            grid=(own_seqs // seqs,),
            in_specs=[
                pl.BlockSpec((seqs * L, D), lambda i, m, n: (i, 0)),
                pl.BlockSpec((seqs * L, D), lambda i, m, n: (i, 0)),
                fixed(2, D),
                fixed(*far.shape),
                fixed(*mate.shape),
                fixed(*table.shape),
                block,
                block,
                fixed(*side_gains.shape),
                fixed(*side_table.shape),
                fixed(*onehot.shape),
                fixed(*turn_onehot.shape),
                hbm,
                hbm,
                hbm,
                hbm,
            ],
            out_specs=[block, block, fixed(*send_shape), fixed(*send_shape)],
            scratch_shapes=[
                pltpu.VMEM((table.shape[0], SPAN), f32),
                pltpu.VMEM((3 * width, D), bf16),
                pltpu.VMEM((width // HD * L, L), f32),
                pltpu.VMEM((width, seqs * L), bf16),
                pltpu.VMEM((seqs * L, D), bf16),
                pltpu.VMEM((width, D), bf16),
                pltpu.VMEM(w_up.shape, bf16),
                pltpu.VMEM(w_down.shape, bf16),
                pltpu.VMEM(w_rows.shape, bf16),
                pltpu.VMEM((w_rows.shape[0], L), bf16),
                pltpu.SemaphoreType.DMA((4,)),
                pltpu.VMEM((3, DS, L), f32),
                pltpu.VMEM((DS, D), bf16),
                pltpu.VMEM((3, DS, DS), bf16),
                pltpu.VMEM((3 * L, DS), bf16),
                pltpu.VMEM((DS, DS), bf16),
                pltpu.VMEM((DS, SFF), bf16),
                pltpu.VMEM((SFF, DS), bf16),
                pltpu.VMEM((DS, SFF), bf16),
                pltpu.VMEM((SH * L, L), f32),
                pltpu.VMEM((SH * L, L), f32),
                pltpu.VMEM((seqs, SH * L, L), bf16),
                pltpu.VMEM((DS, D), f32),
                pltpu.VMEM((3, DS, DS), f32),
                pltpu.VMEM((DS, DS), f32),
                pltpu.VMEM((DS, SFF), f32),
                pltpu.VMEM((SFF, DS), f32),
                pltpu.VMEM((3, DS, L), f32),
            ],
        ),
        out_shape=[
            jax.ShapeDtypeStruct(side_input.shape, f32),
            jax.ShapeDtypeStruct(side_input.shape, f32),
            jax.ShapeDtypeStruct(send_shape, bf16),
            jax.ShapeDtypeStruct(send_shape, bf16),
        ],
        compiler_params=pltpu.CompilerParams(
            dimension_semantics=("arbitrary",), vmem_limit_bytes=VMEM_MAIN * MIB
        ),
        cost_estimate=pl.CostEstimate(
            flops=2 * own_seqs * L * (D * (D + 2 * ff) + width * (3 * D + 2 * L))
            + own_seqs * 300_000_000,
            bytes_accessed=own_seqs * L * (3 * D + 16 * DS) + 2 * D * (D + 2 * ff),
            transcendentals=own_seqs * L * (ff + 2 * SH * L + SFF),
        ),
    )(
        meta,
        lengths,
        normed,
        partial,
        gains,
        far,
        mate,
        table,
        side_input,
        output_grad,
        side_gains,
        side_table,
        onehot,
        turn_onehot,
        w_out,
        w_up,
        w_down,
        w_rows,
    )


def adamw_update(weight_now, first_now, second_now, gradient, rate, decay_rate):
    first_new = BETA_ONE * first_now + (1.0 - BETA_ONE) * gradient
    second_new = BETA_TWO * second_now + (1.0 - BETA_TWO) * gradient * gradient
    first_hat = first_new / (1.0 - BETA_ONE**ADAM_STEP)
    second_hat = second_new / (1.0 - BETA_TWO**ADAM_STEP)
    weight_new = weight_now - rate * (
        first_hat / (jnp.sqrt(second_hat) + ADAM_EPS) + decay_rate * weight_now
    )
    return (first_new, second_new, weight_new)


def collect_kernel(got_ref, shard_ref, gains_ref, table_ref, square_ref):
    total = got_ref[0].astype(jnp.float32)
    for device in range(1, got_ref.shape[0]):
        total = total + got_ref[device].astype(jnp.float32)
    shard = total[0 : shard_ref.shape[0], 0:DS]
    shard_ref[...] = shard
    table_ref[...] = total[0:SH, DS:]
    for row in range(3):
        for part in range(3):
            at = SH + 3 * row + part
            gains_ref[row : row + 1, part * NARROW : (part + 1) * NARROW] = total[at : at + 1, DS:]
    square = jnp.sum(jnp.sum(shard * shard, axis=1, keepdims=True), axis=0, keepdims=True)
    square_ref[...] = jnp.broadcast_to(square, square_ref.shape)


def collect_part(got, shard_rows):
    return pl.pallas_call(
        collect_kernel,
        name="collect",
        out_shape=[
            jax.ShapeDtypeStruct((shard_rows, DS), jnp.float32),
            jax.ShapeDtypeStruct((3, DS), jnp.float32),
            jax.ShapeDtypeStruct((SH, NARROW), jnp.float32),
            jax.ShapeDtypeStruct((2 * got.shape[0], L), jnp.float32),
        ],
        in_specs=[pl.BlockSpec(memory_space=pltpu.VMEM)],
        out_specs=[pl.BlockSpec(memory_space=pltpu.VMEM)] * 4,
    )(got)


def update_kernel(square_ref, gains_sum_ref, table_sum_ref, shard_ref, *refs):
    weights, gains, table = refs[0:3], refs[3:6], refs[6:9]
    norm_ref, copy_ref = refs[9], refs[13]
    gains_total = gains_sum_ref[...]
    table_total = table_sum_ref[...]
    whole = lambda values: jnp.sum(
        jnp.sum(values, axis=1, keepdims=True), axis=0, keepdims=True
    )
    norm = jnp.sqrt(
        jnp.sum(square_ref[:, 0:1], axis=0, keepdims=True)
        + whole(gains_total * gains_total)
        + whole(table_total * table_total)
    )
    norm_ref[...] = norm
    factor = CLIP_NORM / jnp.maximum(norm, CLIP_NORM)

    def update(state, gradient, outs, rate, decay):
        results = adamw_update(*[ref[...] for ref in state], factor * gradient, rate, decay)
        for ref, value in zip(outs, results):
            ref[...] = value
        return results[2]

    new = update(weights, shard_ref[...], refs[10:13], RATE_MATRIX, WEIGHT_DECAY)
    copy_ref[...] = new.astype(jnp.bfloat16)
    update(gains, gains_total, refs[14:17], RATE_SMALL, 0.0)
    update(table, table_total, refs[17:20], RATE_SMALL, 0.0)


def update_part(squares, gains_sum, table_sum, shard, weights, gains, table):
    f32 = jnp.float32
    like = lambda values, dtype=f32: jax.ShapeDtypeStruct(values.shape, dtype)
    operands = (squares, gains_sum, table_sum, shard, *weights, *gains, *table)
    return pl.pallas_call(
        update_kernel,
        name="update",
        out_shape=[
            jax.ShapeDtypeStruct((1, 1), f32),
            *[like(values) for values in weights],
            like(shard, jnp.bfloat16),
            *[like(values) for values in gains],
            *[like(values) for values in table],
        ],
        in_specs=[pl.BlockSpec(memory_space=pltpu.VMEM)] * len(operands),
        out_specs=[pl.BlockSpec(memory_space=pltpu.VMEM)] * 11,
    )(*operands)


def swap(values, distance):
    size = lax.axis_size("mp")
    return lax.ppermute(values, "mp", [(i, i ^ distance) for i in range(size)])


def exchange(values):
    return lax.all_to_all(values, ("batch", "mp"), split_axis=0, concat_axis=0, tiled=True)


def exchange_alike(values):
    groups = [[2 * i + parity for i in range(values.shape[0])] for parity in range(2)]
    return lax.all_to_all(
        values,
        ("batch", "mp"),
        split_axis=0,
        concat_axis=0,
        axis_index_groups=groups,
        tiled=True,
    )


def on_device(
    tokens,
    lengths,
    base_gains,
    base_qkv,
    base_out,
    base_up,
    base_down,
    base_table,
    side_input,
    output_grad,
    side_weights,
    weights_first,
    weights_second,
    side_gains,
    gains_first,
    gains_second,
    side_table,
    table_first,
    table_second,
):
    devices = lax.axis_size(("batch", "mp"))
    model_index = lax.axis_index("mp")
    own_seqs = side_input.shape[0]
    shard_rows = side_weights.shape[0] // DS
    buckets = side_table.shape[0]
    meta = jnp.stack([model_index * own_seqs, model_index % 2, model_index // 2]).astype(jnp.int32)

    turn = lambda values: jnp.transpose(values, (0, 2, 1))
    qkv_own = turn(base_qkv)
    qkv_far = swap(qkv_own, 2)
    lanes = L if side_weights.shape[0] % L == 0 else DS
    flat = lambda values: values.reshape(-1, lanes)
    low_rows = flat(side_weights.astype(jnp.bfloat16))
    low_rows = jnp.broadcast_to(low_rows[None], (devices,) + low_rows.shape)
    w_rows = exchange(low_rows)
    qkv_mate = swap(qkv_own, 1)

    onehot = jnp.asarray(diagonal_onehot(buckets))
    normed, partial = near_part(
        meta,
        lengths,
        tokens,
        base_gains,
        qkv_own,
        qkv_mate,
        base_table.T,
        onehot,
        base_out,
        own_seqs,
        8,
    )
    normed, partial, qkv_far, w_rows = lax.optimization_barrier((normed, partial, qkv_far, w_rows))
    qkv_far_mate = swap(qkv_far, 1)
    side_output, input_grad, mine, other = main_part(
        meta,
        lengths,
        normed,
        partial,
        base_gains,
        qkv_far,
        qkv_far_mate,
        base_table.T,
        turn(side_input),
        turn(output_grad),
        side_gains,
        side_table.T,
        onehot,
        jnp.asarray(gradient_onehot(buckets)),
        base_out,
        base_up,
        base_down,
        w_rows.reshape(devices * shard_rows, DS),
        devices,
        8,
        1536,
    )

    paired = mine.astype(jnp.float32) + swap(other, 1).astype(jnp.float32)
    grad_shard, gains_sum, table_sum, squares = collect_part(
        exchange_alike(paired.astype(jnp.bfloat16)), shard_rows
    )
    (
        grad_norm,
        weights_moment,
        weights_square,
        weights_new,
        weights_copy,
        gains_moment,
        gains_square,
        gains_new,
        table_moment,
        table_square,
        table_new,
    ) = update_part(
        exchange(squares),
        gains_sum,
        table_sum,
        flat(grad_shard),
        [flat(side_weights), flat(weights_first), flat(weights_second)],
        [side_gains, gains_first, gains_second],
        [side_table.T, table_first.T, table_second.T],
    )
    return (
        turn(side_output),
        turn(input_grad),
        grad_norm.reshape(()),
        weights_moment.reshape(-1),
        weights_square.reshape(-1),
        weights_new.reshape(-1),
        weights_copy.reshape(-1),
        gains_moment,
        gains_square,
        gains_new,
        table_moment.T,
        table_square.T,
        table_new.T,
    )


def solution(mesh):
    return jax.shard_map(
        on_device,
        mesh=mesh,
        in_specs=(
            P("batch", None, None),
            P("batch"),
            P(),
            P(None, None, "mp"),
            P(),
            P(),
            P(),
            P(),
            P(("batch", "mp"), None, None),
            P(("batch", "mp"), None, None),
            P(("batch", "mp")),
            P(("batch", "mp")),
            P(("batch", "mp")),
            P(),
            P(),
            P(),
            P(),
            P(),
            P(),
        ),
        out_specs=(
            P(("batch", "mp"), None, None),
            P(("batch", "mp"), None, None),
            P(),
            P(("batch", "mp")),
            P(("batch", "mp")),
            P(("batch", "mp")),
            P(("batch", "mp")),
            P(),
            P(),
            P(),
            P(),
            P(),
            P(),
        ),
        check_vma=False,
    )
```
